128 devices in a mesh: rows: 32 (over x, z, core), modes: 4 (over y).
Axes of the slice: x: 4, y: 4, z: 4, core: 2. Of those that a mesh axis runs over, the one named last changes fastest.
Arguments:
- activations: bfloat16 [2048, 64, 2048], P('rows', None, 'modes'), may hold values from -6 to 6
- cotangent: bfloat16 [2048, 64, 2048], P('rows', None, 'modes'), may hold values from -6 to 6
- spectral_weight: bfloat16 [64, 64, 64, 128], P('rows', None, None, 'modes'), may hold values from -12 to 12
- linear_weight: bfloat16 [64, 64], replicated, may hold values from -0.75 to 0.75
- bias: float32 [64], replicated, may hold values from -4 to 4
Outputs:
- grad_input: bfloat16 [2048, 64, 2048], P('rows', None, 'modes')
- grad_spectral: float32 [64, 64, 64, 128], P('rows', None, None, 'modes')
- grad_linear: float32 [64, 64], replicated
- grad_bias: float32 [64], replicated
The draws below stay inside these ranges and needn't reach their ends.
All inputs are finite; a program needn't handle non-finite values.
Results may differ from the reference program's by a relative error of at most 0.03.
Values may be sent and summed in bfloat16 or wider, within the bound.
A program may use at most 128 MiB of HBM per device.

```python
import math
import jax
import jax.numpy as jnp
from jax import lax

H = 2048
W = 2048
C = 64
K1 = 64
K2 = 64


def level_of(rng, dims, cuts, least, high):
    def one(position, blocks):
        steps = jax.random.uniform(jax.random.fold_in(jax.random.fold_in(rng, 6), position), (blocks,), jnp.float32, least / len(cuts), high / len(cuts))
        return jnp.repeat(jnp.exp(steps), dims[position] // blocks).reshape((-1,) + (1,) * (len(dims) - position - 1))

    gain = one(*cuts[0])
    for cut in cuts[1:]:
        gain = gain * one(*cut)
    return gain


def gaussian(stream_key, extent, spread, most, pieces=(), kind=jnp.bfloat16):
    drawn = spread * jax.random.normal(stream_key, extent, jnp.float32)
    if pieces:
        drawn = drawn * level_of(stream_key, extent, pieces, -0.22, 0.18)
    return jnp.clip(drawn, -most, most).astype(kind)


def setup_inputs(seed: int = 0) -> dict:
    seeds = jax.random.split(jax.random.key(seed), 6)
    activations = gaussian(seeds[0], (H, C, W), 1.0, 6.0, ((0, 32), (2, 4)))
    cotangent = gaussian(seeds[1], (H, C, W), 1.0, 6.0, ((0, 32), (2, 4)))
    spectral_weight = gaussian(seeds[2], (K1, C, C, 2 * K2), 2.0, 12.0, ((0, 32), (3, 4)))
    linear_weight = gaussian(seeds[3], (C, C), C ** -0.5, 0.75)
    bias = gaussian(seeds[4], (C,), 1.0, 4.0, (), jnp.float32)
    return {"activations": activations, "cotangent": cotangent, "spectral_weight": spectral_weight, "linear_weight": linear_weight, "bias": bias}


HIGHEST_PRECISION = lax.Precision.HIGHEST

def row_angles(freq_count, row_start, row_count, period):
    positions = jnp.arange(freq_count, dtype=jnp.int32)
    frequency = jnp.where(positions < freq_count // 2, positions, positions - freq_count)
    grid_rows = row_start + jnp.arange(row_count, dtype=jnp.int32)
    phases = frequency[:, None] * grid_rows[None, :] % period
    angles = phases.astype(jnp.float32) * (2.0 * math.pi / period)
    return (jnp.cos(angles), jnp.sin(angles))

def column_table(mode_count, col_start, col_count, period):
    mode_ids = jnp.arange(mode_count, dtype=jnp.int32)
    grid_cols = col_start + jnp.arange(col_count, dtype=jnp.int32)
    phases = grid_cols[:, None] * mode_ids[None, :] % period
    angles = phases.astype(jnp.float32) * (2.0 * math.pi / period)
    return jnp.stack([jnp.cos(angles), -jnp.sin(angles)], axis=-1).reshape(col_count, 2 * mode_count)

def column_weights(mode_count):
    mode_ids = jnp.arange(mode_count, dtype=jnp.int32)
    return jnp.repeat(jnp.where(mode_ids == 0, 1.0, 2.0).astype(jnp.float32), 2)

def to_freq(values, cos_rows, sin_rows):
    length = cos_rows.shape[0]
    stacked = jnp.concatenate([cos_rows, sin_rows], axis=0)
    product = jnp.dot(stacked, values.reshape(values.shape[0], -1), precision=HIGHEST_PRECISION, preferred_element_type=jnp.float32)
    halves = product.reshape(2, length, values.shape[1], values.shape[2] // 2, 2)
    real_part = halves[0, ..., 0] + halves[1, ..., 1]
    imag_part = halves[0, ..., 1] - halves[1, ..., 0]
    return jnp.stack([real_part, imag_part], axis=-1).reshape(length, values.shape[1], values.shape[2])

def to_rows(values, cos_cols, sin_cols):
    length = cos_cols.shape[0]
    stacked = jnp.concatenate([cos_cols, sin_cols], axis=0).astype(jnp.float32)
    product = jnp.dot(stacked, values.astype(jnp.float32).reshape(values.shape[0], -1), precision=HIGHEST_PRECISION, preferred_element_type=jnp.float32)
    halves = product.reshape(2, length, values.shape[1], values.shape[2] // 2, 2)
    real_part = halves[0, ..., 0] - halves[1, ..., 1]
    imag_part = halves[0, ..., 1] + halves[1, ..., 0]
    return jnp.stack([real_part, imag_part], axis=-1).reshape(length, values.shape[1], values.shape[2])

def gelu_grad(preact):
    cumulative = 0.5 * (1.0 + jax.scipy.special.erf(preact * 0.7071067811865476))
    density = jnp.exp(-0.5 * preact * preact) * 0.3989422804014327
    return cumulative + preact * density

def reference(activations, cotangent, spectral_weight, linear_weight, bias):
    block_rows = 64
    blocks = H // block_rows
    inv_area = 1.0 / (H * W)
    forward_table = column_table(K2, 0, W, W)
    analysis = forward_table.astype(jnp.bfloat16)
    synthesis = (forward_table.T * column_weights(K2)[:, None]).astype(jnp.bfloat16)
    analysis_wide = analysis.astype(jnp.float32)
    synthesis_wide = synthesis.astype(jnp.float32)
    weight_wide = linear_weight.astype(jnp.float32)
    block_ids = jnp.arange(blocks, dtype=jnp.int32)

    def forward_block(accum, block):
        start = (block * block_rows).astype(jnp.int32)
        field = lax.dynamic_slice_in_dim(activations, start, block_rows, 0).astype(jnp.float32)
        partial_cols = jnp.einsum('hcw,wq->hcq', field, analysis_wide, precision=HIGHEST_PRECISION)
        cos_rows, sin_rows = row_angles(K1, start, block_rows, H)
        return (accum + to_freq(partial_cols, cos_rows, sin_rows), None)
    zero_spec = jnp.zeros((K1, C, 2 * K2), jnp.float32)
    spec_sum, _ = lax.scan(forward_block, zero_spec, block_ids)
    spectrum = spec_sum.astype(jnp.bfloat16)
    parts = spectrum.astype(jnp.float32).reshape(K1, C, K2, 2)
    wparts = spectral_weight.astype(jnp.float32).reshape(K1, C, C, K2, 2)
    real_part = jnp.einsum('kcm,kcom->kom', parts[..., 0], wparts[..., 0]) - jnp.einsum('kcm,kcom->kom', parts[..., 1], wparts[..., 1])
    imag_part = jnp.einsum('kcm,kcom->kom', parts[..., 0], wparts[..., 1]) + jnp.einsum('kcm,kcom->kom', parts[..., 1], wparts[..., 0])
    mixed = jnp.stack([real_part, imag_part], axis=-1).reshape(K1, C, 2 * K2).astype(jnp.bfloat16)
    cos_all, sin_all = row_angles(K1, 0, H, H)
    cos_cols = cos_all.T.astype(jnp.bfloat16)
    sin_cols = sin_all.T.astype(jnp.bfloat16)
    rowfield = to_rows(mixed, cos_cols, sin_cols).astype(jnp.bfloat16)

    def backward_block(carry, block):
        dterm, glin, gbias = carry
        start = (block * block_rows).astype(jnp.int32)
        field = lax.dynamic_slice_in_dim(activations, start, block_rows, 0).astype(jnp.float32)
        grad_out = lax.dynamic_slice_in_dim(cotangent, start, block_rows, 0).astype(jnp.float32)
        rows_block = lax.dynamic_slice_in_dim(rowfield, start, block_rows, 0).astype(jnp.float32)
        spectral = jnp.einsum('hcq,qw->hcw', rows_block, synthesis_wide, precision=HIGHEST_PRECISION) * inv_area
        linear = jnp.einsum('hcw,co->how', field, weight_wide, precision=HIGHEST_PRECISION)
        preact = spectral + linear + bias[None, :, None]
        dpre = (grad_out * gelu_grad(preact)).astype(jnp.bfloat16)
        dpre_wide = dpre.astype(jnp.float32)
        partial_cols = jnp.einsum('hcw,qw->hcq', dpre_wide, synthesis_wide, precision=HIGHEST_PRECISION) * inv_area
        cos_rows, sin_rows = row_angles(K1, start, block_rows, H)
        dterm = dterm + to_freq(partial_cols, cos_rows, sin_rows)
        glin = glin + jnp.einsum('hcw,how->co', field, dpre_wide, precision=HIGHEST_PRECISION)
        gbias = gbias + lax.optimization_barrier(jnp.sum(dpre_wide, axis=(0, 2)))
        return ((dterm, glin, gbias), dpre)
    carry_init = (zero_spec, jnp.zeros((C, C), jnp.float32), jnp.zeros((C,), jnp.float32))
    (dterm, glin, gbias), dpre_blocks = lax.scan(backward_block, carry_init, block_ids)
    dmixed = dterm.astype(jnp.bfloat16)
    dparts = dmixed.astype(jnp.float32).reshape(K1, C, K2, 2)
    grad_real = parts[:, :, None, :, 0] * dparts[:, None, :, :, 0] + parts[:, :, None, :, 1] * dparts[:, None, :, :, 1]
    grad_imag = parts[:, :, None, :, 0] * dparts[:, None, :, :, 1] - parts[:, :, None, :, 1] * dparts[:, None, :, :, 0]
    grad_spectral = jnp.stack([grad_real, grad_imag], axis=-1).reshape(K1, C, C, 2 * K2)
    dspec_real = jnp.einsum('kcom,kom->kcm', wparts[..., 0], dparts[..., 0]) + jnp.einsum('kcom,kom->kcm', wparts[..., 1], dparts[..., 1])
    dspec_imag = jnp.einsum('kcom,kom->kcm', wparts[..., 0], dparts[..., 1]) - jnp.einsum('kcom,kom->kcm', wparts[..., 1], dparts[..., 0])
    dspectrum = jnp.stack([dspec_real, dspec_imag], axis=-1).reshape(K1, C, 2 * K2).astype(jnp.bfloat16)
    drows = to_rows(dspectrum, cos_cols, sin_cols).astype(jnp.bfloat16)

    def input_block(block):
        start = (block * block_rows).astype(jnp.int32)
        rows_block = lax.dynamic_slice_in_dim(drows, start, block_rows, 0).astype(jnp.float32)
        dpre_wide = dpre_blocks[block].astype(jnp.float32)
        spectral_part = jnp.einsum('hcq,wq->hcw', rows_block, analysis_wide, precision=HIGHEST_PRECISION)
        local_part = jnp.einsum('how,co->hcw', dpre_wide, weight_wide, precision=HIGHEST_PRECISION)
        return (spectral_part + local_part).astype(jnp.bfloat16)
    grad_input = lax.map(input_block, block_ids).reshape(H, C, W)
    return (grad_input, grad_spectral, glin / H, gbias / H)
```

```python
import functools
import math

import jax
import jax.numpy as jnp
import numpy as np
from jax import lax
from jax.experimental import pallas as pl
from jax.experimental.pallas import tpu as pltpu
from jax.sharding import PartitionSpec as P

MESH = pl.DeviceIdType.MESH
BF = jnp.bfloat16
F32 = jnp.float32
VMEM = pl.BlockSpec(memory_space=pltpu.VMEM)
LIMIT = 60 * 1024 * 1024


def dot(a, b):
    return jnp.dot(a, b, preferred_element_type=F32)


def lanes_of(shape):
    return lax.broadcasted_iota(jnp.int32, shape, len(shape) - 1)


def row_table(row_index):
    slot = jnp.arange(64, dtype=jnp.int32)
    core, z, x, jj = slot // 32, (slot // 8) % 4, (slot // 2) % 4, slot % 2
    mode = x * 16 + z * 4 + core * 2 + jj
    freq = jnp.where(mode < 32, mode, mode - 64)
    rows = row_index * 64 + jnp.arange(64, dtype=jnp.int32)
    ang = (freq[:, None] * rows[None, :] % 2048).astype(F32) * (2.0 * math.pi / 2048)
    return jnp.cos(ang), jnp.sin(ang)


def col_tables(mode_index):
    q = jnp.arange(128, dtype=jnp.int32)
    cols = mode_index * 512 + jnp.arange(512, dtype=jnp.int32)
    ang = ((cols[:, None] * (q // 2)[None, :]) % 2048).astype(F32) * (2.0 * math.pi / 2048)
    even = (q % 2 == 0)[None, :]
    c, s = jnp.cos(ang), jnp.sin(ang)
    ana = jnp.where(even, c, -s).astype(BF)
    swap = jnp.where(even, -s, -c).astype(BF)
    return ana, swap


def kron8(c, s):
    up = (lax.broadcasted_iota(jnp.int32, (512, 64), 0) // 8 == lax.broadcasted_iota(jnp.int32, (512, 64), 1)).astype(BF)
    wide = (lax.broadcasted_iota(jnp.int32, (64, 512), 1) // 8 == lax.broadcasted_iota(jnp.int32, (64, 512), 0)).astype(BF)
    keep = lax.broadcasted_iota(jnp.int32, (512, 512), 0) % 8 == lax.broadcasted_iota(jnp.int32, (512, 512), 1) % 8
    parts = []
    for t in (c, s):
        parts.append(jnp.where(keep, dot(dot(up, t).astype(BF), wide), 0.0).astype(BF))
    return parts


def forward(field_ref, tab_ref, rmat_ref, tile_ref, out_ref):
    tab = tab_ref[...]
    for a in range(4):
        lhs = field_ref[:, 16 * a : 16 * a + 16, :].reshape(1024, 512)
        p = dot(lhs, tab).reshape(64, 2, 8, 256)
        cols = []
        for g in range(2):
            pg = p[:, g].reshape(512, 256)
            cols.append(jnp.concatenate([pg[:, :128], pg[:, 128:]], axis=0).astype(BF))
        o = dot(rmat_ref[...], jnp.concatenate(cols, axis=1))
        for g in range(2):
            tile_ref[a, :, 8 * g : 8 * g + 8, :] = o[:, 128 * g : 128 * g + 128].reshape(64, 8, 128)
    for m in range(4):
        exchange(lambda a: tile_ref[a].reshape(1024, 128), m, lambda v: store_mode(out_ref, m, v))


def store_mode(out_ref, m, v):
    v = v.reshape(2, 4, 4, 2, 16, 128).astype(BF)
    for core in range(2):
        out_ref[core, m] = v[core]


def exchange(get, m, put):
    block = lanes_of((1024, 128)) // 32
    total = None
    for a in range(4):
        v = get(a)
        shift = (32 * (a - m)) % 128
        if shift:
            v = pltpu.roll(v, shift, 1)
        total = v if total is None else jnp.where(block == a, v, total)
    put(total)


def inverse(g_ref, imat_ref, out_ref):
    even = lanes_of((1024, 128)) % 2 == 0
    for b in range(4):
        def build(v, b=b):
            swapped = jnp.where(even, -pltpu.roll(v, 127, 1), pltpu.roll(v, 1, 1))
            v3, s3 = v.reshape(64, 16, 128), swapped.reshape(64, 16, 128)
            cols = []
            for g in range(2):
                cols.append(
                    jnp.concatenate(
                        [v3[:, 8 * g : 8 * g + 8].reshape(512, 128), s3[:, 8 * g : 8 * g + 8].reshape(512, 128)], axis=0
                    ).astype(BF)
                )
            o = dot(imat_ref[...], jnp.concatenate(cols, axis=1))
            both = jnp.concatenate([o[:, :128].reshape(64, 8, 128), o[:, 128:].reshape(64, 8, 128)], axis=1)
            out_ref[:, 16 * b : 16 * b + 16, :] = both.astype(BF)

        def get(m):
            parts = [g_ref[core, m].reshape(512, 128) for core in range(2)]
            return jnp.concatenate(parts, axis=0).astype(F32)

        exchange(get, b, build)


def gelu_grad(z):
    e = jnp.exp(-0.5 * z * z)
    az = jnp.abs(z)
    t = 1.0 / (1.0 + (0.3275911 * 0.7071067811865476) * az)
    poly = t * (0.5 * 0.254829592 + t * (-0.5 * 0.284496736 + t * (0.5 * 1.421413741 + t * (-0.5 * 1.453152027 + t * (0.5 * 1.061405429)))))
    tail = poly * e
    return jnp.where(z >= 0, 1.0 - tail, tail) + (0.3989422804014327 * z) * e


def first_kernel(act_ref, tab_ref, crow_ref, srow_ref, crow_t_ref, srow_t_ref, out_ref, rmat_ref, imat_ref, tile_ref):
    c, s = kron8(crow_ref[...], srow_ref[...])
    rmat_ref[:, :512] = c
    rmat_ref[:, 512:] = s
    c, s = kron8(crow_t_ref[...], srow_t_ref[...])
    imat_ref[:, :512] = c
    imat_ref[:, 512:] = s
    forward(act_ref, tab_ref, rmat_ref, tile_ref, out_ref)


def middle_kernel(g_ref, act_ref, cot_ref, rmat_ref, imat_ref, syn_ref, lw_t_ref, bias_ref, tab_ref,
                  dpre_ref, out_ref, lin_ref, rf_ref, tile_ref):
    inverse(g_ref, imat_ref, rf_ref)
    lin_ref[...] = jnp.zeros_like(lin_ref)
    bias = bias_ref[...]

    def row(h, _):
        lhs = jnp.concatenate([rf_ref[h], lw_t_ref[...]], axis=1)
        rhs = jnp.concatenate([syn_ref[...], act_ref[h]], axis=0)
        pre = dot(lhs, rhs) + bias
        d = (cot_ref[h].astype(F32) * gelu_grad(pre)).astype(BF)
        dpre_ref[h] = d
        both = jnp.concatenate([act_ref[h], jnp.ones((16, 512), BF)], axis=0)
        lin_ref[...] += lax.dot_general(both, d, (((1,), (1,)), ((), ())), preferred_element_type=F32)
        return 0

    lax.fori_loop(0, 64, row, 0)
    forward(dpre_ref, tab_ref, rmat_ref, tile_ref, out_ref)


def last_kernel(g_ref, dpre_ref, imat_ref, ana_ref, lw_ref, s_ref, d_ref, gin_ref, gspec_ref, rf_ref):
    inverse(g_ref, imat_ref, rf_ref)

    def row(h, _):
        lhs = jnp.concatenate([rf_ref[h], lw_ref[...]], axis=1)
        rhs = jnp.concatenate([ana_ref[...], dpre_ref[h]], axis=0)
        gin_ref[h] = dot(lhs, rhs).astype(BF)
        return 0

    lax.fori_loop(0, 64, row, 0)
    for jj in range(2):
        re, im = duplicate(s_ref[jj])
        d = d_ref[jj]
        even = lax.broadcasted_iota(jnp.int32, (32, 64), 0) % 2 == 0
        dsw = jnp.where(even, pltpu.roll(d, 31, 0), -pltpu.roll(d, 1, 0))
        for c in range(64):
            gspec_ref[jj, c] = re[:, c : c + 1] * d + im[:, c : c + 1] * dsw


def duplicate(v):
    even = lax.broadcasted_iota(jnp.int32, v.shape, 0) % 2 == 0
    return jnp.where(even, v, pltpu.roll(v, 1, 0)), jnp.where(even, pltpu.roll(v, v.shape[0] - 1, 0), v)


def to_columns(block):
    rows = [block if a == 0 else pltpu.roll(block, (128 - 32 * a) % 128, 1) for a in range(4)]
    stacked = jnp.concatenate(rows + rows, axis=0)
    return stacked.T[:32, :64]


def to_block(cols):
    wide = jnp.concatenate([cols, cols], axis=1)
    square = jnp.concatenate([wide] * 4, axis=0).T
    out = None
    block = lanes_of((16, 128)) // 32
    for a in range(4):
        v = square[16 * a : 16 * a + 16, :]
        out = v if out is None else jnp.where(block == a, v, out)
    return out


def weigh(s, w_ref, jj):
    re, im = duplicate(s)
    t1 = jnp.zeros((32, 64), F32)
    t2 = jnp.zeros((32, 64), F32)
    for c in range(64):
        w = w_ref[jj, c].astype(F32)
        t1 += re[:, c : c + 1] * w
        t2 += im[:, c : c + 1] * w
    even = lax.broadcasted_iota(jnp.int32, (32, 64), 0) % 2 == 0
    return t1 + jnp.where(even, -pltpu.roll(t2, 31, 0), pltpu.roll(t2, 1, 0))


def weigh_back(d, w_ref, jj):
    even = lax.broadcasted_iota(jnp.int32, (32, 64), 0) % 2 == 0
    dsw = jnp.where(even, pltpu.roll(d, 31, 0), pltpu.roll(d, 1, 0))
    lane = lanes_of((32, 64))
    u1 = jnp.zeros((32, 64), F32)
    u2 = jnp.zeros((32, 64), F32)
    for c in range(64):
        w = w_ref[jj, c].astype(F32)
        u1 = jnp.where(lane == c, jnp.sum(w * d, axis=1, keepdims=True), u1)
        u2 = jnp.where(lane == c, jnp.sum(w * dsw, axis=1, keepdims=True), u2)
    return jnp.where(even, u1 + pltpu.roll(u1, 31, 0), pltpu.roll(u2, 1, 0) - u2)


def place():
    r, y = lax.axis_index("rows"), lax.axis_index("modes")
    return r // 8, y, (r // 2) % 4, r % 2


def device(x, y, z, core):
    return ((x * 4 + z) * 2 + core, y)


def greet():
    x, y, z, core = place()
    barrier = pltpu.get_barrier_semaphore()
    peers = [device(x, y, z, 1 - core)]
    for d in range(1, 4):
        peers += [device((x + d) % 4, y, z, core), device(x, (y + d) % 4, z, core), device(x, y, (z + d) % 4, core)]
    for p in peers:
        pl.semaphore_signal(barrier, inc=1, device_id=p, device_id_type=MESH)
    pl.semaphore_wait(barrier, len(peers))


def remote(src, dst, send, recv, target):
    return pltpu.make_async_remote_copy(src_ref=src, dst_ref=dst, send_sem=send, recv_sem=recv, device_id=target, device_id_type=MESH)


def reduce_scatter(t_ref, b0, a1, b1, a2, b2, a3, b3, send, recv):
    x, y, z, core = place()
    pending = []
    first = []
    for i, d in enumerate((1, 2, 3, 0)):
        yt = (y + d) % 4
        cp = remote(t_ref.at[1 - core, yt], b0.at[yt], send.at[i], recv.at[i], device(x, y, z, 1 - core))
        cp.start()
        first.append(cp)
    pending += first
    stage = []
    for i, d in enumerate((1, 2, 3, 0)):
        yt = (y + d) % 4
        first[i].wait_recv()
        a1[yt] = (t_ref[core, yt].astype(F32) + b0[yt].astype(F32)).astype(BF)
        if d:
            cp = remote(a1.at[yt], b1.at[d - 1], send.at[3 + d], recv.at[3 + d], device(x, yt, z, core))
            cp.start()
            stage.append(cp)
    for cp in stage:
        cp.wait_recv()
    pending += stage
    stage = []
    for d in (1, 2, 3, 0):
        zt = (z + d) % 4
        v = a1[y, zt].astype(F32)
        for k in range(3):
            v += b1[k, zt].astype(F32)
        a2[zt] = v.astype(BF)
        if d:
            cp = remote(a2.at[zt], b2.at[d - 1], send.at[6 + d], recv.at[6 + d], device(x, y, zt, core))
            cp.start()
            stage.append(cp)
    for cp in stage:
        cp.wait_recv()
    pending += stage
    stage = []
    for d in (1, 2, 3, 0):
        xt = (x + d) % 4
        v = a2[z, xt].astype(F32)
        for k in range(3):
            v += b2[k, xt].astype(F32)
        a3[xt] = v.astype(BF)
        if d:
            cp = remote(a3.at[xt], b3.at[d - 1], send.at[9 + d], recv.at[9 + d], device(xt, y, z, core))
            cp.start()
            stage.append(cp)
        else:
            own = v
    for cp in stage:
        cp.wait_recv()
    pending += stage
    for k in range(3):
        own += b3[k].astype(F32)
    for cp in pending:
        cp.wait_send()
    return own


def all_gather(g_ref, send, recv):
    x, y, z, core = place()
    pending = []

    def stage(base, target, source, mine, theirs):
        cps = []
        for d in range(1, 4):
            out = remote(mine, mine, send.at[base + d], recv.at[base + d], target(d))
            out.start()
            cps.append(out)
        pending.extend(cps)
        return [remote(theirs(d), theirs(d), send.at[base + d], recv.at[base + d], source(d)) for d in range(1, 4)]

    for cp in stage(-1, lambda d: device((x + d) % 4, y, z, core), lambda d: device((x - d) % 4, y, z, core),
                    g_ref.at[core, y, z, x], lambda d: g_ref.at[core, y, z, (x + 4 - d) % 4]):
        cp.wait_recv()
    for cp in stage(2, lambda d: device(x, y, (z + d) % 4, core), lambda d: device(x, y, (z - d) % 4, core),
                    g_ref.at[core, y, z], lambda d: g_ref.at[core, y, (z + 4 - d) % 4]):
        cp.wait_recv()
    waits = stage(5, lambda d: device(x, (y + d) % 4, z, core), lambda d: device(x, (y - d) % 4, z, core),
                  g_ref.at[core, y], lambda d: g_ref.at[core, (y + 4 - d) % 4])
    last = []
    for d in range(4):
        ys = (y + 4 - d) % 4
        if d:
            waits[d - 1].wait_recv()
        cp = remote(g_ref.at[core, ys], g_ref.at[core, ys], send.at[9 + d], recv.at[9 + d], device(x, y, z, 1 - core))
        cp.start()
        last.append(cp)
    for d in range(4):
        ys = (y + 4 - d) % 4
        remote(g_ref.at[1 - core, ys], g_ref.at[1 - core, ys], send.at[9 + d], recv.at[9 + d], device(x, y, z, 1 - core)).wait_recv()
    for cp in pending + last:
        cp.wait_send()


def forward_exchange(t_ref, w_ref, s_ref, g_ref, b0, a1, b1, a2, b2, a3, b3, send, recv, send2, recv2):
    x, y, z, core = place()
    greet()
    own = reduce_scatter(t_ref, b0, a1, b1, a2, b2, a3, b3, send, recv)
    for jj in range(2):
        s = to_columns(own[jj].astype(BF).astype(F32))
        s_ref[jj] = s
        g_ref[core, y, z, x, jj] = to_block(weigh(s, w_ref, jj)).astype(BF)
    all_gather(g_ref, send2, recv2)


def backward_exchange(t_ref, w_ref, lin_ref, d_ref, g_ref, lin_out_ref,
                      b0, a1, b1, a2, b2, a3, b3, part, send, recv, send2, recv2, send3, recv3):
    x, y, z, core = place()
    greet()
    own = reduce_scatter(t_ref, b0, a1, b1, a2, b2, a3, b3, send, recv)
    for jj in range(2):
        d = to_columns(own[jj].astype(BF).astype(F32))
        d_ref[jj] = d
        g_ref[core, y, z, x, jj] = to_block(weigh_back(d, w_ref, jj)).astype(BF)
    all_gather(g_ref, send2, recv2)
    part[0, core] = lin_ref[...]
    cp = remote(part.at[0, core], part.at[0, core], send3.at[0], recv3.at[0], device(x, y, z, 1 - core))
    cp.start()
    remote(part.at[0, 1 - core], part.at[0, 1 - core], send3.at[0], recv3.at[0], device(x, y, z, 1 - core)).wait_recv()
    cp.wait_send()
    v = part[0, 0] + part[0, 1]
    for i, (me, at) in enumerate(((y, lambda p: device(x, p, z, core)), (z, lambda p: device(x, y, p, core)), (x, lambda p: device(p, y, z, core)))):
        part[i + 1, me] = v
        cps = []
        for d in range(1, 4):
            cp = remote(part.at[i + 1, me], part.at[i + 1, me], send3.at[3 * i + d], recv3.at[3 * i + d], at((me + d) % 4))
            cp.start()
            cps.append(cp)
        for d in range(1, 4):
            src = (me + 4 - d) % 4
            remote(part.at[i + 1, src], part.at[i + 1, src], send3.at[3 * i + d], recv3.at[3 * i + d], at(src)).wait_recv()
        for cp in cps:
            cp.wait_send()
        v = part[i + 1, 0] + part[i + 1, 1] + part[i + 1, 2] + part[i + 1, 3]
    lin_out_ref[...] = v * (1.0 / 2048)


def exchange_scratch():
    dma = pltpu.SemaphoreType.DMA
    return [
        pltpu.VMEM((4, 4, 4, 2, 16, 128), BF),
        pltpu.VMEM((4, 4, 4, 2, 16, 128), BF),
        pltpu.VMEM((3, 4, 4, 2, 16, 128), BF),
        pltpu.VMEM((4, 4, 2, 16, 128), BF),
        pltpu.VMEM((3, 4, 2, 16, 128), BF),
        pltpu.VMEM((4, 2, 16, 128), BF),
        pltpu.VMEM((3, 2, 16, 128), BF),
    ], [dma((13,))] * 4


def call(kernel, outs, scratch, args, collective=None):
    params = dict(vmem_limit_bytes=LIMIT)
    if collective is not None:
        params.update(collective_id=collective, has_side_effects=True)
    return pl.pallas_call(
        kernel,
        out_shape=[jax.ShapeDtypeStruct(s, t) for s, t in outs],
        in_specs=[VMEM] * len(args),
        out_specs=[VMEM] * len(outs),
        scratch_shapes=scratch,
        compiler_params=pltpu.CompilerParams(**params),
    )(*args)


SPEC = (2, 4, 4, 4, 2, 16, 128)


def body(activations, cotangent, spectral_weight, linear_weight, bias):
    row_index, mode_index = lax.axis_index("rows"), lax.axis_index("modes")
    crow, srow = row_table(row_index)
    crow, srow = crow.astype(BF), srow.astype(BF)
    ana, swap = col_tables(mode_index)
    tab = jnp.concatenate([ana, swap], axis=1)
    weights = jnp.where(jnp.arange(128) < 2, 1.0, 2.0).astype(BF) * BF(2.0**-22)
    dtab = tab * jnp.concatenate([weights, weights])[None, :]
    syn = (ana * weights[None, :]).T
    w = spectral_weight.transpose(0, 1, 3, 2)

    tile = pltpu.VMEM((4, 64, 16, 128), F32)
    t, rmat, imat = call(
        first_kernel, [(SPEC, BF), ((512, 1024), BF), ((512, 1024), BF)], [tile],
        [activations, tab, crow, srow, crow.T, srow.T],
    )
    buffers, sems = exchange_scratch()
    s, g = call(forward_exchange, [((2, 32, 64), F32), (SPEC, BF)], buffers + sems, [t, w], 0)
    dpre, t, lin = call(
        middle_kernel, [((64, 64, 512), BF), (SPEC, BF), ((80, 64), F32)],
        [pltpu.VMEM((64, 64, 128), BF), tile],
        [g, activations, cotangent, rmat, imat, syn, linear_weight.T, bias[:, None], dtab],
    )
    d, g, lin = call(
        backward_exchange, [((2, 32, 64), F32), (SPEC, BF), ((80, 64), F32)],
        buffers + [pltpu.VMEM((4, 4, 80, 64), F32)] + sems + [pltpu.SemaphoreType.DMA((10,))] * 2, [t, w, lin], 1,
    )
    gin, gspec = call(
        last_kernel, [((64, 64, 512), BF), ((2, 64, 32, 64), F32)], [pltpu.VMEM((64, 64, 128), BF)],
        [g, dpre, imat, ana.T, linear_weight, s, d],
    )
    return gin, gspec.transpose(0, 1, 3, 2), lin[:64], lin[64]


def solution(mesh):
    return jax.shard_map(
        body,
        mesh=mesh,
        in_specs=(
            P("rows", None, "modes"),
            P("rows", None, "modes"),
            P("rows", None, None, "modes"),
            P(),
            P(),
        ),
        out_specs=(P("rows", None, "modes"), P("rows", None, None, "modes"), P(), P()),
        check_vma=False,
    )
```

```python
import math

import jax
import jax.numpy as jnp
import numpy as np
from jax import lax
from jax.experimental import pallas as pl
from jax.experimental.pallas import tpu as pltpu
from jax.sharding import PartitionSpec as P

MESH = pl.DeviceIdType.MESH
BF = jnp.bfloat16
F32 = jnp.float32
VMEM = pl.BlockSpec(memory_space=pltpu.VMEM)
LIMIT = 60 * 1024 * 1024


def dot(a, b):
    return jnp.dot(a, b, preferred_element_type=F32)


def lanes_of(shape):
    return lax.broadcasted_iota(jnp.int32, shape, len(shape) - 1)


def column_constants():
    k = np.arange(128) // 2
    w = np.arange(2048)
    ang = ((w[:, None] * k[None, :]) % 2048) * (2.0 * math.pi / 2048)
    even = (np.arange(128) % 2 == 0)[None, :]
    ana = np.where(even, np.cos(ang), -np.sin(ang))
    swap = np.where(even, -np.sin(ang), -np.cos(ang))
    return np.concatenate([ana, swap], axis=1).reshape(4, 512, 256).astype(np.float32).astype(jnp.bfloat16)


def row_constants():
    slot = np.arange(64)
    core, z, x, jj = slot // 32, (slot // 8) % 4, (slot // 2) % 4, slot % 2
    mode = x * 16 + z * 4 + core * 2 + jj
    freq = np.where(mode < 32, mode, mode - 64)
    rows = np.arange(2048).reshape(32, 64)
    ang = ((freq[None, :, None] * rows[:, None, :]) % 2048) * (2.0 * math.pi / 2048)
    return np.stack([np.cos(ang), np.sin(ang)], axis=1).astype(np.float32).astype(jnp.bfloat16)


def kron8(table, flip):
    up = (lax.broadcasted_iota(jnp.int32, (512, 64), 0) // 8 == lax.broadcasted_iota(jnp.int32, (512, 64), 1)).astype(BF)
    wide = (lax.broadcasted_iota(jnp.int32, (64, 512), 1) // 8 == lax.broadcasted_iota(jnp.int32, (64, 512), 0)).astype(BF)
    keep = lax.broadcasted_iota(jnp.int32, (512, 512), 0) % 8 == lax.broadcasted_iota(jnp.int32, (512, 512), 1) % 8
    left = lax.dot_general(up, table, (((1,), (1 if flip else 0,)), ((), ())), preferred_element_type=F32).astype(BF)
    return jnp.where(keep, dot(left, wide), 0.0).astype(BF)


def place():
    r, y = lax.axis_index("rows"), lax.axis_index("modes")
    x, z, core = r // 8, (r // 2) % 4, r % 2
    return y * (1 - core) + z * core, z * (1 - core) + y * core, x, core


def device(p, q, x, core):
    y, z = p * (1 - core) + q * core, q * (1 - core) + p * core
    return ((x * 4 + z) * 2 + core, y)


def sibling(p, q, x, core):
    return device(q, p, x, 1 - core)


def signal_peers():
    p, q, x, core = place()
    barrier = pltpu.get_barrier_semaphore()
    pl.semaphore_signal(barrier, inc=1, device_id=sibling(p, q, x, core), device_id_type=MESH)
    for d in range(1, 4):
        pl.semaphore_signal(barrier, inc=1, device_id=device((p + d) % 4, q, x, core), device_id_type=MESH)
    for k in range(1, 16):
        pl.semaphore_signal(barrier, inc=1, device_id=device(p, (q + k // 4) % 4, (x + k % 4) % 4, core), device_id_type=MESH)


def wait_peers():
    pl.semaphore_wait(pltpu.get_barrier_semaphore(), 19)


def remote(src, dst, send, recv, target):
    return pltpu.make_async_remote_copy(src_ref=src, dst_ref=dst, send_sem=send, recv_sem=recv, device_id=target, device_id_type=MESH)


def columns(block, tab, xs_ref, h0, count):
    prod = dot(block.reshape(count * 64, 512), tab).reshape(count, 8, 8, 256)
    for a in range(4):
        for g in range(2):
            v = prod[:, 2 * a + g].reshape(count * 8, 256).astype(BF)
            xs_ref[g, pl.ds(h0 * 8, count * 8), 128 * a : 128 * a + 128] = v[:, :128]
            xs_ref[g, pl.ds(512 + h0 * 8, count * 8), 128 * a : 128 * a + 128] = v[:, 128:]


def row_modes(xs_ref, rmat_ref, t_ref, owner):
    block = lanes_of((256, 128)) // 32
    for g in range(2):
        o = dot(rmat_ref[pl.ds(pl.multiple_of(owner * 256, 256), 256), :], xs_ref[g])
        for m in range(4):
            total = None
            for a in range(4):
                v = o[:, 128 * a : 128 * a + 128]
                shift = (32 * (a - m)) % 128
                if shift:
                    v = pltpu.roll(v, shift, 1)
                total = v if total is None else jnp.where(block == a, v, total)
            total = total.astype(BF).reshape(4, 4, 16, 128)
            for z in range(4):
                t_ref[owner, m * (1 - owner) + z * owner, z * (1 - owner) + m * owner, :, g] = total[z]


def inverse(g_ref, imat_ref, out_ref):
    even = lanes_of((512, 128)) % 2 == 0
    block = lanes_of((512, 128)) // 32
    for b in range(4):
        cols = []
        for g in range(2):
            total = None
            for m in range(4):
                parts = [g_ref[0, m, :, :, g].reshape(256, 128)]
                parts += [g_ref[1, z, m, :, g].reshape(64, 128) for z in range(4)]
                v = jnp.concatenate(parts, axis=0).astype(F32)
                shift = (32 * (m - b)) % 128
                if shift:
                    v = pltpu.roll(v, shift, 1)
                total = v if total is None else jnp.where(block == m, v, total)
            swapped = jnp.where(even, -pltpu.roll(total, 127, 1), pltpu.roll(total, 1, 1))
            cols.append(jnp.concatenate([total.astype(BF), swapped.astype(BF)], axis=0))
        o = dot(imat_ref[...], jnp.concatenate(cols, axis=1))
        both = jnp.concatenate([o[:, :128].reshape(64, 8, 128), o[:, 128:].reshape(64, 8, 128)], axis=1)
        out_ref[:, 16 * b : 16 * b + 16, :] = both.astype(BF)


def gelu_grad(z):
    e = jnp.exp(-0.5 * z * z)
    t = 1.0 / (1.0 + (0.3275911 * 0.7071067811865476) * jnp.abs(z))
    poly = t * (0.5 * 0.254829592 + t * (-0.5 * 0.284496736 + t * (0.5 * 1.421413741 + t * (-0.5 * 1.453152027 + t * (0.5 * 1.061405429)))))
    tail = poly * e
    return jnp.where(z >= 0, 1.0 - tail, tail) + (0.3989422804014327 * z) * e


def duplicate(v):
    even = lax.broadcasted_iota(jnp.int32, v.shape, 0) % 2 == 0
    return jnp.where(even, v, pltpu.roll(v, 1, 0)), jnp.where(even, pltpu.roll(v, v.shape[0] - 1, 0), v)


def to_columns(block):
    turned = [[block[g] if a == 0 else pltpu.roll(block[g], 128 - 32 * a, 1) for g in range(2)] for a in range(4)]
    out = []
    for jj in range(2):
        rows = [turned[a][g][8 * jj : 8 * jj + 8] for a in range(4) for g in range(2)]
        out.append(jnp.concatenate(rows + rows, axis=0).T[:32, :64])
    return out


def to_block(cols):
    block = lanes_of((8, 128)) // 32
    parts = []
    for v in cols:
        square = jnp.concatenate([jnp.concatenate([v, v], axis=1)] * 4, axis=0).T
        parts.append([])
        for g in range(2):
            out = square[8 * g : 8 * g + 8]
            for a in range(1, 4):
                out = jnp.where(block == a, square[16 * a + 8 * g : 16 * a + 8 * g + 8], out)
            parts[-1].append(out)
    return [jnp.concatenate([parts[0][g], parts[1][g]], axis=0) for g in range(2)]


def weigh(s, w_ref, jj):
    re, im = duplicate(s)
    t1 = jnp.zeros((32, 64), F32)
    t2 = jnp.zeros((32, 64), F32)
    for c in range(64):
        w = w_ref[jj, c].astype(F32)
        t1 += re[:, c : c + 1] * w
        t2 += im[:, c : c + 1] * w
    even = lax.broadcasted_iota(jnp.int32, (32, 64), 0) % 2 == 0
    return t1 + jnp.where(even, -pltpu.roll(t2, 31, 0), pltpu.roll(t2, 1, 0))


def weigh_back(d, w_ref, jj):
    even = lax.broadcasted_iota(jnp.int32, (32, 64), 0) % 2 == 0
    dsw = jnp.where(even, pltpu.roll(d, 31, 0), pltpu.roll(d, 1, 0))
    lane = lanes_of((32, 64))
    u1 = jnp.zeros((32, 64), F32)
    u2 = jnp.zeros((32, 64), F32)
    for c in range(64):
        w = w_ref[jj, c].astype(F32)
        u1 = jnp.where(lane == c, jnp.sum(w * d, axis=1, keepdims=True), u1)
        u2 = jnp.where(lane == c, jnp.sum(w * dsw, axis=1, keepdims=True), u2)
    return jnp.where(even, u1 + pltpu.roll(u1, 31, 0), pltpu.roll(u2, 1, 0) - u2)


def start_core(t_ref, b0, send, recv):
    p, q, x, core = place()
    cps = []
    for d in (1, 2, 3, 0):
        cp = remote(t_ref.at[1 - core, (q + d) % 4], b0.at[(q + d) % 4], send.at[d], recv.at[d], sibling(p, q, x, core))
        cp.start()
        cps.append(cp)
    return cps


def reduce_scatter(t_ref, bufs, send, recv, between=lambda i: None):
    b0, a1, b1, a2, b2 = bufs
    p, q, x, core = place()
    pending = []
    for d in (1, 2, 3, 0):
        pt = (p + d) % 4
        remote(b0.at[pt], b0.at[pt], send.at[d], recv.at[d], sibling(p, q, x, core)).wait_recv()
        a1[pt] = (t_ref[core, pt].astype(F32) + b0[pt].astype(F32)).astype(BF)
        if d:
            cp = remote(a1.at[pt], b1.at[d - 1], send.at[3 + d], recv.at[3 + d], device(pt, q, x, core))
            cp.start()
            pending.append(cp)
    between(0)
    for cp in pending:
        cp.wait_recv()
    a2[...] = (a1[p].astype(F32) + b1[0].astype(F32) + b1[1].astype(F32) + b1[2].astype(F32)).astype(BF)
    stage = []
    for k in range(1, 16):
        qt, xt = (q + k // 4) % 4, (x + k % 4) % 4
        cp = remote(a2.at[qt, xt], b2.at[k - 1], send.at[6 + k], recv.at[6 + k], device(p, qt, xt, core))
        cp.start()
        stage.append(cp)
    own = a1[p, q, x].astype(F32)
    for k in range(3):
        own += b1[k, q, x].astype(F32)
    between(1)
    for cp in stage:
        cp.wait_recv()
    for k in range(15):
        own += b2[k].astype(F32)
    for d in range(4):
        remote(t_ref.at[1 - core, (q + d) % 4], b0.at[(q + d) % 4], send.at[d], recv.at[d], sibling(p, q, x, core)).wait_send()
    for cp in pending + stage:
        cp.wait_send()
    return own


def all_gather(g_ref, send, recv, between=lambda i: None):
    p, q, x, core = place()
    pending = []
    mine = g_ref.at[core, p, q, x]
    for k in range(1, 16):
        cp = remote(mine, mine, send.at[6 + k], recv.at[6 + k], device(p, (q + k // 4) % 4, (x + k % 4) % 4, core))
        cp.start()
        pending.append(cp)
    between(2)
    for k in range(1, 16):
        qs, xs = (q + 4 - k // 4) % 4, (x + 4 - k % 4) % 4
        theirs = g_ref.at[core, p, qs, xs]
        remote(theirs, theirs, send.at[6 + k], recv.at[6 + k], device(p, qs, xs, core)).wait_recv()
    mine = g_ref.at[core, p]
    for d in range(1, 4):
        cp = remote(mine, mine, send.at[3 + d], recv.at[3 + d], device((p + d) % 4, q, x, core))
        cp.start()
        pending.append(cp)
    between(3)
    for d in range(4):
        ps = (p + 4 - d) % 4
        theirs = g_ref.at[core, ps]
        if d:
            remote(theirs, theirs, send.at[3 + d], recv.at[3 + d], device(ps, q, x, core)).wait_recv()
        cp = remote(theirs, theirs, send.at[d], recv.at[d], sibling(p, q, x, core))
        cp.start()
        pending.append(cp)
    between(4)
    for d in range(4):
        theirs = g_ref.at[1 - core, (q + 4 - d) % 4]
        remote(theirs, theirs, send.at[d], recv.at[d], sibling(p, q, x, core)).wait_recv()
    for cp in pending:
        cp.wait_send()


def main_kernel(act_hbm, cot_hbm, w_hbm, coltab_hbm, rowtab_hbm, lw_ref, bias_ref,
                dpre_hbm, s_ref, d_ref, g2_ref, lin_out_ref, imat_ref,
                act, cot, w_ref, tab, dtab, syn, rowtab, rmat, lw_t, xs, rf, dpre, lin, t1, t2, g1, part,
                b0, a1, b1, a2, b2, c0, e1, c1, e2, c2,
                in_sem, out_sem, send1, recv1, send2, recv2, send3, recv3, send4, recv4, send5, recv5):
    p, q, x, core = place()
    signal_peers()
    row_dev, mode_dev = lax.axis_index("rows"), lax.axis_index("modes")
    loads = [
        pltpu.make_async_copy(coltab_hbm.at[mode_dev], tab, in_sem.at[0]),
        pltpu.make_async_copy(rowtab_hbm.at[row_dev], rowtab, in_sem.at[1]),
    ]
    loads += [pltpu.make_async_copy(act_hbm.at[pl.ds(16 * i, 16)], act.at[pl.ds(16 * i, 16)], in_sem.at[2 + i]) for i in range(4)]
    loads.append(pltpu.make_async_copy(w_hbm, w_ref, in_sem.at[6]))
    loads.append(pltpu.make_async_copy(cot_hbm, cot, in_sem.at[7]))
    for cp in loads:
        cp.start()
    loads[1].wait()
    rmat[:, :512] = kron8(rowtab[0], False)
    rmat[:, 512:] = kron8(rowtab[1], False)
    loads[0].wait()
    for i in range(4):
        loads[2 + i].wait()
        columns(act[16 * i : 16 * i + 16], tab[...], xs, 16 * i, 16)
    row_modes(xs, rmat, t1, 1 - core)
    wait_peers()
    start_core(t1, b0, send1, recv1)
    row_modes(xs, rmat, t1, core)

    def prepare(i):
        if i == 0:
            imat_ref[:, :512] = kron8(rowtab[0], True)
            imat_ref[:, 512:] = kron8(rowtab[1], True)
            lw_t[...] = lw_ref[...].astype(F32).T.astype(BF)
        if i == 1:
            lane = lanes_of((512, 256)) % 128
            scaled = tab[...].astype(F32) * jnp.where(lane < 2, 2.0**-22, 2.0**-21)
            dtab[...] = scaled.astype(BF)
            syn[...] = scaled[:, :128].T.astype(BF)

    own = reduce_scatter(t1, (b0, a1, b1, a2, b2), send1, recv1, prepare)
    loads[6].wait()
    s = to_columns(own.astype(BF).astype(F32))
    mixed = []
    for jj in range(2):
        s_ref[jj] = s[jj]
        mixed.append(weigh(s[jj], w_ref, jj))
    for g, v in enumerate(to_block(mixed)):
        g1[core, p, q, x, g] = v.astype(BF)
    all_gather(g1, send2, recv2)

    inverse(g1, imat_ref, rf)
    loads[7].wait()
    bias = bias_ref[...]

    def rows(i, _):
        for n in range(2):
            ds = []
            for k in range(2):
                h = 4 * i + 2 * n + k
                lhs = jnp.concatenate([rf[h], lw_t[...]], axis=1)
                rhs = jnp.concatenate([syn[...], act[h]], axis=0)
                d = (cot[h].astype(F32) * gelu_grad(dot(lhs, rhs) + bias)).astype(BF)
                dpre[h] = d
                ds.append(d)
            columns(jnp.concatenate(ds, axis=0).reshape(2, 64, 512), dtab[...], xs, pl.multiple_of(4 * i + 2 * n, 2), 2)
        return 0

    stores = []
    for i in range(4):
        lax.fori_loop(4 * i, 4 * i + 4, rows, 0)
        cp = pltpu.make_async_copy(dpre.at[pl.ds(16 * i, 16)], dpre_hbm.at[pl.ds(16 * i, 16)], out_sem.at[i])
        cp.start()
        stores.append(cp)

    row_modes(xs, rmat, t2, 1 - core)
    start_core(t2, c0, send3, recv3)
    row_modes(xs, rmat, t2, core)

    steps = ((p, lambda v: device(v, q, x, core)), (q, lambda v: device(p, v, x, core)), (x, lambda v: device(p, q, v, core)))

    def swap_lin():
        part[0, core] = lin[...]
        remote(part.at[0, core], part.at[0, core], send5.at[0], recv5.at[0], sibling(p, q, x, core)).start()

    def join_lin(i):
        if i == 0:
            cp = remote(part.at[0, core], part.at[0, core], send5.at[0], recv5.at[0], sibling(p, q, x, core))
            cp.wait_send()
            remote(part.at[0, 1 - core], part.at[0, 1 - core], send5.at[0], recv5.at[0], sibling(p, q, x, core)).wait_recv()
            return part[0, 0] + part[0, 1]
        me, at = steps[i - 1]
        for d in range(1, 4):
            src = (me + 4 - d) % 4
            remote(part.at[i, src], part.at[i, src], send5.at[3 * i - 3 + d], recv5.at[3 * i - 3 + d], at(src)).wait_recv()
            remote(part.at[i, me], part.at[i, me], send5.at[3 * i - 3 + d], recv5.at[3 * i - 3 + d], at((me + d) % 4)).wait_send()
        return part[i, 0] + part[i, 1] + part[i, 2] + part[i, 3]

    def pass_lin(i):
        me, at = steps[i]
        part[i + 1, me] = join_lin(i)
        for d in range(1, 4):
            remote(part.at[i + 1, me], part.at[i + 1, me], send5.at[3 * i + d], recv5.at[3 * i + d], at((me + d) % 4)).start()

    def products(i, _):
        left = jnp.concatenate([act[4 * i + k] for k in range(4)], axis=1)
        right = jnp.concatenate([dpre[4 * i + k] for k in range(4)], axis=1)
        left = jnp.concatenate([left, jnp.ones((16, 2048), BF)], axis=0)
        lin[...] += lax.dot_general(left, right, (((1,), (1,)), ((), ())), preferred_element_type=F32)
        return 0

    def local_products(i):
        if i == 0:
            lin[...] = jnp.zeros_like(lin)
            lax.fori_loop(0, 16, products, 0)
            swap_lin()
        if i >= 2:
            pass_lin(i - 2)

    own = reduce_scatter(t2, (c0, e1, c1, e2, c2), send3, recv3, local_products)
    d = to_columns(own.astype(BF).astype(F32))
    back = []
    for jj in range(2):
        d_ref[jj] = d[jj]
        back.append(weigh_back(d[jj], w_ref, jj))
    for g, v in enumerate(to_block(back)):
        g2_ref[core, p, q, x, g] = v.astype(BF)
    all_gather(g2_ref, send4, recv4, local_products)
    lin_out_ref[...] = join_lin(3) * (1.0 / 2048)
    for cp in stores:
        cp.wait()


def last_kernel(g_ref, dpre_ref, imat_ref, coltab_hbm, lw_ref, s_ref, d_ref, gin_ref, gspec_ref, rf_ref, tab, ana, sem):
    load = pltpu.make_async_copy(coltab_hbm.at[lax.axis_index("modes")], tab, sem)
    load.start()
    inverse(g_ref, imat_ref, rf_ref)
    load.wait()
    ana[...] = tab[:, :128].astype(F32).T.astype(BF)

    def row(h, _):
        for k in range(4):
            lhs = jnp.concatenate([rf_ref[4 * h + k], lw_ref[...]], axis=1)
            rhs = jnp.concatenate([ana[...], dpre_ref[4 * h + k]], axis=0)
            gin_ref[4 * h + k] = dot(lhs, rhs).astype(BF)
        return 0

    lax.fori_loop(0, 16, row, 0)
    for jj in range(2):
        re, im = duplicate(s_ref[jj])
        d = d_ref[jj]
        even = lax.broadcasted_iota(jnp.int32, (32, 64), 0) % 2 == 0
        dsw = jnp.where(even, pltpu.roll(d, 31, 0), -pltpu.roll(d, 1, 0))
        for c in range(64):
            gspec_ref[jj, c] = re[:, c : c + 1] * d + im[:, c : c + 1] * dsw


SPEC = (2, 4, 4, 4, 2, 16, 128)
ANY = pl.BlockSpec(memory_space=pl.ANY)


def body(activations, cotangent, spectral_weight, linear_weight, bias):
    w = spectral_weight.transpose(0, 1, 3, 2)
    coltab, rowtab = jnp.asarray(column_constants()), jnp.asarray(row_constants())
    dma = pltpu.SemaphoreType.DMA
    quarter = (4, 4, 4, 2, 16, 128)
    buffers = [pltpu.VMEM(quarter, BF), pltpu.VMEM(quarter, BF), pltpu.VMEM((3, 4, 4, 2, 16, 128), BF),
               pltpu.VMEM((4, 4, 2, 16, 128), BF), pltpu.VMEM((15, 2, 16, 128), BF)]
    shape = jax.ShapeDtypeStruct
    dpre, s, d, g, lin, imat = pl.pallas_call(
        main_kernel,
        out_shape=[shape((64, 64, 512), BF), shape((2, 32, 64), F32), shape((2, 32, 64), F32), shape(SPEC, BF),
                   shape((80, 64), F32), shape((512, 1024), BF)],
        in_specs=[ANY] * 5 + [VMEM] * 2,
        out_specs=[ANY] + [VMEM] * 5,
        scratch_shapes=[
            pltpu.VMEM((64, 64, 512), BF), pltpu.VMEM((64, 64, 512), BF), pltpu.VMEM((2, 64, 32, 64), BF),
            pltpu.VMEM((512, 256), BF), pltpu.VMEM((512, 256), BF), pltpu.VMEM((128, 512), BF), pltpu.VMEM((2, 64, 64), BF),
            pltpu.VMEM((512, 1024), BF), pltpu.VMEM((64, 64), BF), pltpu.VMEM((2, 1024, 512), BF),
            pltpu.VMEM((64, 64, 128), BF), pltpu.VMEM((64, 64, 512), BF), pltpu.VMEM((80, 64), F32),
            pltpu.VMEM(SPEC, BF), pltpu.VMEM(SPEC, BF), pltpu.VMEM(SPEC, BF), pltpu.VMEM((4, 4, 80, 64), F32),
        ] + buffers + buffers + [dma((8,)), dma((4,))] + [dma((22,))] * 8 + [dma((10,))] * 2,
        compiler_params=pltpu.CompilerParams(vmem_limit_bytes=LIMIT, collective_id=0, has_side_effects=True),
        name="main",
    )(activations, cotangent, w, coltab, rowtab, linear_weight, bias[:, None])
    gin, gspec = pl.pallas_call(
        last_kernel,
        out_shape=[shape((64, 64, 512), BF), shape((2, 64, 32, 64), F32)],
        in_specs=[VMEM] * 3 + [ANY] + [VMEM] * 3,
        out_specs=[VMEM] * 2,
        scratch_shapes=[pltpu.VMEM((64, 64, 128), BF), pltpu.VMEM((512, 256), BF), pltpu.VMEM((128, 512), BF), dma],
        compiler_params=pltpu.CompilerParams(vmem_limit_bytes=LIMIT),
        name="last",
    )(g, dpre, imat, coltab, linear_weight, s, d)
    return gin, gspec.transpose(0, 1, 3, 2), lin[:64], lin[64]


def solution(mesh):
    return jax.shard_map(
        body,
        mesh=mesh,
        in_specs=(
            P("rows", None, "modes"),
            P("rows", None, "modes"),
            P("rows", None, None, "modes"),
            P(),
            P(),
        ),
        out_specs=(P("rows", None, "modes"), P("rows", None, None, "modes"), P(), P()),
        check_vma=False,
    )
```

```python
import math

import jax
import jax.numpy as jnp
import numpy as np
from jax import lax
from jax.experimental import pallas as pl
from jax.experimental.pallas import tpu as pltpu
from jax.sharding import PartitionSpec as P

MESH = pl.DeviceIdType.MESH
BF = jnp.bfloat16
F32 = jnp.float32
VMEM = pl.BlockSpec(memory_space=pltpu.VMEM)
LIMIT = 60 * 1024 * 1024


def dot(a, b):
    return jnp.dot(a, b, preferred_element_type=F32)


def lanes_of(shape):
    return lax.broadcasted_iota(jnp.int32, shape, len(shape) - 1)


def column_constants():
    k = np.arange(128) // 2
    w = np.arange(2048)
    ang = ((w[:, None] * k[None, :]) % 2048) * (2.0 * math.pi / 2048)
    even = (np.arange(128) % 2 == 0)[None, :]
    ana = np.where(even, np.cos(ang), -np.sin(ang))
    swap = np.where(even, -np.sin(ang), -np.cos(ang))
    return np.concatenate([ana, swap], axis=1).reshape(4, 512, 256).astype(np.float32).astype(jnp.bfloat16)


def row_constants():
    slot = np.arange(64)
    core, z, x, jj = slot // 32, (slot // 8) % 4, (slot // 2) % 4, slot % 2
    mode = x * 16 + z * 4 + core * 2 + jj
    freq = np.where(mode < 32, mode, mode - 64)
    rows = np.arange(2048).reshape(32, 64)
    ang = ((freq[None, :, None] * rows[:, None, :]) % 2048) * (2.0 * math.pi / 2048)
    return np.stack([np.cos(ang), np.sin(ang)], axis=1).astype(np.float32).astype(jnp.bfloat16)


def kron8(table, flip):
    up = (lax.broadcasted_iota(jnp.int32, (512, 64), 0) // 8 == lax.broadcasted_iota(jnp.int32, (512, 64), 1)).astype(BF)
    wide = (lax.broadcasted_iota(jnp.int32, (64, 512), 1) // 8 == lax.broadcasted_iota(jnp.int32, (64, 512), 0)).astype(BF)
    keep = lax.broadcasted_iota(jnp.int32, (512, 512), 0) % 8 == lax.broadcasted_iota(jnp.int32, (512, 512), 1) % 8
    left = lax.dot_general(up, table, (((1,), (1 if flip else 0,)), ((), ())), preferred_element_type=F32).astype(BF)
    return jnp.where(keep, dot(left, wide), 0.0).astype(BF)


def place():
    r, y = lax.axis_index("rows"), lax.axis_index("modes")
    x, z, core = r // 8, (r // 2) % 4, r % 2
    return y * (1 - core) + z * core, z * (1 - core) + y * core, x, core


def device(p, q, x, core):
    y, z = p * (1 - core) + q * core, q * (1 - core) + p * core
    return ((x * 4 + z) * 2 + core, y)


def sibling(p, q, x, core):
    return device(q, p, x, 1 - core)


def signal_peers():
    p, q, x, core = place()
    barrier = pltpu.get_barrier_semaphore()
    pl.semaphore_signal(barrier, inc=1, device_id=sibling(p, q, x, core), device_id_type=MESH)
    for d in range(1, 4):
        pl.semaphore_signal(barrier, inc=1, device_id=device((p + d) % 4, q, x, core), device_id_type=MESH)
    for k in range(1, 16):
        pl.semaphore_signal(barrier, inc=1, device_id=device(p, (q + k // 4) % 4, (x + k % 4) % 4, core), device_id_type=MESH)


def wait_peers():
    pl.semaphore_wait(pltpu.get_barrier_semaphore(), 19)


def remote(src, dst, send, recv, target):
    return pltpu.make_async_remote_copy(src_ref=src, dst_ref=dst, send_sem=send, recv_sem=recv, device_id=target, device_id_type=MESH)


def columns(block, tab, xs_ref, h0, count):
    prod = dot(block.reshape(count * 64, 512), tab).reshape(count, 8, 8, 256)
    for a in range(4):
        for g in range(2):
            v = prod[:, 2 * a + g].reshape(count * 8, 256).astype(BF)
            xs_ref[g, pl.ds(h0 * 8, count * 8), 128 * a : 128 * a + 128] = v[:, :128]
            xs_ref[g, pl.ds(512 + h0 * 8, count * 8), 128 * a : 128 * a + 128] = v[:, 128:]


def row_modes(xs_ref, rmat_ref, t_ref, owner):
    block = lanes_of((256, 128)) // 32
    for g in range(2):
        o = dot(rmat_ref[pl.ds(pl.multiple_of(owner * 256, 256), 256), :], xs_ref[g])
        for m in range(4):
            total = None
            for a in range(4):
                v = o[:, 128 * a : 128 * a + 128]
                shift = (32 * (a - m)) % 128
                if shift:
                    v = pltpu.roll(v, shift, 1)
                total = v if total is None else jnp.where(block == a, v, total)
            total = total.astype(BF).reshape(4, 4, 16, 128)
            for z in range(4):
                t_ref[owner, m * (1 - owner) + z * owner, z * (1 - owner) + m * owner, :, g] = total[z]


def inverse(g_ref, imat_ref, out_ref):
    even = lanes_of((512, 128)) % 2 == 0
    block = lanes_of((512, 128)) // 32
    for b in range(4):
        cols = []
        for g in range(2):
            total = None
            for m in range(4):
                parts = [g_ref[0, m, :, :, g].reshape(256, 128)]
                parts += [g_ref[1, z, m, :, g].reshape(64, 128) for z in range(4)]
                v = jnp.concatenate(parts, axis=0).astype(F32)
                shift = (32 * (m - b)) % 128
                if shift:
                    v = pltpu.roll(v, shift, 1)
                total = v if total is None else jnp.where(block == m, v, total)
            swapped = jnp.where(even, -pltpu.roll(total, 127, 1), pltpu.roll(total, 1, 1))
            cols.append(jnp.concatenate([total.astype(BF), swapped.astype(BF)], axis=0))
        o = dot(imat_ref[...], jnp.concatenate(cols, axis=1))
        both = jnp.concatenate([o[:, :128].reshape(64, 8, 128), o[:, 128:].reshape(64, 8, 128)], axis=1)
        out_ref[:, 16 * b : 16 * b + 16, :] = both.astype(BF)


def gelu_grad(z):
    u = (0.3275911 * 0.7071067811865476) * jnp.abs(z)
    e = jnp.exp2((-0.5 * 1.4426950408889634) * z * z)
    t = 1.0 / (1.0 + u)
    poly = t * (0.5 * 0.254829592 + t * (-0.5 * 0.284496736 + t * (0.5 * 1.421413741 + t * (-0.5 * 1.453152027 + t * (0.5 * 1.061405429)))))
    r = (poly - (0.3989422804014327 / (0.3275911 * 0.7071067811865476)) * u) * e
    return jnp.where(z >= 0, 1.0 - r, r)


def duplicate(v):
    even = lax.broadcasted_iota(jnp.int32, v.shape, 0) % 2 == 0
    return jnp.where(even, v, pltpu.roll(v, 1, 0)), jnp.where(even, pltpu.roll(v, v.shape[0] - 1, 0), v)


def to_columns(block):
    turned = [[block[g] if a == 0 else pltpu.roll(block[g], 128 - 32 * a, 1) for g in range(2)] for a in range(4)]
    out = []
    for jj in range(2):
        rows = [turned[a][g][8 * jj : 8 * jj + 8] for a in range(4) for g in range(2)]
        out.append(jnp.concatenate(rows + rows, axis=0).T[:32, :64])
    return out


def to_block(cols):
    block = lanes_of((8, 128)) // 32
    parts = []
    for v in cols:
        square = jnp.concatenate([jnp.concatenate([v, v], axis=1)] * 4, axis=0).T
        parts.append([])
        for g in range(2):
            out = square[8 * g : 8 * g + 8]
            for a in range(1, 4):
                out = jnp.where(block == a, square[16 * a + 8 * g : 16 * a + 8 * g + 8], out)
            parts[-1].append(out)
    return [jnp.concatenate([parts[0][g], parts[1][g]], axis=0) for g in range(2)]


def weigh(s, w_ref, jj):
    re, im = duplicate(s)
    t1 = jnp.zeros((32, 64), F32)
    t2 = jnp.zeros((32, 64), F32)
    for c in range(64):
        w = w_ref[jj, c].astype(F32)
        t1 += re[:, c : c + 1] * w
        t2 += im[:, c : c + 1] * w
    even = lax.broadcasted_iota(jnp.int32, (32, 64), 0) % 2 == 0
    return t1 + jnp.where(even, -pltpu.roll(t2, 31, 0), pltpu.roll(t2, 1, 0))


def weigh_back(d, w_ref, jj):
    even = lax.broadcasted_iota(jnp.int32, (32, 64), 0) % 2 == 0
    dsw = jnp.where(even, pltpu.roll(d, 31, 0), pltpu.roll(d, 1, 0))
    lane = lanes_of((32, 64))
    u1 = jnp.zeros((32, 64), F32)
    u2 = jnp.zeros((32, 64), F32)
    for c in range(64):
        w = w_ref[jj, c].astype(F32)
        u1 = jnp.where(lane == c, jnp.sum(w * d, axis=1, keepdims=True), u1)
        u2 = jnp.where(lane == c, jnp.sum(w * dsw, axis=1, keepdims=True), u2)
    return jnp.where(even, u1 + pltpu.roll(u1, 31, 0), pltpu.roll(u2, 1, 0) - u2)


def start_core(t_ref, b0, send, recv):
    p, q, x, core = place()
    for d in (1, 2, 3, 0):
        row = (p + d) % 4
        remote(t_ref.at[1 - core, :, row], b0.at[:, row], send.at[d], recv.at[d], sibling(p, q, x, core)).start()


def reduce_scatter(t_ref, bufs, send, recv, between=lambda i: None):
    b0, a1, b1, a2, b2 = bufs
    p, q, x, core = place()
    pending = []
    for d in (1, 2, 3, 0):
        row = (q + d) % 4
        remote(b0.at[:, row], b0.at[:, row], send.at[d], recv.at[d], sibling(p, q, x, core)).wait_recv()
        for e in (1, 2, 3, 0):
            pt = (p + e) % 4
            a1[pt, row] = (t_ref[core, pt, row].astype(F32) + b0[pt, row].astype(F32)).astype(BF)
            if e:
                k = 3 + 3 * d + e
                cp = remote(a1.at[pt, row], b1.at[e - 1, row], send.at[k], recv.at[k], device(pt, q, x, core))
                cp.start()
                pending.append(cp)
    between(0)
    stage = []
    for i, d in enumerate((1, 2, 3, 0)):
        row = (q + d) % 4
        for cp in pending[3 * i : 3 * i + 3]:
            cp.wait_recv()
        a2[row] = (a1[p, row].astype(F32) + b1[0, row].astype(F32) + b1[1, row].astype(F32) + b1[2, row].astype(F32)).astype(BF)
        for n in range(4):
            k = 4 * d + n
            if k:
                xt = (x + n) % 4
                cp = remote(a2.at[row, xt], b2.at[k - 1], send.at[15 + k], recv.at[15 + k], device(p, row, xt, core))
                cp.start()
                stage.append(cp)
    own = a1[p, q, x].astype(F32)
    for k in range(3):
        own += b1[k, q, x].astype(F32)
    between(1)
    for cp in stage:
        cp.wait_recv()
    for k in range(15):
        own += b2[k].astype(F32)
    for d in range(4):
        row = (p + d) % 4
        remote(t_ref.at[1 - core, :, row], b0.at[:, row], send.at[d], recv.at[d], sibling(p, q, x, core)).wait_send()
    for cp in pending + stage:
        cp.wait_send()
    return own


def all_gather(g_ref, send, recv, between=lambda i: None):
    p, q, x, core = place()
    pending = []
    mine = g_ref.at[core, p, q, x]
    for d in (0, 2, 1, 3):
        for n in range(4):
            k = 4 * d + n
            if k:
                cp = remote(mine, mine, send.at[15 + k], recv.at[15 + k], device(p, (q + d) % 4, (x + n) % 4, core))
                cp.start()
                pending.append(cp)
    between(2)
    order = (0, 1, 3, 2)
    for d in order:
        row = (q + 4 - d) % 4
        for n in range(4):
            k = 4 * d + n
            if k:
                xs = (x + 4 - n) % 4
                theirs = g_ref.at[core, p, row, xs]
                remote(theirs, theirs, send.at[15 + k], recv.at[15 + k], device(p, row, xs, core)).wait_recv()
        mine = g_ref.at[core, p, row]
        for e in (1, 2, 3):
            k = 3 + 3 * d + e
            cp = remote(mine, mine, send.at[k], recv.at[k], device((p + e) % 4, q, x, core))
            cp.start()
            pending.append(cp)
    between(3)
    for d in order:
        row = (q + 4 - d) % 4
        for e in (1, 2, 3):
            k = 3 + 3 * d + e
            ps = (p + 4 - e) % 4
            theirs = g_ref.at[core, ps, row]
            remote(theirs, theirs, send.at[k], recv.at[k], device(ps, q, x, core)).wait_recv()
        theirs = g_ref.at[core, :, row]
        cp = remote(theirs, theirs, send.at[d], recv.at[d], sibling(p, q, x, core))
        cp.start()
        pending.append(cp)
    between(4)
    for d in order:
        theirs = g_ref.at[1 - core, :, (p + 4 - d) % 4]
        remote(theirs, theirs, send.at[d], recv.at[d], sibling(p, q, x, core)).wait_recv()
    for cp in pending:
        cp.wait_send()


def main_kernel(act_hbm, cot_hbm, w_hbm, coltab_hbm, rowtab_hbm, lw_ref, bias_ref,
                dpre_hbm, s_ref, d_ref, rf2_ref, lin_out_ref,
                act, cot, w_ref, tab, dtab, syn, rowtab, rmat, imat_ref, lw_t, bias_col, xs, rf, dpre, lin, t1, t2, g1, g2_ref, part,
                b0, a1, b1, a2, b2, c0, e1, c1, e2, c2,
                in_sem, out_sem, send1, recv1, send2, recv2, send3, recv3, send4, recv4, send5, recv5):
    p, q, x, core = place()
    signal_peers()
    row_dev, mode_dev = lax.axis_index("rows"), lax.axis_index("modes")
    loads = [
        pltpu.make_async_copy(coltab_hbm.at[mode_dev], tab, in_sem.at[0]),
        pltpu.make_async_copy(rowtab_hbm.at[row_dev], rowtab, in_sem.at[1]),
    ]
    loads += [pltpu.make_async_copy(act_hbm.at[pl.ds(16 * i, 16)], act.at[pl.ds(16 * i, 16)], in_sem.at[2 + i]) for i in range(4)]
    loads.append(pltpu.make_async_copy(w_hbm, w_ref, in_sem.at[6]))
    loads.append(pltpu.make_async_copy(cot_hbm, cot, in_sem.at[7]))
    for cp in loads:
        cp.start()
    loads[1].wait()
    rmat[:, :512] = kron8(rowtab[0], False)
    rmat[:, 512:] = kron8(rowtab[1], False)
    loads[0].wait()

    def analyse(i, _):
        rows = pl.ds(16 * i, 16)
        pltpu.make_async_copy(act_hbm.at[rows], act.at[rows], in_sem.at[2 + i]).wait()
        columns(act[rows], tab[...], xs, pl.multiple_of(16 * i, 16), 16)
        return 0

    lax.fori_loop(0, 4, analyse, 0)
    row_modes(xs, rmat, t1, 1 - core)
    wait_peers()
    start_core(t1, b0, send1, recv1)
    row_modes(xs, rmat, t1, core)

    def prepare(i):
        if i == 0:
            imat_ref[:, :512] = kron8(rowtab[0], True)
            imat_ref[:, 512:] = kron8(rowtab[1], True)
            lw_t[...] = lw_ref[...].astype(F32).T.astype(BF)
            bias_col[...] = jnp.broadcast_to(bias_ref[...], (128, 64)).T
        if i == 1:
            lane = lanes_of((512, 256)) % 128
            scaled = tab[...].astype(F32) * jnp.where(lane < 2, 2.0**-22, 2.0**-21)
            dtab[...] = scaled.astype(BF)
            syn[...] = scaled[:, :128].T.astype(BF)

    own = reduce_scatter(t1, (b0, a1, b1, a2, b2), send1, recv1, prepare)
    loads[6].wait()
    s = to_columns(own.astype(BF).astype(F32))
    mixed = []
    for jj in range(2):
        s_ref[jj] = s[jj]
        mixed.append(weigh(s[jj], w_ref, jj))
    for g, v in enumerate(to_block(mixed)):
        g1[core, p, q, x, g] = v.astype(BF)
    all_gather(g1, send2, recv2)

    inverse(g1, imat_ref, rf)
    loads[7].wait()

    def rows(i, _):
        bias = jnp.concatenate([bias_col[...]] * 4, axis=1)
        for n in range(2):
            first = pl.multiple_of(16 * i + 8 * n, 8)
            ds = []
            for k in range(8):
                h = first + k
                lhs = jnp.concatenate([rf[h], lw_t[...]], axis=1)
                rhs = jnp.concatenate([syn[...], act[h]], axis=0)
                d = (cot[h].astype(F32) * gelu_grad(dot(lhs, rhs) + bias)).astype(BF)
                dpre[h] = d
                ds.append(d)
            columns(jnp.concatenate(ds, axis=0).reshape(8, 64, 512), dtab[...], xs, first, 8)
        some = pl.ds(16 * i, 16)
        pltpu.make_async_copy(dpre.at[some], dpre_hbm.at[some], out_sem.at[i]).start()
        return 0

    lax.fori_loop(0, 4, rows, 0)
    row_modes(xs, rmat, t2, 1 - core)
    start_core(t2, c0, send3, recv3)
    row_modes(xs, rmat, t2, core)

    steps = ((p, lambda v: device(v, q, x, core)), (q, lambda v: device(p, v, x, core)), (x, lambda v: device(p, q, v, core)))

    def swap_lin():
        part[0, core] = lin[...]
        remote(part.at[0, core], part.at[0, core], send5.at[0], recv5.at[0], sibling(p, q, x, core)).start()

    def join_lin(i):
        if i == 0:
            cp = remote(part.at[0, core], part.at[0, core], send5.at[0], recv5.at[0], sibling(p, q, x, core))
            cp.wait_send()
            remote(part.at[0, 1 - core], part.at[0, 1 - core], send5.at[0], recv5.at[0], sibling(p, q, x, core)).wait_recv()
            return part[0, 0] + part[0, 1]
        me, at = steps[i - 1]
        for d in range(1, 4):
            src = (me + 4 - d) % 4
            remote(part.at[i, src], part.at[i, src], send5.at[3 * i - 3 + d], recv5.at[3 * i - 3 + d], at(src)).wait_recv()
            remote(part.at[i, me], part.at[i, me], send5.at[3 * i - 3 + d], recv5.at[3 * i - 3 + d], at((me + d) % 4)).wait_send()
        return part[i, 0] + part[i, 1] + part[i, 2] + part[i, 3]

    def pass_lin(i):
        me, at = steps[i]
        part[i + 1, me] = join_lin(i)
        for d in range(1, 4):
            remote(part.at[i + 1, me], part.at[i + 1, me], send5.at[3 * i + d], recv5.at[3 * i + d], at((me + d) % 4)).start()

    def products(i, _):
        left = jnp.concatenate([act[4 * i + k] for k in range(4)], axis=1)
        right = jnp.concatenate([dpre[4 * i + k] for k in range(4)], axis=1)
        left = jnp.concatenate([left, jnp.ones((16, 2048), BF)], axis=0)
        lin[...] += lax.dot_general(left, right, (((1,), (1,)), ((), ())), preferred_element_type=F32)
        return 0

    def local_products(i):
        if i == 0:
            lin[...] = jnp.zeros_like(lin)
            lax.fori_loop(0, 16, products, 0)
            swap_lin()
        if i >= 2:
            pass_lin(i - 2)

    own = reduce_scatter(t2, (c0, e1, c1, e2, c2), send3, recv3, local_products)
    d = to_columns(own.astype(BF).astype(F32))
    back = []
    for jj in range(2):
        d_ref[jj] = d[jj]
        back.append(weigh_back(d[jj], w_ref, jj))
    for g, v in enumerate(to_block(back)):
        g2_ref[core, p, q, x, g] = v.astype(BF)
    all_gather(g2_ref, send4, recv4, local_products)
    lin_out_ref[...] = join_lin(3) * (1.0 / 2048)
    inverse(g2_ref, imat_ref, rf2_ref)
    for i in range(4):
        some = pl.ds(16 * i, 16)
        pltpu.make_async_copy(dpre.at[some], dpre_hbm.at[some], out_sem.at[i]).wait()


def last_kernel(rf_hbm, dpre_hbm, coltab_hbm, lw_ref, s_ref, d_ref, lin_ref,
                gin_hbm, gspec_hbm, glin_ref, gbias_ref, rf, dpre, tab, ana, gin, gspec, in_sem, out_sem):
    load = pltpu.make_async_copy(coltab_hbm.at[lax.axis_index("modes")], tab, in_sem.at[8])
    load.start()

    def copy(n, i):
        some = pl.ds(16 * i, 16)
        if n == 2:
            return pltpu.make_async_copy(gin.at[some], gin_hbm.at[some], out_sem.at[i])
        src, dst = ((rf_hbm, rf), (dpre_hbm, dpre))[n]
        return pltpu.make_async_copy(src.at[some], dst.at[some], in_sem.at[2 * i + n])

    for i in range(4):
        copy(0, i).start()
        copy(1, i).start()
    glin_ref[...] = lin_ref[:64]
    gbias_ref[...] = lin_ref[64:65]
    even = lax.broadcasted_iota(jnp.int32, (32, 64), 0) % 2 == 0
    for jj in range(2):
        re, im = duplicate(s_ref[jj])
        d = d_ref[jj]
        dsw = jnp.where(even, pltpu.roll(d, 31, 0), -pltpu.roll(d, 1, 0))
        for c in range(64):
            gspec[jj, c] = re[:, c : c + 1] * d + im[:, c : c + 1] * dsw
        pltpu.make_async_copy(gspec.at[jj], gspec_hbm.at[jj], out_sem.at[4 + jj]).start()
    load.wait()
    ana[...] = tab[:, :128].astype(F32).T.astype(BF)

    def row(i, _):
        copy(0, i).wait()
        copy(1, i).wait()
        for k in range(16):
            lhs = jnp.concatenate([rf[16 * i + k], lw_ref[...]], axis=1)
            rhs = jnp.concatenate([ana[...], dpre[16 * i + k]], axis=0)
            gin[16 * i + k] = dot(lhs, rhs).astype(BF)
        copy(2, i).start()
        return 0

    lax.fori_loop(0, 4, row, 0)
    for jj in range(2):
        pltpu.make_async_copy(gspec.at[jj], gspec_hbm.at[jj], out_sem.at[4 + jj]).wait()
    for i in range(4):
        copy(2, i).wait()


SPEC = (2, 4, 4, 4, 2, 16, 128)
ANY = pl.BlockSpec(memory_space=pl.ANY)


def body(activations, cotangent, spectral_weight, linear_weight, bias):
    w = spectral_weight.transpose(0, 1, 3, 2)
    coltab, rowtab = jnp.asarray(column_constants()), jnp.asarray(row_constants())
    dma = pltpu.SemaphoreType.DMA
    quarter = (4, 4, 4, 2, 16, 128)
    buffers = [pltpu.VMEM(quarter, BF), pltpu.VMEM(quarter, BF), pltpu.VMEM((3, 4, 4, 2, 16, 128), BF),
               pltpu.VMEM((4, 4, 2, 16, 128), BF), pltpu.VMEM((15, 2, 16, 128), BF)]
    shape = jax.ShapeDtypeStruct
    dpre, s, d, rf, lin = pl.pallas_call(
        main_kernel,
        out_shape=[shape((64, 64, 512), BF), shape((2, 32, 64), F32), shape((2, 32, 64), F32), shape((64, 64, 128), BF),
                   shape((80, 64), F32)],
        in_specs=[ANY] * 5 + [VMEM] * 2,
        out_specs=[ANY] + [VMEM] * 4,
        scratch_shapes=[
            pltpu.VMEM((64, 64, 512), BF), pltpu.VMEM((64, 64, 512), BF), pltpu.VMEM((2, 64, 32, 64), BF),
            pltpu.VMEM((512, 256), BF), pltpu.VMEM((512, 256), BF), pltpu.VMEM((128, 512), BF), pltpu.VMEM((2, 64, 64), BF),
            pltpu.VMEM((512, 1024), BF), pltpu.VMEM((512, 1024), BF), pltpu.VMEM((64, 64), BF), pltpu.VMEM((64, 128), F32),
            pltpu.VMEM((2, 1024, 512), BF),
            pltpu.VMEM((64, 64, 128), BF), pltpu.VMEM((64, 64, 512), BF), pltpu.VMEM((80, 64), F32),
            pltpu.VMEM(SPEC, BF), pltpu.VMEM(SPEC, BF), pltpu.VMEM(SPEC, BF), pltpu.VMEM(SPEC, BF), pltpu.VMEM((4, 4, 80, 64), F32),
        ] + buffers + buffers + [dma((8,)), dma((4,))] + [dma((31,))] * 8 + [dma((10,))] * 2,
        compiler_params=pltpu.CompilerParams(vmem_limit_bytes=LIMIT, collective_id=0, has_side_effects=True),
        name="main",
    )(activations, cotangent, w, coltab, rowtab, linear_weight, bias.reshape(1, 64))
    gin, gspec, glin, gbias = pl.pallas_call(
        last_kernel,
        out_shape=[shape((64, 64, 512), BF), shape((2, 64, 32, 64), F32), shape((64, 64), F32), shape((1, 64), F32)],
        in_specs=[ANY] * 3 + [VMEM] * 4,
        out_specs=[ANY] * 2 + [VMEM] * 2,
        scratch_shapes=[pltpu.VMEM((64, 64, 128), BF), pltpu.VMEM((64, 64, 512), BF), pltpu.VMEM((512, 256), BF),
                        pltpu.VMEM((128, 512), BF), pltpu.VMEM((64, 64, 512), BF), pltpu.VMEM((2, 64, 32, 64), F32),
                        dma((9,)), dma((6,))],
        compiler_params=pltpu.CompilerParams(vmem_limit_bytes=LIMIT),
        name="last",
    )(rf, dpre, coltab, linear_weight, s, d, lin)
    return gin, gspec.transpose(0, 1, 3, 2), glin, gbias.reshape(64)


def solution(mesh):
    return jax.shard_map(
        body,
        mesh=mesh,
        in_specs=(
            P("rows", None, "modes"),
            P("rows", None, "modes"),
            P("rows", None, None, "modes"),
            P(),
            P(),
        ),
        out_specs=(P("rows", None, "modes"), P("rows", None, None, "modes"), P(), P()),
        check_vma=False,
    )
```

```python
import math

import jax
import jax.numpy as jnp
import numpy as np
from jax import lax
from jax.experimental import pallas as pl
from jax.experimental.pallas import tpu as pltpu
from jax.sharding import PartitionSpec as P

MESH = pl.DeviceIdType.MESH
BF = jnp.bfloat16
F32 = jnp.float32
VMEM = pl.BlockSpec(memory_space=pltpu.VMEM)
LIMIT = 60 * 1024 * 1024


def dot(a, b):
    return jnp.dot(a, b, preferred_element_type=F32)


def lanes_of(shape):
    return lax.broadcasted_iota(jnp.int32, shape, len(shape) - 1)


def column_constants():
    k = np.arange(128) // 2
    w = np.arange(2048)
    ang = ((w[:, None] * k[None, :]) % 2048) * (2.0 * math.pi / 2048)
    even = (np.arange(128) % 2 == 0)[None, :]
    ana = np.where(even, np.cos(ang), -np.sin(ang))
    swap = np.where(even, -np.sin(ang), -np.cos(ang))
    return np.concatenate([ana, swap], axis=1).reshape(4, 512, 256).astype(np.float32).astype(jnp.bfloat16)


def row_constants():
    slot = np.arange(64)
    core, z, x, jj = slot // 32, (slot // 8) % 4, (slot // 2) % 4, slot % 2
    mode = x * 16 + z * 4 + core * 2 + jj
    freq = np.where(mode < 32, mode, mode - 64)
    rows = np.arange(2048).reshape(32, 64)
    ang = ((freq[None, :, None] * rows[:, None, :]) % 2048) * (2.0 * math.pi / 2048)
    return np.stack([np.cos(ang), np.sin(ang)], axis=1).astype(np.float32).astype(jnp.bfloat16)


def kron8(table, flip):
    up = (lax.broadcasted_iota(jnp.int32, (512, 64), 0) >> 3 == lax.broadcasted_iota(jnp.int32, (512, 64), 1)).astype(BF)
    wide = (lax.broadcasted_iota(jnp.int32, (64, 512), 1) >> 3 == lax.broadcasted_iota(jnp.int32, (64, 512), 0)).astype(BF)
    keep = (lax.broadcasted_iota(jnp.int32, (512, 512), 0) ^ lax.broadcasted_iota(jnp.int32, (512, 512), 1)) & 7 == 0
    left = lax.dot_general(up, table, (((1,), (1 if flip else 0,)), ((), ())), preferred_element_type=F32).astype(BF)
    return jnp.where(keep, dot(left, wide), 0.0).astype(BF)


def place():
    r, y = lax.axis_index("rows"), lax.axis_index("modes")
    x, z, core = r // 8, (r // 2) % 4, r % 2
    return y * (1 - core) + z * core, z * (1 - core) + y * core, x, core


def device(p, q, x, core):
    y, z = p * (1 - core) + q * core, q * (1 - core) + p * core
    return ((x * 4 + z) * 2 + core, y)


def sibling(p, q, x, core):
    return device(q, p, x, 1 - core)


def signal_peers():
    p, q, x, core = place()
    barrier = pltpu.get_barrier_semaphore()
    pl.semaphore_signal(barrier, inc=1, device_id=sibling(p, q, x, core), device_id_type=MESH)
    for d in range(1, 4):
        pl.semaphore_signal(barrier, inc=1, device_id=device((p + d) % 4, q, x, core), device_id_type=MESH)
    for k in range(1, 16):
        pl.semaphore_signal(barrier, inc=1, device_id=device(p, (q + k // 4) % 4, (x + k % 4) % 4, core), device_id_type=MESH)


def wait_peers():
    pl.semaphore_wait(pltpu.get_barrier_semaphore(), 19)


def remote(src, dst, send, recv, target):
    return pltpu.make_async_remote_copy(src_ref=src, dst_ref=dst, send_sem=send, recv_sem=recv, device_id=target, device_id_type=MESH)


def columns(block, tab, xs_ref, h0, count):
    prod = dot(block.reshape(count * 64, 512), tab).reshape(count, 8, 8, 256)
    for a in range(4):
        for g in range(2):
            v = prod[:, 2 * a + g].reshape(count * 8, 256).astype(BF)
            xs_ref[g, pl.ds(h0 * 8, count * 8), 128 * a : 128 * a + 128] = v[:, :128]
            xs_ref[g, pl.ds(512 + h0 * 8, count * 8), 128 * a : 128 * a + 128] = v[:, 128:]


def row_modes(xs_ref, rmat_ref, t_ref, owner):
    block = lanes_of((256, 128)) >> 5
    for g in range(2):
        o = dot(rmat_ref[pl.ds(pl.multiple_of(owner * 256, 256), 256), :], xs_ref[g])
        for m in range(4):
            total = None
            for a in range(4):
                v = o[:, 128 * a : 128 * a + 128]
                shift = (32 * (a - m)) % 128
                if shift:
                    v = pltpu.roll(v, shift, 1)
                total = v if total is None else jnp.where(block == a, v, total)
            total = total.astype(BF).reshape(4, 4, 16, 128)
            for z in range(4):
                t_ref[owner, m * (1 - owner) + z * owner, z * (1 - owner) + m * owner, :, g] = total[z]


def inverse(g_ref, imat_ref, out_ref, after=lambda b: None):
    even = lanes_of((512, 128)) & 1 == 0
    block = lanes_of((512, 128)) >> 5
    for b in range(4):
        cols = []
        for g in range(2):
            total = None
            for m in range(4):
                parts = [g_ref[0, m, :, :, g].reshape(256, 128)]
                parts += [g_ref[1, z, m, :, g].reshape(64, 128) for z in range(4)]
                v = jnp.concatenate(parts, axis=0).astype(F32)
                shift = (32 * (m - b)) % 128
                if shift:
                    v = pltpu.roll(v, shift, 1)
                total = v if total is None else jnp.where(block == m, v, total)
            swapped = jnp.where(even, -pltpu.roll(total, 127, 1), pltpu.roll(total, 1, 1))
            cols.append(jnp.concatenate([total.astype(BF), swapped.astype(BF)], axis=0))
        o = dot(imat_ref[...], jnp.concatenate(cols, axis=1))
        both = jnp.concatenate([o[:, :128].reshape(64, 8, 128), o[:, 128:].reshape(64, 8, 128)], axis=1)
        out_ref[:, 16 * b : 16 * b + 16, :] = both.astype(BF)
        after(b)


def gelu_grad(z):
    u = (0.3275911 * 0.7071067811865476) * jnp.abs(z)
    e = jnp.exp2((-0.5 * 1.4426950408889634) * z * z)
    t = 1.0 / (1.0 + u)
    poly = t * (0.5 * 0.254829592 + t * (-0.5 * 0.284496736 + t * (0.5 * 1.421413741 + t * (-0.5 * 1.453152027 + t * (0.5 * 1.061405429)))))
    r = (poly - (0.3989422804014327 / (0.3275911 * 0.7071067811865476)) * u) * e
    return jnp.where(z >= 0, 1.0 - r, r)


def duplicate(v):
    even = lax.broadcasted_iota(jnp.int32, v.shape, 0) & 1 == 0
    return jnp.where(even, v, pltpu.roll(v, 1, 0)), jnp.where(even, pltpu.roll(v, v.shape[0] - 1, 0), v)


def to_columns(block):
    turned = [[block[g] if a == 0 else pltpu.roll(block[g], 128 - 32 * a, 1) for g in range(2)] for a in range(4)]
    out = []
    for jj in range(2):
        rows = [turned[a][g][8 * jj : 8 * jj + 8] for a in range(4) for g in range(2)]
        out.append(jnp.concatenate(rows + rows, axis=0).T[:32, :64])
    return out


def to_block(cols):
    block = lanes_of((8, 128)) >> 5
    parts = []
    for v in cols:
        square = jnp.concatenate([jnp.concatenate([v, v], axis=1)] * 4, axis=0).T
        parts.append([])
        for g in range(2):
            out = square[8 * g : 8 * g + 8]
            for a in range(1, 4):
                out = jnp.where(block == a, square[16 * a + 8 * g : 16 * a + 8 * g + 8], out)
            parts[-1].append(out)
    return [jnp.concatenate([parts[0][g], parts[1][g]], axis=0) for g in range(2)]


def weigh(s, w_ref, jj):
    re, im = duplicate(s)
    t1 = jnp.zeros((32, 64), F32)
    t2 = jnp.zeros((32, 64), F32)
    for c in range(64):
        w = w_ref[jj, c].astype(F32)
        t1 += re[:, c : c + 1] * w
        t2 += im[:, c : c + 1] * w
    even = lax.broadcasted_iota(jnp.int32, (32, 64), 0) & 1 == 0
    return t1 + jnp.where(even, -pltpu.roll(t2, 31, 0), pltpu.roll(t2, 1, 0))


def weigh_back(d, w_ref, jj):
    even = lax.broadcasted_iota(jnp.int32, (32, 64), 0) & 1 == 0
    dsw = jnp.where(even, pltpu.roll(d, 31, 0), pltpu.roll(d, 1, 0))
    lane = lanes_of((32, 64))
    u1 = jnp.zeros((32, 64), F32)
    u2 = jnp.zeros((32, 64), F32)
    for c in range(64):
        w = w_ref[jj, c].astype(F32)
        u1 = jnp.where(lane == c, jnp.sum(w * d, axis=1, keepdims=True), u1)
        u2 = jnp.where(lane == c, jnp.sum(w * dsw, axis=1, keepdims=True), u2)
    return jnp.where(even, u1 + pltpu.roll(u1, 31, 0), pltpu.roll(u2, 1, 0) - u2)


FAR = (2, 1, 3, 0)
NEAR = (0, 1, 3, 2)


def arrived(ref, recv, k):
    p, q, x, core = place()
    remote(ref, ref, recv.at[k], recv.at[k], sibling(p, q, x, core)).wait_recv()


def sent(ref, send, k):
    p, q, x, core = place()
    remote(ref, ref, send.at[k], send.at[k], sibling(p, q, x, core)).wait_send()


def start_core(t_ref, b0, send, recv):
    p, q, x, core = place()
    for d in FAR:
        row = (p + d) % 4
        remote(t_ref.at[1 - core, :, row], b0.at[:, row], send.at[0], recv.at[d], sibling(p, q, x, core)).start()


def reduce_scatter(t_ref, bufs, send, recv, between=lambda i: None):
    b0, a1, b1, a2, b2 = bufs
    p, q, x, core = place()
    for d in FAR:
        row = (q + d) % 4
        arrived(b0.at[:, row], recv, d)
        for e in FAR:
            pt = (p + e) % 4
            a1[pt, row] = (t_ref[core, pt, row].astype(F32) + b0[pt, row].astype(F32)).astype(BF)
            if e:
                remote(a1.at[pt, row], b1.at[e - 1, row], send.at[1], recv.at[4 + d], device(pt, q, x, core)).start()
    between(0)
    for d in FAR:
        row = (q + d) % 4
        arrived(b1.at[:, row], recv, 4 + d)
        a2[row] = (a1[p, row].astype(F32) + b1[0, row].astype(F32) + b1[1, row].astype(F32) + b1[2, row].astype(F32)).astype(BF)
        for n in FAR:
            k = 4 * d + n
            if k:
                xt = (x + n) % 4
                remote(a2.at[row, xt], b2.at[k - 1], send.at[2], recv.at[8], device(p, row, xt, core)).start()
    own = a1[p, q, x].astype(F32)
    for k in range(3):
        own += b1[k, q, x].astype(F32)
    between(1)
    arrived(b2, recv, 8)
    for k in range(15):
        own += b2[k].astype(F32)
    return own


def drain_scatter(t_ref, bufs, send):
    sent(t_ref.at[0], send, 0)
    sent(bufs[2], send, 1)
    sent(bufs[4], send, 2)


def all_gather(g_ref, send, recv, between=lambda i: None):
    p, q, x, core = place()
    mine = g_ref.at[core, p, q, x]
    for d in (0, 2, 1, 3):
        for n in FAR:
            if 4 * d + n:
                remote(mine, mine, send.at[2], recv.at[8 + d], device(p, (q + d) % 4, (x + n) % 4, core)).start()
    between(2)
    for d in NEAR:
        row = (q + 4 - d) % 4
        arrived(g_ref.at[core, p, row, pl.ds(0, 4 if d else 3)], recv, 8 + d)
        mine = g_ref.at[core, p, row]
        for e in (2, 1, 3):
            remote(mine, mine, send.at[1], recv.at[4 + d], device((p + e) % 4, q, x, core)).start()
    between(3)
    for d in NEAR:
        row = (q + 4 - d) % 4
        arrived(g_ref.at[core, pl.ds(0, 3), row], recv, 4 + d)
        theirs = g_ref.at[core, :, row]
        remote(theirs, theirs, send.at[0], recv.at[0], sibling(p, q, x, core)).start()
    between(4)
    arrived(g_ref.at[1 - core], recv, 0)


def drain_gather(g_ref, bufs, send):
    sent(g_ref.at[0], send, 0)
    sent(g_ref.at[0, pl.ds(0, 3)], send, 1)
    sent(bufs[4], send, 2)


def main_kernel(act_hbm, cot_hbm, w_hbm, coltab_hbm, rowtab_hbm, lw_ref, bias_ref,
                dpre_hbm, rf2_hbm, s_ref, d_ref, lin_out_ref,
                act, cot, w_ref, tab, dtab, syn, rowtab, rmat, imat_ref, lw_t, bias_col, xs, rf, dpre, lin, t1, t2, g1, g2_ref, part,
                b0, a1, b1, a2, b2, c0, e1, c1, e2, c2,
                in_sem, out_sem, send1, recv1, send2, recv2, send3, recv3, send4, recv4, send5, recv5):
    p, q, x, core = place()
    signal_peers()
    row_dev, mode_dev = lax.axis_index("rows"), lax.axis_index("modes")
    loads = [
        pltpu.make_async_copy(coltab_hbm.at[mode_dev], tab, in_sem.at[0]),
        pltpu.make_async_copy(rowtab_hbm.at[row_dev], rowtab, in_sem.at[1]),
    ]
    loads += [pltpu.make_async_copy(act_hbm.at[pl.ds(16 * i, 16)], act.at[pl.ds(16 * i, 16)], in_sem.at[2 + i]) for i in range(4)]
    loads.append(pltpu.make_async_copy(w_hbm, w_ref, in_sem.at[6]))
    loads.append(pltpu.make_async_copy(cot_hbm, cot, in_sem.at[7]))
    for cp in loads:
        cp.start()
    loads[1].wait()
    rmat[:, :512] = kron8(rowtab[0], False)
    rmat[:, 512:] = kron8(rowtab[1], False)
    loads[0].wait()

    def analyse(i, _):
        rows = pl.ds(16 * i, 16)
        pltpu.make_async_copy(act_hbm.at[rows], act.at[rows], in_sem.at[2 + i]).wait()
        columns(act[rows], tab[...], xs, pl.multiple_of(16 * i, 16), 16)
        return 0

    lax.fori_loop(0, 4, analyse, 0)
    row_modes(xs, rmat, t1, 1 - core)
    wait_peers()
    start_core(t1, b0, send1, recv1)
    row_modes(xs, rmat, t1, core)

    def prepare(i):
        if i == 0:
            imat_ref[:, :512] = kron8(rowtab[0], True)
            imat_ref[:, 512:] = kron8(rowtab[1], True)
            lw_t[...] = lw_ref[...].astype(F32).T.astype(BF)
            bias_col[...] = jnp.broadcast_to(bias_ref[...], (128, 64)).T
        if i == 1:
            lane = lanes_of((512, 256)) % 128
            scaled = tab[...].astype(F32) * jnp.where(lane < 2, 2.0**-22, 2.0**-21)
            dtab[...] = scaled.astype(BF)
            syn[...] = scaled[:, :128].T.astype(BF)

    first, second = (b0, a1, b1, a2, b2), (c0, e1, c1, e2, c2)
    own = reduce_scatter(t1, first, send1, recv1, prepare)
    loads[6].wait()
    s = to_columns(own.astype(BF).astype(F32))
    mixed = []
    for jj in range(2):
        s_ref[jj] = s[jj]
        mixed.append(weigh(s[jj], w_ref, jj))
    for g, v in enumerate(to_block(mixed)):
        g1[core, p, q, x, g] = v.astype(BF)
    all_gather(g1, send2, recv2, lambda i: drain_scatter(t1, first, send1) if i == 3 else None)

    inverse(g1, imat_ref, rf)
    loads[7].wait()

    def rows(i, _):
        bias = jnp.concatenate([bias_col[...]] * 4, axis=1)
        for n in range(2):
            first = pl.multiple_of(16 * i + 8 * n, 8)
            ds = []
            for k in range(8):
                h = first + k
                lhs = jnp.concatenate([rf[h], lw_t[...]], axis=1)
                rhs = jnp.concatenate([syn[...], act[h]], axis=0)
                d = (cot[h].astype(F32) * gelu_grad(dot(lhs, rhs) + bias)).astype(BF)
                dpre[h] = d
                ds.append(d)
            columns(jnp.concatenate(ds, axis=0).reshape(8, 64, 512), dtab[...], xs, first, 8)
        some = pl.ds(16 * i, 16)
        pltpu.make_async_copy(dpre.at[some], dpre_hbm.at[some], out_sem.at[i]).start()
        return 0

    lax.fori_loop(0, 4, rows, 0)
    row_modes(xs, rmat, t2, 1 - core)
    start_core(t2, c0, send3, recv3)
    row_modes(xs, rmat, t2, core)

    steps = ((p, lambda v: device(v, q, x, core)), (q, lambda v: device(p, v, x, core)), (x, lambda v: device(p, q, v, core)))

    def swap_lin():
        part[0, core] = lin[...]
        drain_gather(g1, first, send2)
        remote(part.at[0, core], part.at[0, core], send5.at[0], recv5.at[0], sibling(p, q, x, core)).start()

    def join_lin(i):
        if i == 0:
            sent(part.at[0, 0], send5, 0)
            arrived(part.at[0, 0], recv5, 0)
            return part[0, 0] + part[0, 1]
        sent(part.at[i, pl.ds(0, 3)], send5, i)
        arrived(part.at[i, pl.ds(0, 3)], recv5, i)
        return part[i, 0] + part[i, 1] + part[i, 2] + part[i, 3]

    def pass_lin(i):
        me, at = steps[i]
        part[i + 1, me] = join_lin(i)
        mine = part.at[i + 1, me]
        for d in range(1, 4):
            remote(mine, mine, send5.at[i + 1], recv5.at[i + 1], at((me + d) % 4)).start()

    def products(i, _):
        left = jnp.concatenate([act[4 * i + k] for k in range(4)], axis=1)
        right = jnp.concatenate([dpre[4 * i + k] for k in range(4)], axis=1)
        left = jnp.concatenate([left, jnp.ones((16, 2048), BF)], axis=0)
        lin[...] += lax.dot_general(left, right, (((1,), (1,)), ((), ())), preferred_element_type=F32)
        return 0

    def local_products(i):
        if i == 0:
            lin[...] = jnp.zeros_like(lin)
            lax.fori_loop(0, 16, products, 0)
            swap_lin()
        if i >= 2:
            pass_lin(i - 2)
        if i == 3:
            drain_scatter(t2, second, send3)

    own = reduce_scatter(t2, second, send3, recv3, local_products)
    d = to_columns(own.astype(BF).astype(F32))
    back = []
    for jj in range(2):
        d_ref[jj] = d[jj]
        back.append(weigh_back(d[jj], w_ref, jj))
    for g, v in enumerate(to_block(back)):
        g2_ref[core, p, q, x, g] = v.astype(BF)
    all_gather(g2_ref, send4, recv4, local_products)

    def ship(b):
        return pltpu.make_async_copy(rf.at[:, pl.ds(16 * b, 16)], rf2_hbm.at[:, pl.ds(16 * b, 16)], out_sem.at[4 + b])

    inverse(g2_ref, imat_ref, rf, lambda b: ship(b).start())
    lin_out_ref[...] = join_lin(3) * (1.0 / 2048)
    drain_gather(g2_ref, second, send4)
    for i in range(4):
        some = pl.ds(16 * i, 16)
        pltpu.make_async_copy(dpre.at[some], dpre_hbm.at[some], out_sem.at[i]).wait()
        ship(i).wait()


def last_kernel(rf_hbm, dpre_hbm, coltab_hbm, lw_ref, s_ref, d_ref, lin_ref,
                gin_hbm, gspec_hbm, glin_ref, gbias_ref, rf, dpre, tab, ana, gin, gspec, in_sem, out_sem):
    load = pltpu.make_async_copy(coltab_hbm.at[lax.axis_index("modes")], tab, in_sem.at[8])
    load.start()

    def copy(n, i):
        some = pl.ds(16 * i, 16)
        if n == 2:
            return pltpu.make_async_copy(gin.at[some], gin_hbm.at[some], out_sem.at[i])
        src, dst = ((rf_hbm, rf), (dpre_hbm, dpre))[n]
        return pltpu.make_async_copy(src.at[some], dst.at[some], in_sem.at[2 * i + n])

    for i in range(4):
        copy(0, i).start()
        copy(1, i).start()
    glin_ref[...] = lin_ref[:64]
    gbias_ref[...] = lin_ref[64:65]
    even = lax.broadcasted_iota(jnp.int32, (32, 64), 0) & 1 == 0
    for jj in range(2):
        re, im = duplicate(s_ref[jj])
        d = d_ref[jj]
        dsw = jnp.where(even, pltpu.roll(d, 31, 0), -pltpu.roll(d, 1, 0))
        for c in range(64):
            gspec[jj, c] = re[:, c : c + 1] * d + im[:, c : c + 1] * dsw
        pltpu.make_async_copy(gspec.at[jj], gspec_hbm.at[jj], out_sem.at[4 + jj]).start()
    load.wait()
    ana[...] = tab[:, :128].astype(F32).T.astype(BF)

    def row(i, _):
        copy(0, i).wait()
        copy(1, i).wait()
        for k in range(16):
            lhs = jnp.concatenate([rf[16 * i + k], lw_ref[...]], axis=1)
            rhs = jnp.concatenate([ana[...], dpre[16 * i + k]], axis=0)
            gin[16 * i + k] = dot(lhs, rhs).astype(BF)
        copy(2, i).start()
        return 0

    lax.fori_loop(0, 4, row, 0)
    for jj in range(2):
        pltpu.make_async_copy(gspec.at[jj], gspec_hbm.at[jj], out_sem.at[4 + jj]).wait()
    for i in range(4):
        copy(2, i).wait()


SPEC = (2, 4, 4, 4, 2, 16, 128)
ANY = pl.BlockSpec(memory_space=pl.ANY)


def body(activations, cotangent, spectral_weight, linear_weight, bias):
    w = spectral_weight.transpose(0, 1, 3, 2)
    coltab, rowtab = jnp.asarray(column_constants()), jnp.asarray(row_constants())
    dma = pltpu.SemaphoreType.DMA
    quarter = (4, 4, 4, 2, 16, 128)
    buffers = [pltpu.VMEM(quarter, BF), pltpu.VMEM(quarter, BF), pltpu.VMEM((3, 4, 4, 2, 16, 128), BF),
               pltpu.VMEM((4, 4, 2, 16, 128), BF), pltpu.VMEM((15, 2, 16, 128), BF)]
    shape = jax.ShapeDtypeStruct
    dpre, rf, s, d, lin = pl.pallas_call(
        main_kernel,
        out_shape=[shape((64, 64, 512), BF), shape((64, 64, 128), BF), shape((2, 32, 64), F32), shape((2, 32, 64), F32),
                   shape((80, 64), F32)],
        in_specs=[ANY] * 5 + [VMEM] * 2,
        out_specs=[ANY] * 2 + [VMEM] * 3,
        scratch_shapes=[
            pltpu.VMEM((64, 64, 512), BF), pltpu.VMEM((64, 64, 512), BF), pltpu.VMEM((2, 64, 32, 64), BF),
            pltpu.VMEM((512, 256), BF), pltpu.VMEM((512, 256), BF), pltpu.VMEM((128, 512), BF), pltpu.VMEM((2, 64, 64), BF),
            pltpu.VMEM((512, 1024), BF), pltpu.VMEM((512, 1024), BF), pltpu.VMEM((64, 64), BF), pltpu.VMEM((64, 128), F32),
            pltpu.VMEM((2, 1024, 512), BF),
            pltpu.VMEM((64, 64, 128), BF), pltpu.VMEM((64, 64, 512), BF), pltpu.VMEM((80, 64), F32),
            pltpu.VMEM(SPEC, BF), pltpu.VMEM(SPEC, BF), pltpu.VMEM(SPEC, BF), pltpu.VMEM(SPEC, BF), pltpu.VMEM((4, 4, 80, 64), F32),
        ] + buffers + buffers + [dma((8,)), dma((8,))] + [dma((3,)), dma((12,))] * 4 + [dma((4,))] * 2,
        compiler_params=pltpu.CompilerParams(vmem_limit_bytes=LIMIT, collective_id=0, has_side_effects=True),
        name="main",
    )(activations, cotangent, w, coltab, rowtab, linear_weight, bias.reshape(1, 64))
    gin, gspec, glin, gbias = pl.pallas_call(
        last_kernel,
        out_shape=[shape((64, 64, 512), BF), shape((2, 64, 32, 64), F32), shape((64, 64), F32), shape((1, 64), F32)],
        in_specs=[ANY] * 3 + [VMEM] * 4,
        out_specs=[ANY] * 2 + [VMEM] * 2,
        scratch_shapes=[pltpu.VMEM((64, 64, 128), BF), pltpu.VMEM((64, 64, 512), BF), pltpu.VMEM((512, 256), BF),
                        pltpu.VMEM((128, 512), BF), pltpu.VMEM((64, 64, 512), BF), pltpu.VMEM((2, 64, 32, 64), F32),
                        dma((9,)), dma((6,))],
        compiler_params=pltpu.CompilerParams(vmem_limit_bytes=LIMIT),
        name="last",
    )(rf, dpre, coltab, linear_weight, s, d, lin)
    return gin, gspec.transpose(0, 1, 3, 2), glin, gbias.reshape(64)


def solution(mesh):
    return jax.shard_map(
        body,
        mesh=mesh,
        in_specs=(
            P("rows", None, "modes"),
            P("rows", None, "modes"),
            P("rows", None, None, "modes"),
            P(),
            P(),
        ),
        out_specs=(P("rows", None, "modes"), P("rows", None, None, "modes"), P(), P()),
        check_vma=False,
    )
```

```python
import math

import jax
import jax.numpy as jnp
import numpy as np
from jax import lax
from jax.experimental import pallas as pl
from jax.experimental.pallas import tpu as pltpu
from jax.sharding import PartitionSpec as P

MESH = pl.DeviceIdType.MESH
BF = jnp.bfloat16
F32 = jnp.float32
VMEM = pl.BlockSpec(memory_space=pltpu.VMEM)
LIMIT = 60 * 1024 * 1024


def dot(a, b):
    return jnp.dot(a, b, preferred_element_type=F32)


def lanes_of(shape):
    return lax.broadcasted_iota(jnp.int32, shape, len(shape) - 1)


def column_constants():
    k = np.arange(128) // 2
    w = np.arange(2048)
    ang = ((w[:, None] * k[None, :]) % 2048) * (2.0 * math.pi / 2048)
    even = (np.arange(128) % 2 == 0)[None, :]
    ana = np.where(even, np.cos(ang), -np.sin(ang))
    swap = np.where(even, -np.sin(ang), -np.cos(ang))
    return np.concatenate([ana, swap], axis=1).reshape(4, 512, 256).astype(np.float32).astype(jnp.bfloat16)


def row_constants():
    slot = np.arange(64)
    core, z, x, jj = slot // 32, (slot // 8) % 4, (slot // 2) % 4, slot % 2
    mode = x * 16 + z * 4 + core * 2 + jj
    freq = np.where(mode < 32, mode, mode - 64)
    rows = np.arange(2048).reshape(32, 64)
    ang = ((freq[None, :, None] * rows[:, None, :]) % 2048) * (2.0 * math.pi / 2048)
    return np.stack([np.cos(ang), np.sin(ang)], axis=1).astype(np.float32).astype(jnp.bfloat16)


def kron8(table, flip):
    up = (lax.broadcasted_iota(jnp.int32, (512, 64), 0) >> 3 == lax.broadcasted_iota(jnp.int32, (512, 64), 1)).astype(BF)
    wide = (lax.broadcasted_iota(jnp.int32, (64, 512), 1) >> 3 == lax.broadcasted_iota(jnp.int32, (64, 512), 0)).astype(BF)
    keep = (lax.broadcasted_iota(jnp.int32, (512, 512), 0) ^ lax.broadcasted_iota(jnp.int32, (512, 512), 1)) & 7 == 0
    left = lax.dot_general(up, table, (((1,), (1 if flip else 0,)), ((), ())), preferred_element_type=F32).astype(BF)
    return jnp.where(keep, dot(left, wide), 0.0).astype(BF)


def place():
    r, y = lax.axis_index("rows"), lax.axis_index("modes")
    x, z, core = r // 8, (r // 2) % 4, r % 2
    return y * (1 - core) + z * core, z * (1 - core) + y * core, x, core


def device(p, q, x, core):
    y, z = p * (1 - core) + q * core, q * (1 - core) + p * core
    return ((x * 4 + z) * 2 + core, y)


def sibling(p, q, x, core):
    return device(q, p, x, 1 - core)


def signal_peers():
    p, q, x, core = place()
    barrier = pltpu.get_barrier_semaphore()
    pl.semaphore_signal(barrier, inc=1, device_id=sibling(p, q, x, core), device_id_type=MESH)
    for d in range(1, 4):
        pl.semaphore_signal(barrier, inc=1, device_id=device((p + d) % 4, q, x, core), device_id_type=MESH)
    for k in range(1, 16):
        pl.semaphore_signal(barrier, inc=1, device_id=device(p, (q + k // 4) % 4, (x + k % 4) % 4, core), device_id_type=MESH)


def wait_peers():
    pl.semaphore_wait(pltpu.get_barrier_semaphore(), 19)


def remote(src, dst, send, recv, target):
    return pltpu.make_async_remote_copy(src_ref=src, dst_ref=dst, send_sem=send, recv_sem=recv, device_id=target, device_id_type=MESH)


def columns(block, tab, xs_ref, h0, count):
    prod = dot(block.reshape(count * 64, 512), tab).reshape(count, 8, 8, 256)
    for a in range(4):
        for g in range(2):
            v = prod[:, 2 * a + g].reshape(count * 8, 256).astype(BF)
            xs_ref[g, pl.ds(h0 * 8, count * 8), 128 * a : 128 * a + 128] = v[:, :128]
            xs_ref[g, pl.ds(512 + h0 * 8, count * 8), 128 * a : 128 * a + 128] = v[:, 128:]


def row_modes(xs_ref, rmat_ref, t_ref, owner):
    block = lanes_of((256, 128)) >> 5
    for g in range(2):
        o = dot(rmat_ref[pl.ds(pl.multiple_of(owner * 256, 256), 256), :], xs_ref[g])
        for m in range(4):
            total = None
            for a in range(4):
                v = o[:, 128 * a : 128 * a + 128]
                shift = (32 * (a - m)) % 128
                if shift:
                    v = pltpu.roll(v, shift, 1)
                total = v if total is None else jnp.where(block == a, v, total)
            total = total.astype(BF).reshape(4, 4, 16, 128)
            for z in range(4):
                t_ref[owner, m * (1 - owner) + z * owner, z * (1 - owner) + m * owner, :, g] = total[z]


def inverse(g_ref, imat_ref, out_ref, after=lambda b: None):
    even = lanes_of((512, 128)) & 1 == 0
    block = lanes_of((512, 128)) >> 5
    for b in range(4):
        cols = []
        for g in range(2):
            total = None
            for m in range(4):
                parts = [g_ref[0, m, :, :, g].reshape(256, 128)]
                parts += [g_ref[1, z, m, :, g].reshape(64, 128) for z in range(4)]
                v = jnp.concatenate(parts, axis=0).astype(F32)
                shift = (32 * (m - b)) % 128
                if shift:
                    v = pltpu.roll(v, shift, 1)
                total = v if total is None else jnp.where(block == m, v, total)
            swapped = jnp.where(even, -pltpu.roll(total, 127, 1), pltpu.roll(total, 1, 1))
            cols.append(jnp.concatenate([total.astype(BF), swapped.astype(BF)], axis=0))
        o = dot(imat_ref[...], jnp.concatenate(cols, axis=1))
        both = jnp.concatenate([o[:, :128].reshape(64, 8, 128), o[:, 128:].reshape(64, 8, 128)], axis=1)
        out_ref[:, 16 * b : 16 * b + 16, :] = both.astype(BF)
        after(b)


def gelu_grad(z):
    u = (0.3275911 * 0.7071067811865476) * jnp.abs(z)
    e = jnp.exp2((-0.5 * 1.4426950408889634) * z * z)
    t = 1.0 / (1.0 + u)
    poly = t * (0.5 * 0.254829592 + t * (-0.5 * 0.284496736 + t * (0.5 * 1.421413741 + t * (-0.5 * 1.453152027 + t * (0.5 * 1.061405429)))))
    r = (poly - (0.3989422804014327 / (0.3275911 * 0.7071067811865476)) * u) * e
    return jnp.where(z >= 0, 1.0 - r, r)


def duplicate(v):
    even = lax.broadcasted_iota(jnp.int32, v.shape, 0) & 1 == 0
    return jnp.where(even, v, pltpu.roll(v, 1, 0)), jnp.where(even, pltpu.roll(v, v.shape[0] - 1, 0), v)


def to_columns(block):
    turned = [[block[g] if a == 0 else pltpu.roll(block[g], 128 - 32 * a, 1) for g in range(2)] for a in range(4)]
    out = []
    for jj in range(2):
        rows = [turned[a][g][8 * jj : 8 * jj + 8] for a in range(4) for g in range(2)]
        out.append(jnp.concatenate(rows + rows, axis=0).T[:32, :64])
    return out


def to_block(cols):
    block = lanes_of((8, 128)) >> 5
    parts = []
    for v in cols:
        square = jnp.concatenate([jnp.concatenate([v, v], axis=1)] * 4, axis=0).T
        parts.append([])
        for g in range(2):
            out = square[8 * g : 8 * g + 8]
            for a in range(1, 4):
                out = jnp.where(block == a, square[16 * a + 8 * g : 16 * a + 8 * g + 8], out)
            parts[-1].append(out)
    return [jnp.concatenate([parts[0][g], parts[1][g]], axis=0) for g in range(2)]


def weigh(s, w_ref, jj):
    re, im = duplicate(s)
    t1 = jnp.zeros((32, 64), F32)
    t2 = jnp.zeros((32, 64), F32)
    for c in range(64):
        w = w_ref[jj, c].astype(F32)
        t1 += re[:, c : c + 1] * w
        t2 += im[:, c : c + 1] * w
    even = lax.broadcasted_iota(jnp.int32, (32, 64), 0) & 1 == 0
    return t1 + jnp.where(even, -pltpu.roll(t2, 31, 0), pltpu.roll(t2, 1, 0))


def weigh_back(d, w_ref, jj):
    even = lax.broadcasted_iota(jnp.int32, (32, 64), 0) & 1 == 0
    dsw = jnp.where(even, pltpu.roll(d, 31, 0), pltpu.roll(d, 1, 0))
    lane = lanes_of((32, 64))
    u1 = jnp.zeros((32, 64), F32)
    u2 = jnp.zeros((32, 64), F32)
    for c in range(64):
        w = w_ref[jj, c].astype(F32)
        u1 = jnp.where(lane == c, jnp.sum(w * d, axis=1, keepdims=True), u1)
        u2 = jnp.where(lane == c, jnp.sum(w * dsw, axis=1, keepdims=True), u2)
    return jnp.where(even, u1 + pltpu.roll(u1, 31, 0), pltpu.roll(u2, 1, 0) - u2)


FAR = (2, 1, 3, 0)
NEAR = (0, 1, 3, 2)


def arrived(ref, recv, k):
    p, q, x, core = place()
    remote(ref, ref, recv.at[k], recv.at[k], sibling(p, q, x, core)).wait_recv()


def sent(ref, send, k):
    p, q, x, core = place()
    remote(ref, ref, send.at[k], send.at[k], sibling(p, q, x, core)).wait_send()


def start_core(t_ref, b0, send, recv):
    p, q, x, core = place()
    for d in FAR:
        row = (p + d) % 4
        remote(t_ref.at[1 - core, :, row], b0.at[:, row], send.at[0], recv.at[d], sibling(p, q, x, core)).start()


def reduce_scatter(t_ref, bufs, send, recv, between=lambda i: None):
    b0, a1, b1, a2, b2 = bufs
    p, q, x, core = place()
    for d in FAR:
        row = (q + d) % 4
        arrived(b0.at[:, row], recv, d)
        for e in FAR:
            pt = (p + e) % 4
            a1[pt, row] = (t_ref[core, pt, row].astype(F32) + b0[pt, row].astype(F32)).astype(BF)
            if e:
                remote(a1.at[pt, row], b1.at[e - 1, row], send.at[1], recv.at[4 + d], device(pt, q, x, core)).start()
    between(0)
    for d in FAR:
        row = (q + d) % 4
        arrived(b1.at[:, row], recv, 4 + d)
        a2[row] = (a1[p, row].astype(F32) + b1[0, row].astype(F32) + b1[1, row].astype(F32) + b1[2, row].astype(F32)).astype(BF)
        for n in FAR:
            k = 4 * d + n
            if k:
                xt = (x + n) % 4
                remote(a2.at[row, xt], b2.at[k - 1], send.at[2], recv.at[8], device(p, row, xt, core)).start()
    own = a1[p, q, x].astype(F32)
    for k in range(3):
        own += b1[k, q, x].astype(F32)
    between(1)
    arrived(b2, recv, 8)
    for k in range(15):
        own += b2[k].astype(F32)
    return own


def drain_scatter(t_ref, bufs, send):
    sent(t_ref.at[0], send, 0)
    sent(bufs[2], send, 1)
    sent(bufs[4], send, 2)


def all_gather(g_ref, send, recv, between=lambda i: None):
    p, q, x, core = place()
    mine = g_ref.at[core, p, q, x]
    for d in (0, 2, 1, 3):
        for n in FAR:
            if 4 * d + n:
                remote(mine, mine, send.at[2], recv.at[8 + d], device(p, (q + d) % 4, (x + n) % 4, core)).start()
    between(2)
    for d in NEAR:
        row = (q + 4 - d) % 4
        arrived(g_ref.at[core, p, row, pl.ds(0, 4 if d else 3)], recv, 8 + d)
        mine = g_ref.at[core, p, row]
        for e in (2, 1, 3):
            remote(mine, mine, send.at[1], recv.at[4 + d], device((p + e) % 4, q, x, core)).start()
    between(3)
    for d in NEAR:
        row = (q + 4 - d) % 4
        arrived(g_ref.at[core, pl.ds(0, 3), row], recv, 4 + d)
        theirs = g_ref.at[core, :, row]
        remote(theirs, theirs, send.at[0], recv.at[0], sibling(p, q, x, core)).start()
    between(4)
    arrived(g_ref.at[1 - core], recv, 0)


def drain_gather(g_ref, bufs, send):
    sent(g_ref.at[0], send, 0)
    sent(g_ref.at[0, pl.ds(0, 3)], send, 1)
    sent(bufs[4], send, 2)


def main_kernel(act_hbm, cot_hbm, w_hbm, coltab_hbm, rowtab_hbm, lw_ref, bias_ref,
                loc_hbm, rf2_hbm, s_ref, d_ref, lin_out_ref,
                act, cot, w_ref, tab, dtab, syn, rowtab, rmat, imat_ref, lw_t, bias_col, xs, rf, dpre, loc, lin, t1, t2, g1, g2_ref, part,
                b0, a1, b1, a2, b2, c0, e1, c1, e2, c2,
                in_sem, out_sem, send1, recv1, send2, recv2, send3, recv3, send4, recv4, send5, recv5):
    p, q, x, core = place()
    signal_peers()
    row_dev, mode_dev = lax.axis_index("rows"), lax.axis_index("modes")
    def load_act(i):
        some = pl.ds(16 * i, 16)
        return pltpu.make_async_copy(act_hbm.at[some], act.at[some], in_sem.at[2 + i])

    load_rows = pltpu.make_async_copy(rowtab_hbm.at[row_dev], rowtab, in_sem.at[1])
    load_cols = pltpu.make_async_copy(coltab_hbm.at[mode_dev], tab, in_sem.at[0])
    load_w = pltpu.make_async_copy(w_hbm, w_ref, in_sem.at[6])
    load_cot = pltpu.make_async_copy(cot_hbm, cot, in_sem.at[7])
    load_rows.start()
    load_cols.start()
    for i in range(4):
        load_act(i).start()
    load_rows.wait()
    rmat[:, :512] = kron8(rowtab[0], False)
    rmat[:, 512:] = kron8(rowtab[1], False)
    load_cols.wait()

    def analyse(i, _):
        load_act(i).wait()
        columns(act[pl.ds(16 * i, 16)], tab[...], xs, pl.multiple_of(16 * i, 16), 16)
        return 0

    lax.fori_loop(0, 4, analyse, 0)
    load_w.start()
    load_cot.start()
    row_modes(xs, rmat, t1, 1 - core)
    wait_peers()
    start_core(t1, b0, send1, recv1)
    row_modes(xs, rmat, t1, core)

    def prepare(i):
        if i == 0:
            imat_ref[:, :512] = kron8(rowtab[0], True)
            imat_ref[:, 512:] = kron8(rowtab[1], True)
            lw_t[...] = lw_ref[...].astype(F32).T.astype(BF)
            bias_col[...] = jnp.broadcast_to(bias_ref[...], (128, 64)).T
        if i == 1:
            lane = lanes_of((512, 256)) % 128
            scaled = tab[...].astype(F32) * jnp.where(lane < 2, 2.0**-22, 2.0**-21)
            dtab[...] = scaled.astype(BF)
            syn[...] = scaled[:, :128].T.astype(BF)

    first, second = (b0, a1, b1, a2, b2), (c0, e1, c1, e2, c2)
    own = reduce_scatter(t1, first, send1, recv1, prepare)
    load_w.wait()
    s = to_columns(own.astype(BF).astype(F32))
    mixed = []
    for jj in range(2):
        s_ref[jj] = s[jj]
        mixed.append(weigh(s[jj], w_ref, jj))
    for g, v in enumerate(to_block(mixed)):
        g1[core, p, q, x, g] = v.astype(BF)
    all_gather(g1, send2, recv2, lambda i: drain_scatter(t1, first, send1) if i == 3 else None)

    inverse(g1, imat_ref, rf)
    load_cot.wait()

    def rows(i, _):
        bias = jnp.concatenate([bias_col[...]] * 4, axis=1)
        for n in range(2):
            first = pl.multiple_of(16 * i + 8 * n, 8)
            ds = []
            for k in range(8):
                h = first + k
                lhs = jnp.concatenate([rf[h], lw_t[...]], axis=1)
                rhs = jnp.concatenate([syn[...], act[h]], axis=0)
                d = (cot[h].astype(F32) * gelu_grad(dot(lhs, rhs) + bias)).astype(BF)
                dpre[h] = d
                ds.append(d)
            columns(jnp.concatenate(ds, axis=0).reshape(8, 64, 512), dtab[...], xs, first, 8)
        return 0

    lax.fori_loop(0, 4, rows, 0)
    row_modes(xs, rmat, t2, 1 - core)
    start_core(t2, c0, send3, recv3)
    row_modes(xs, rmat, t2, core)

    steps = ((p, lambda v: device(v, q, x, core)), (q, lambda v: device(p, v, x, core)), (x, lambda v: device(p, q, v, core)))

    def swap_lin():
        part[0, core] = lin[...]
        drain_gather(g1, first, send2)
        remote(part.at[0, core], part.at[0, core], send5.at[0], recv5.at[0], sibling(p, q, x, core)).start()

    def join_lin(i):
        if i == 0:
            sent(part.at[0, 0], send5, 0)
            arrived(part.at[0, 0], recv5, 0)
            return part[0, 0] + part[0, 1]
        sent(part.at[i, pl.ds(0, 3)], send5, i)
        arrived(part.at[i, pl.ds(0, 3)], recv5, i)
        return part[i, 0] + part[i, 1] + part[i, 2] + part[i, 3]

    def pass_lin(i):
        me, at = steps[i]
        part[i + 1, me] = join_lin(i)
        mine = part.at[i + 1, me]
        for d in range(1, 4):
            remote(mine, mine, send5.at[i + 1], recv5.at[i + 1], at((me + d) % 4)).start()

    def products(i, _):
        left = jnp.concatenate([act[4 * i + k] for k in range(4)], axis=1)
        right = jnp.concatenate([dpre[4 * i + k] for k in range(4)], axis=1)
        left = jnp.concatenate([left, jnp.ones((16, 2048), BF)], axis=0)
        lin[...] += lax.dot_general(left, right, (((1,), (1,)), ((), ())), preferred_element_type=F32)
        return 0

    def local_products(i):
        if i == 0:
            lin[...] = jnp.zeros_like(lin)
            lax.fori_loop(0, 16, products, 0)
            swap_lin()
        if i >= 2:
            pass_lin(i - 2)
        if i == 3:
            drain_scatter(t2, second, send3)
        if i in (1, 2):
            lax.fori_loop(2 * i - 2, 2 * i, pointwise, 0)

    def pointwise(i, _):
        def some_rows(n, _):
            for k in range(8):
                h = 16 * i + 8 * n + k
                loc[h] = dot(lw_ref[...], dpre[h]).astype(BF)
            return 0

        lax.fori_loop(0, 2, some_rows, 0)
        some = pl.ds(16 * i, 16)
        pltpu.make_async_copy(loc.at[some], loc_hbm.at[some], out_sem.at[i]).start()
        return 0

    own = reduce_scatter(t2, second, send3, recv3, local_products)
    d = to_columns(own.astype(BF).astype(F32))
    back = []
    for jj in range(2):
        d_ref[jj] = d[jj]
        back.append(weigh_back(d[jj], w_ref, jj))
    for g, v in enumerate(to_block(back)):
        g2_ref[core, p, q, x, g] = v.astype(BF)
    all_gather(g2_ref, send4, recv4, local_products)

    def ship(b):
        return pltpu.make_async_copy(rf.at[:, pl.ds(16 * b, 16)], rf2_hbm.at[:, pl.ds(16 * b, 16)], out_sem.at[4 + b])

    inverse(g2_ref, imat_ref, rf, lambda b: ship(b).start())
    lin_out_ref[...] = join_lin(3) * (1.0 / 2048)
    drain_gather(g2_ref, second, send4)
    for i in range(4):
        some = pl.ds(16 * i, 16)
        pltpu.make_async_copy(loc.at[some], loc_hbm.at[some], out_sem.at[i]).wait()
        ship(i).wait()


def last_kernel(rf_hbm, loc_hbm, coltab_hbm, s_ref, d_ref, lin_ref,
                gin_hbm, gspec_hbm, glin_ref, gbias_ref, rf, loc, tab, ana, gin, gspec, in_sem, out_sem):
    load = pltpu.make_async_copy(coltab_hbm.at[lax.axis_index("modes")], tab, in_sem.at[8])
    load.start()

    def copy(n, i):
        some = pl.ds(16 * i, 16)
        if n == 2:
            return pltpu.make_async_copy(gin.at[some], gin_hbm.at[some], out_sem.at[i])
        src, dst = ((rf_hbm, rf), (loc_hbm, loc))[n]
        return pltpu.make_async_copy(src.at[some], dst.at[some], in_sem.at[2 * i + n])

    for i in range(2):
        copy(0, i).start()
        copy(1, i).start()
    glin_ref[...] = lin_ref[:64]
    gbias_ref[...] = lin_ref[64:65]
    even = lax.broadcasted_iota(jnp.int32, (32, 64), 0) & 1 == 0
    def products(jj, _):
        re, im = duplicate(s_ref[jj])
        d = d_ref[jj]
        dsw = jnp.where(even, pltpu.roll(d, 31, 0), -pltpu.roll(d, 1, 0))
        for c in range(64):
            gspec[jj, c] = re[:, c : c + 1] * d + im[:, c : c + 1] * dsw
        pltpu.make_async_copy(gspec.at[jj], gspec_hbm.at[jj], out_sem.at[4 + jj]).start()
        return 0

    lax.fori_loop(0, 2, products, 0)
    load.wait()
    ana[...] = tab[:, :128].astype(F32).T.astype(BF)

    def row(i, _):
        copy(0, i).wait()
        copy(1, i).wait()

        @pl.when(i < 2)
        def _():
            copy(0, i + 2).start()
            copy(1, i + 2).start()

        for k in range(4):
            some = pl.ds(16 * i + 4 * k, 4)
            part = dot(rf[some].reshape(256, 128), ana[...]).reshape(4, 64, 512)
            gin[some] = (part + loc[some].astype(F32)).astype(BF)
        copy(2, i).start()
        return 0

    lax.fori_loop(0, 4, row, 0)
    for jj in range(2):
        pltpu.make_async_copy(gspec.at[jj], gspec_hbm.at[jj], out_sem.at[4 + jj]).wait()
    for i in range(4):
        copy(2, i).wait()


SPEC = (2, 4, 4, 4, 2, 16, 128)
ANY = pl.BlockSpec(memory_space=pl.ANY)


def body(activations, cotangent, spectral_weight, linear_weight, bias):
    w = spectral_weight.transpose(0, 1, 3, 2)
    coltab, rowtab = jnp.asarray(column_constants()), jnp.asarray(row_constants())
    dma = pltpu.SemaphoreType.DMA
    quarter = (4, 4, 4, 2, 16, 128)
    buffers = [pltpu.VMEM(quarter, BF), pltpu.VMEM(quarter, BF), pltpu.VMEM((3, 4, 4, 2, 16, 128), BF),
               pltpu.VMEM((4, 4, 2, 16, 128), BF), pltpu.VMEM((15, 2, 16, 128), BF)]
    shape = jax.ShapeDtypeStruct
    loc, rf, s, d, lin = pl.pallas_call(
        main_kernel,
        out_shape=[shape((64, 64, 512), BF), shape((64, 64, 128), BF), shape((2, 32, 64), F32), shape((2, 32, 64), F32),
                   shape((80, 64), F32)],
        in_specs=[ANY] * 5 + [VMEM] * 2,
        out_specs=[ANY] * 2 + [VMEM] * 3,
        scratch_shapes=[
            pltpu.VMEM((64, 64, 512), BF), pltpu.VMEM((64, 64, 512), BF), pltpu.VMEM((2, 64, 32, 64), BF),
            pltpu.VMEM((512, 256), BF), pltpu.VMEM((512, 256), BF), pltpu.VMEM((128, 512), BF), pltpu.VMEM((2, 64, 64), BF),
            pltpu.VMEM((512, 1024), BF), pltpu.VMEM((512, 1024), BF), pltpu.VMEM((64, 64), BF), pltpu.VMEM((64, 128), F32),
            pltpu.VMEM((2, 1024, 512), BF),
            pltpu.VMEM((64, 64, 128), BF), pltpu.VMEM((64, 64, 512), BF), pltpu.VMEM((64, 64, 512), BF), pltpu.VMEM((80, 64), F32),
            pltpu.VMEM(SPEC, BF), pltpu.VMEM(SPEC, BF), pltpu.VMEM(SPEC, BF), pltpu.VMEM(SPEC, BF), pltpu.VMEM((4, 4, 80, 64), F32),
        ] + buffers + buffers + [dma((8,)), dma((8,))] + [dma((3,)), dma((12,))] * 4 + [dma((4,))] * 2,
        compiler_params=pltpu.CompilerParams(vmem_limit_bytes=LIMIT, collective_id=0, has_side_effects=True),
        name="main",
    )(activations, cotangent, w, coltab, rowtab, linear_weight, bias.reshape(1, 64))
    gin, gspec, glin, gbias = pl.pallas_call(
        last_kernel,
        out_shape=[shape((64, 64, 512), BF), shape((2, 64, 32, 64), F32), shape((64, 64), F32), shape((1, 64), F32)],
        in_specs=[ANY] * 3 + [VMEM] * 3,
        out_specs=[ANY] * 2 + [VMEM] * 2,
        scratch_shapes=[pltpu.VMEM((64, 64, 128), BF), pltpu.VMEM((64, 64, 512), BF), pltpu.VMEM((512, 256), BF),
                        pltpu.VMEM((128, 512), BF), pltpu.VMEM((64, 64, 512), BF), pltpu.VMEM((2, 64, 32, 64), F32),
                        dma((9,)), dma((6,))],
        compiler_params=pltpu.CompilerParams(vmem_limit_bytes=LIMIT),
        name="last",
    )(rf, loc, coltab, s, d, lin)
    return gin, gspec.transpose(0, 1, 3, 2), glin, gbias.reshape(64)


def solution(mesh):
    return jax.shard_map(
        body,
        mesh=mesh,
        in_specs=(
            P("rows", None, "modes"),
            P("rows", None, "modes"),
            P("rows", None, None, "modes"),
            P(),
            P(),
        ),
        out_specs=(P("rows", None, "modes"), P("rows", None, None, "modes"), P(), P()),
        check_vma=False,
    )
```

```python
import math

import jax
import jax.numpy as jnp
import numpy as np
from jax import lax
from jax.experimental import pallas as pl
from jax.experimental.pallas import tpu as pltpu
from jax.sharding import PartitionSpec as P

MESH = pl.DeviceIdType.MESH
BF = jnp.bfloat16
F32 = jnp.float32
VMEM = pl.BlockSpec(memory_space=pltpu.VMEM)
LIMIT = 60 * 1024 * 1024


def dot(a, b):
    return jnp.dot(a, b, preferred_element_type=F32)


def lanes_of(shape):
    return lax.broadcasted_iota(jnp.int32, shape, len(shape) - 1)


def column_constants():
    k = np.arange(128) // 2
    w = np.arange(2048)
    ang = ((w[:, None] * k[None, :]) % 2048) * (2.0 * math.pi / 2048)
    even = (np.arange(128) % 2 == 0)[None, :]
    ana = np.where(even, np.cos(ang), -np.sin(ang))
    swap = np.where(even, -np.sin(ang), -np.cos(ang))
    return np.concatenate([ana, swap], axis=1).reshape(4, 512, 256).astype(np.float32).astype(jnp.bfloat16)


def row_constants():
    slot = np.arange(64)
    core, z, x, jj = slot // 32, (slot // 8) % 4, (slot // 2) % 4, slot % 2
    mode = x * 16 + z * 4 + core * 2 + jj
    freq = np.where(mode < 32, mode, mode - 64)
    rows = np.arange(2048).reshape(32, 64)
    ang = ((freq[None, :, None] * rows[:, None, :]) % 2048) * (2.0 * math.pi / 2048)
    return np.stack([np.cos(ang), np.sin(ang)], axis=1).astype(np.float32).astype(jnp.bfloat16)


def kron8(table, flip):
    up = (lax.broadcasted_iota(jnp.int32, (512, 64), 0) >> 3 == lax.broadcasted_iota(jnp.int32, (512, 64), 1)).astype(BF)
    wide = (lax.broadcasted_iota(jnp.int32, (64, 512), 1) >> 3 == lax.broadcasted_iota(jnp.int32, (64, 512), 0)).astype(BF)
    keep = (lax.broadcasted_iota(jnp.int32, (512, 512), 0) ^ lax.broadcasted_iota(jnp.int32, (512, 512), 1)) & 7 == 0
    left = lax.dot_general(up, table, (((1,), (1 if flip else 0,)), ((), ())), preferred_element_type=F32).astype(BF)
    return jnp.where(keep, dot(left, wide), 0.0).astype(BF)


class Spot:
    def __init__(self):
        r, y = lax.axis_index("rows"), lax.axis_index("modes")
        x, z, core = lax.div(r, 8), lax.rem(lax.div(r, 2), 4), lax.rem(r, 2)
        p, q = y * (1 - core) + z * core, z * (1 - core) + y * core
        self.core, self.other = core, 1 - core
        self.p = [lax.rem(p + d, 4) for d in range(4)]
        self.q = [lax.rem(q + d, 4) for d in range(4)]
        self.x = [lax.rem(x + d, 4) for d in range(4)]
        self.sibling = (r + 1 - 2 * core, y)
        self.first = [self.at(v, q, x) for v in self.p]
        self.plane = [[self.at(p, v, u) for u in self.x] for v in self.q]

    def at(self, p, q, x):
        y, z = p * self.other + q * self.core, q * self.other + p * self.core
        return ((x * 4 + z) * 2 + self.core, y)


def signal_peers(spot):
    barrier = pltpu.get_barrier_semaphore()
    peers = [spot.sibling] + spot.first[1:] + [spot.plane[k // 4][k % 4] for k in range(1, 16)]
    for peer in peers:
        pl.semaphore_signal(barrier, inc=1, device_id=peer, device_id_type=MESH)


def wait_peers():
    pl.semaphore_wait(pltpu.get_barrier_semaphore(), 19)


def remote(src, dst, send, recv, target):
    return pltpu.make_async_remote_copy(src_ref=src, dst_ref=dst, send_sem=send, recv_sem=recv, device_id=target, device_id_type=MESH)


def columns(block, tab, xs_ref, h0, count):
    prod = dot(block.reshape(count * 64, 512), tab).reshape(count, 8, 8, 256)
    for a in range(4):
        for g in range(2):
            v = prod[:, 2 * a + g].reshape(count * 8, 256).astype(BF)
            xs_ref[g, pl.ds(h0 * 8, count * 8), 128 * a : 128 * a + 128] = v[:, :128]
            xs_ref[g, pl.ds(512 + h0 * 8, count * 8), 128 * a : 128 * a + 128] = v[:, 128:]


def row_modes(xs_ref, rmat_ref, t_ref, owner):
    block = lanes_of((256, 128)) >> 5
    for g in range(2):
        o = dot(rmat_ref[pl.ds(pl.multiple_of(owner * 256, 256), 256), :], xs_ref[g])
        for m in range(4):
            total = None
            for a in range(4):
                v = o[:, 128 * a : 128 * a + 128]
                shift = (32 * (a - m)) % 128
                if shift:
                    v = pltpu.roll(v, shift, 1)
                total = v if total is None else jnp.where(block == a, v, total)
            total = total.astype(BF).reshape(4, 4, 16, 128)
            for z in range(4):
                t_ref[owner, m * (1 - owner) + z * owner, z * (1 - owner) + m * owner, :, g] = total[z]


def inverse(g_ref, imat_ref, out_ref, after=lambda b: None):
    even = lanes_of((512, 128)) & 1 == 0
    block = lanes_of((512, 128)) >> 5
    for b in range(4):
        cols = []
        for g in range(2):
            total = None
            for m in range(4):
                parts = [g_ref[0, m, :, :, g].reshape(256, 128)]
                parts += [g_ref[1, z, m, :, g].reshape(64, 128) for z in range(4)]
                v = jnp.concatenate(parts, axis=0).astype(F32)
                shift = (32 * (m - b)) % 128
                if shift:
                    v = pltpu.roll(v, shift, 1)
                total = v if total is None else jnp.where(block == m, v, total)
            swapped = jnp.where(even, -pltpu.roll(total, 127, 1), pltpu.roll(total, 1, 1))
            cols.append(jnp.concatenate([total.astype(BF), swapped.astype(BF)], axis=0))
        o = dot(imat_ref[...], jnp.concatenate(cols, axis=1))
        both = jnp.concatenate([o[:, :128].reshape(64, 8, 128), o[:, 128:].reshape(64, 8, 128)], axis=1)
        out_ref[:, 16 * b : 16 * b + 16, :] = both.astype(BF)
        after(b)


def gelu_grad(z):
    u = (0.3275911 * 0.7071067811865476) * jnp.abs(z)
    e = jnp.exp2((-0.5 * 1.4426950408889634) * z * z)
    t = 1.0 / (1.0 + u)
    poly = t * (0.5 * 0.254829592 + t * (-0.5 * 0.284496736 + t * (0.5 * 1.421413741 + t * (-0.5 * 1.453152027 + t * (0.5 * 1.061405429)))))
    r = (poly - (0.3989422804014327 / (0.3275911 * 0.7071067811865476)) * u) * e
    return jnp.where(z >= 0, 1.0 - r, r)


def duplicate(v):
    even = lax.broadcasted_iota(jnp.int32, v.shape, 0) & 1 == 0
    return jnp.where(even, v, pltpu.roll(v, 1, 0)), jnp.where(even, pltpu.roll(v, v.shape[0] - 1, 0), v)


def to_columns(block):
    turned = [[block[g] if a == 0 else pltpu.roll(block[g], 128 - 32 * a, 1) for g in range(2)] for a in range(4)]
    out = []
    for jj in range(2):
        rows = [turned[a][g][8 * jj : 8 * jj + 8] for a in range(4) for g in range(2)]
        out.append(jnp.concatenate(rows + rows, axis=0).T[:32, :64])
    return out


def to_block(cols):
    block = lanes_of((8, 128)) >> 5
    parts = []
    for v in cols:
        square = jnp.concatenate([jnp.concatenate([v, v], axis=1)] * 4, axis=0).T
        parts.append([])
        for g in range(2):
            out = square[8 * g : 8 * g + 8]
            for a in range(1, 4):
                out = jnp.where(block == a, square[16 * a + 8 * g : 16 * a + 8 * g + 8], out)
            parts[-1].append(out)
    return [jnp.concatenate([parts[0][g], parts[1][g]], axis=0) for g in range(2)]


def weigh(s, w_ref, jj):
    re, im = duplicate(s)
    t1 = jnp.zeros((32, 64), F32)
    t2 = jnp.zeros((32, 64), F32)
    for c in range(64):
        w = w_ref[jj, c].astype(F32)
        t1 += re[:, c : c + 1] * w
        t2 += im[:, c : c + 1] * w
    even = lax.broadcasted_iota(jnp.int32, (32, 64), 0) & 1 == 0
    return t1 + jnp.where(even, -pltpu.roll(t2, 31, 0), pltpu.roll(t2, 1, 0))


def weigh_back(d, w_ref, jj):
    even = lax.broadcasted_iota(jnp.int32, (32, 64), 0) & 1 == 0
    dsw = jnp.where(even, pltpu.roll(d, 31, 0), pltpu.roll(d, 1, 0))
    lane = lanes_of((32, 64))
    u1 = jnp.zeros((32, 64), F32)
    u2 = jnp.zeros((32, 64), F32)
    for c in range(64):
        w = w_ref[jj, c].astype(F32)
        u1 = jnp.where(lane == c, jnp.sum(w * d, axis=1, keepdims=True), u1)
        u2 = jnp.where(lane == c, jnp.sum(w * dsw, axis=1, keepdims=True), u2)
    return jnp.where(even, u1 + pltpu.roll(u1, 31, 0), pltpu.roll(u2, 1, 0) - u2)


FAR = (2, 1, 3, 0)
NEAR = (0, 1, 3, 2)


def arrived(spot, ref, recv, k):
    remote(ref, ref, recv.at[k], recv.at[k], spot.sibling).wait_recv()


def sent(spot, ref, send, k):
    remote(ref, ref, send.at[k], send.at[k], spot.sibling).wait_send()


def start_core(spot, t_ref, b0, send, recv):
    for d in FAR:
        row = spot.p[d]
        remote(t_ref.at[spot.other, :, row], b0.at[:, row], send.at[0], recv.at[d], spot.sibling).start()


def reduce_scatter(spot, t_ref, bufs, send, recv, between):
    b0, a1, b1, a2, b2 = bufs
    core, p, q, x = spot.core, spot.p[0], spot.q[0], spot.x[0]
    for d in FAR:
        row = spot.q[d]
        arrived(spot, b0.at[:, row], recv, d)
        for e in FAR:
            pt = spot.p[e]
            a1[pt, row] = (t_ref[core, pt, row].astype(F32) + b0[pt, row].astype(F32)).astype(BF)
            if e:
                remote(a1.at[pt, row], b1.at[e - 1, row], send.at[1], recv.at[4 + d], spot.first[e]).start()
    between(0)
    for d in FAR:
        row = spot.q[d]
        arrived(spot, b1.at[:, row], recv, 4 + d)
        a2[row] = (a1[p, row].astype(F32) + b1[0, row].astype(F32) + b1[1, row].astype(F32) + b1[2, row].astype(F32)).astype(BF)
        for n in FAR:
            k = 4 * d + n
            if k:
                remote(a2.at[row, spot.x[n]], b2.at[k - 1], send.at[2], recv.at[8], spot.plane[d][n]).start()
    own = a1[p, q, x].astype(F32)
    for k in range(3):
        own += b1[k, q, x].astype(F32)
    between(1)
    arrived(spot, b2, recv, 8)
    for k in range(15):
        own += b2[k].astype(F32)
    return own


def drain_scatter(spot, t_ref, bufs, send):
    sent(spot, t_ref.at[0], send, 0)
    sent(spot, bufs[2], send, 1)
    sent(spot, bufs[4], send, 2)


def all_gather(spot, g_ref, send, recv, between):
    core, p = spot.core, spot.p[0]
    mine = g_ref.at[core, p, spot.q[0], spot.x[0]]
    for d in (0, 2, 1, 3):
        for n in FAR:
            if 4 * d + n:
                remote(mine, mine, send.at[2], recv.at[8 + d], spot.plane[d][n]).start()
    between(2)
    for d in NEAR:
        row = spot.q[(4 - d) % 4]
        arrived(spot, g_ref.at[core, p, row, pl.ds(0, 4 if d else 3)], recv, 8 + d)
        mine = g_ref.at[core, p, row]
        for e in (2, 1, 3):
            remote(mine, mine, send.at[1], recv.at[4 + d], spot.first[e]).start()
    between(3)
    for d in NEAR:
        row = spot.q[(4 - d) % 4]
        arrived(spot, g_ref.at[core, pl.ds(0, 3), row], recv, 4 + d)
        theirs = g_ref.at[core, :, row]
        remote(theirs, theirs, send.at[0], recv.at[0], spot.sibling).start()
    between(4)
    arrived(spot, g_ref.at[spot.other], recv, 0)


def drain_gather(spot, g_ref, bufs, send):
    sent(spot, g_ref.at[0], send, 0)
    sent(spot, g_ref.at[0, pl.ds(0, 3)], send, 1)
    sent(spot, bufs[4], send, 2)


def main_kernel(act_hbm, cot_hbm, w_hbm, coltab_hbm, rowtab_hbm, lw_ref, bias_ref,
                loc_hbm, rf2_hbm, s_ref, d_ref, lin_out_ref,
                act, cot, w_ref, tab, dtab, syn, rowtab, rmat, imat_ref, lw_t, bias_col, xs, rf, dpre, loc, lin, t1, t2, g1, g2_ref, part,
                b0, a1, b1, a2, b2, c0, e1, c1, e2, c2,
                in_sem, out_sem, send1, recv1, send2, recv2, send3, recv3, send4, recv4, send5, recv5):
    spot = Spot()
    core, p, q, x = spot.core, spot.p[0], spot.q[0], spot.x[0]
    signal_peers(spot)
    row_dev, mode_dev = lax.axis_index("rows"), lax.axis_index("modes")
    def load_act(i):
        some = pl.ds(16 * i, 16)
        return pltpu.make_async_copy(act_hbm.at[some], act.at[some], in_sem.at[2 + i])

    load_rows = pltpu.make_async_copy(rowtab_hbm.at[row_dev], rowtab, in_sem.at[1])
    load_cols = pltpu.make_async_copy(coltab_hbm.at[mode_dev], tab, in_sem.at[0])
    load_w = pltpu.make_async_copy(w_hbm, w_ref, in_sem.at[6])
    load_cot = pltpu.make_async_copy(cot_hbm, cot, in_sem.at[7])
    load_rows.start()
    load_cols.start()
    for i in range(4):
        load_act(i).start()
    load_rows.wait()
    rmat[:, :512] = kron8(rowtab[0], False)
    rmat[:, 512:] = kron8(rowtab[1], False)
    load_cols.wait()

    def analyse(i, _):
        load_act(i).wait()
        columns(act[pl.ds(16 * i, 16)], tab[...], xs, pl.multiple_of(16 * i, 16), 16)
        return 0

    lax.fori_loop(0, 4, analyse, 0)
    load_w.start()
    load_cot.start()
    row_modes(xs, rmat, t1, spot.other)
    wait_peers()
    start_core(spot, t1, b0, send1, recv1)
    row_modes(xs, rmat, t1, core)

    def prepare(i):
        if i == 0:
            imat_ref[:, :512] = kron8(rowtab[0], True)
            imat_ref[:, 512:] = kron8(rowtab[1], True)
            lw_t[...] = lw_ref[...].astype(F32).T.astype(BF)
            bias_col[...] = jnp.broadcast_to(bias_ref[...], (128, 64)).T
        if i == 1:
            lane = lanes_of((512, 256)) % 128
            scaled = tab[...].astype(F32) * jnp.where(lane < 2, 2.0**-22, 2.0**-21)
            dtab[...] = scaled.astype(BF)
            syn[...] = scaled[:, :128].T.astype(BF)

    first, second = (b0, a1, b1, a2, b2), (c0, e1, c1, e2, c2)
    own = reduce_scatter(spot, t1, first, send1, recv1, prepare)
    load_w.wait()
    s = to_columns(own.astype(BF).astype(F32))
    mixed = []
    for jj in range(2):
        s_ref[jj] = s[jj]
        mixed.append(weigh(s[jj], w_ref, jj))
    for g, v in enumerate(to_block(mixed)):
        g1[core, p, q, x, g] = v.astype(BF)
    all_gather(spot, g1, send2, recv2, lambda i: drain_scatter(spot, t1, first, send1) if i == 3 else None)

    inverse(g1, imat_ref, rf)
    load_cot.wait()

    def rows(i, _):
        bias = jnp.concatenate([bias_col[...]] * 4, axis=1)
        for n in range(2):
            first = pl.multiple_of(16 * i + 8 * n, 8)
            ds = []
            for k in range(8):
                h = first + k
                lhs = jnp.concatenate([rf[h], lw_t[...]], axis=1)
                rhs = jnp.concatenate([syn[...], act[h]], axis=0)
                d = (cot[h].astype(F32) * gelu_grad(dot(lhs, rhs) + bias)).astype(BF)
                dpre[h] = d
                ds.append(d)
            columns(jnp.concatenate(ds, axis=0).reshape(8, 64, 512), dtab[...], xs, first, 8)
        return 0

    lax.fori_loop(0, 4, rows, 0)
    row_modes(xs, rmat, t2, spot.other)
    start_core(spot, t2, c0, send3, recv3)
    row_modes(xs, rmat, t2, core)

    steps = (
        (p, spot.first[1:]),
        (q, [spot.plane[d][0] for d in (1, 2, 3)]),
        (x, [spot.plane[0][d] for d in (1, 2, 3)]),
    )

    def swap_lin():
        part[0, core] = lin[...]
        drain_gather(spot, g1, first, send2)
        remote(part.at[0, core], part.at[0, core], send5.at[0], recv5.at[0], spot.sibling).start()

    def join_lin(i):
        if i == 0:
            sent(spot, part.at[0, 0], send5, 0)
            arrived(spot, part.at[0, 0], recv5, 0)
            return part[0, 0] + part[0, 1]
        sent(spot, part.at[i, pl.ds(0, 3)], send5, i)
        arrived(spot, part.at[i, pl.ds(0, 3)], recv5, i)
        return part[i, 0] + part[i, 1] + part[i, 2] + part[i, 3]

    def pass_lin(i):
        me, peers = steps[i]
        part[i + 1, me] = join_lin(i)
        mine = part.at[i + 1, me]
        for peer in peers:
            remote(mine, mine, send5.at[i + 1], recv5.at[i + 1], peer).start()

    def products(i, _):
        left = jnp.concatenate([act[4 * i + k] for k in range(4)], axis=1)
        right = jnp.concatenate([dpre[4 * i + k] for k in range(4)], axis=1)
        left = jnp.concatenate([left, jnp.ones((16, 2048), BF)], axis=0)
        lin[...] += lax.dot_general(left, right, (((1,), (1,)), ((), ())), preferred_element_type=F32)
        return 0

    def local_products(i):
        if i == 0:
            lin[...] = jnp.zeros_like(lin)
            lax.fori_loop(0, 8, products, 0)
        if i == 1:
            lax.fori_loop(8, 16, products, 0)
            swap_lin()
        if i >= 2:
            pass_lin(i - 2)
        if i == 3:
            drain_scatter(spot, t2, second, send3)
        if i in (2, 3):
            lax.fori_loop(2 * i - 4, 2 * i - 2, pointwise, 0)

    def pointwise(i, _):
        def some_rows(n, _):
            for k in range(8):
                h = 16 * i + 8 * n + k
                loc[h] = dot(lw_ref[...], dpre[h]).astype(BF)
            return 0

        lax.fori_loop(0, 2, some_rows, 0)
        some = pl.ds(16 * i, 16)
        pltpu.make_async_copy(loc.at[some], loc_hbm.at[some], out_sem.at[i]).start()
        return 0

    own = reduce_scatter(spot, t2, second, send3, recv3, local_products)
    d = to_columns(own.astype(BF).astype(F32))
    back = []
    for jj in range(2):
        d_ref[jj] = d[jj]
        back.append(weigh_back(d[jj], w_ref, jj))
    for g, v in enumerate(to_block(back)):
        g2_ref[core, p, q, x, g] = v.astype(BF)
    all_gather(spot, g2_ref, send4, recv4, local_products)

    def ship(b):
        return pltpu.make_async_copy(rf.at[:, pl.ds(16 * b, 16)], rf2_hbm.at[:, pl.ds(16 * b, 16)], out_sem.at[4 + b])

    inverse(g2_ref, imat_ref, rf, lambda b: ship(b).start())
    lin_out_ref[...] = join_lin(3) * (1.0 / 2048)
    drain_gather(spot, g2_ref, second, send4)
    for i in range(4):
        some = pl.ds(16 * i, 16)
        pltpu.make_async_copy(loc.at[some], loc_hbm.at[some], out_sem.at[i]).wait()
        ship(i).wait()


def last_kernel(rf_hbm, loc_hbm, coltab_hbm, s_ref, d_ref, lin_ref,
                gin_hbm, gspec_hbm, glin_ref, gbias_ref, rf, loc, tab, ana, gin, gspec, in_sem, out_sem):
    load = pltpu.make_async_copy(coltab_hbm.at[lax.axis_index("modes")], tab, in_sem.at[8])
    load.start()

    def copy(n, i):
        some = pl.ds(16 * i, 16)
        if n == 2:
            return pltpu.make_async_copy(gin.at[some], gin_hbm.at[some], out_sem.at[i])
        src, dst = ((rf_hbm, rf), (loc_hbm, loc))[n]
        return pltpu.make_async_copy(src.at[some], dst.at[some], in_sem.at[2 * i + n])

    for i in range(4):
        copy(0, i).start()
        copy(1, i).start()
    glin_ref[...] = lin_ref[:64]
    gbias_ref[...] = lin_ref[64:65]
    even = lax.broadcasted_iota(jnp.int32, (32, 64), 0) & 1 == 0
    def products(jj, _):
        re, im = duplicate(s_ref[jj])
        d = d_ref[jj]
        dsw = jnp.where(even, pltpu.roll(d, 31, 0), -pltpu.roll(d, 1, 0))
        for c in range(64):
            gspec[jj, c] = re[:, c : c + 1] * d + im[:, c : c + 1] * dsw
        pltpu.make_async_copy(gspec.at[jj], gspec_hbm.at[jj], out_sem.at[4 + jj]).start()
        return 0

    lax.fori_loop(0, 2, products, 0)
    load.wait()
    ana[...] = tab[:, :128].astype(F32).T.astype(BF)

    def row(i, _):
        copy(0, i).wait()
        copy(1, i).wait()
        for k in range(4):
            some = pl.ds(16 * i + 4 * k, 4)
            part = dot(rf[some].reshape(256, 128), ana[...]).reshape(4, 64, 512)
            gin[some] = (part + loc[some].astype(F32)).astype(BF)
        copy(2, i).start()
        return 0

    lax.fori_loop(0, 4, row, 0)
    for jj in range(2):
        pltpu.make_async_copy(gspec.at[jj], gspec_hbm.at[jj], out_sem.at[4 + jj]).wait()
    for i in range(4):
        copy(2, i).wait()


SPEC = (2, 4, 4, 4, 2, 16, 128)
ANY = pl.BlockSpec(memory_space=pl.ANY)


def body(activations, cotangent, spectral_weight, linear_weight, bias):
    w = spectral_weight.transpose(0, 1, 3, 2)
    coltab, rowtab = jnp.asarray(column_constants()), jnp.asarray(row_constants())
    dma = pltpu.SemaphoreType.DMA
    quarter = (4, 4, 4, 2, 16, 128)
    buffers = [pltpu.VMEM(quarter, BF), pltpu.VMEM(quarter, BF), pltpu.VMEM((3, 4, 4, 2, 16, 128), BF),
               pltpu.VMEM((4, 4, 2, 16, 128), BF), pltpu.VMEM((15, 2, 16, 128), BF)]
    shape = jax.ShapeDtypeStruct
    loc, rf, s, d, lin = pl.pallas_call(
        main_kernel,
        out_shape=[shape((64, 64, 512), BF), shape((64, 64, 128), BF), shape((2, 32, 64), F32), shape((2, 32, 64), F32),
                   shape((80, 64), F32)],
        in_specs=[ANY] * 5 + [VMEM] * 2,
        out_specs=[ANY] * 2 + [VMEM] * 3,
        scratch_shapes=[
            pltpu.VMEM((64, 64, 512), BF), pltpu.VMEM((64, 64, 512), BF), pltpu.VMEM((2, 64, 32, 64), BF),
            pltpu.VMEM((512, 256), BF), pltpu.VMEM((512, 256), BF), pltpu.VMEM((128, 512), BF), pltpu.VMEM((2, 64, 64), BF),
            pltpu.VMEM((512, 1024), BF), pltpu.VMEM((512, 1024), BF), pltpu.VMEM((64, 64), BF), pltpu.VMEM((64, 128), F32),
            pltpu.VMEM((2, 1024, 512), BF),
            pltpu.VMEM((64, 64, 128), BF), pltpu.VMEM((64, 64, 512), BF), pltpu.VMEM((64, 64, 512), BF), pltpu.VMEM((80, 64), F32),
            pltpu.VMEM(SPEC, BF), pltpu.VMEM(SPEC, BF), pltpu.VMEM(SPEC, BF), pltpu.VMEM(SPEC, BF), pltpu.VMEM((4, 4, 80, 64), F32),
        ] + buffers + buffers + [dma((8,)), dma((8,))] + [dma((3,)), dma((12,))] * 4 + [dma((4,))] * 2,
        compiler_params=pltpu.CompilerParams(vmem_limit_bytes=LIMIT, collective_id=0, has_side_effects=True),
        name="main",
    )(activations, cotangent, w, coltab, rowtab, linear_weight, bias.reshape(1, 64))
    gin, gspec, glin, gbias = pl.pallas_call(
        last_kernel,
        out_shape=[shape((64, 64, 512), BF), shape((2, 64, 32, 64), F32), shape((64, 64), F32), shape((1, 64), F32)],
        in_specs=[ANY] * 3 + [VMEM] * 3,
        out_specs=[ANY] * 2 + [VMEM] * 2,
        scratch_shapes=[pltpu.VMEM((64, 64, 128), BF), pltpu.VMEM((64, 64, 512), BF), pltpu.VMEM((512, 256), BF),
                        pltpu.VMEM((128, 512), BF), pltpu.VMEM((64, 64, 512), BF), pltpu.VMEM((2, 64, 32, 64), F32),
                        dma((9,)), dma((6,))],
        compiler_params=pltpu.CompilerParams(vmem_limit_bytes=LIMIT),
        name="last",
    )(rf, loc, coltab, s, d, lin)
    return gin, gspec.transpose(0, 1, 3, 2), glin, gbias.reshape(64)


def solution(mesh):
    return jax.shard_map(
        body,
        mesh=mesh,
        in_specs=(
            P("rows", None, "modes"),
            P("rows", None, "modes"),
            P("rows", None, None, "modes"),
            P(),
            P(),
        ),
        out_specs=(P("rows", None, "modes"), P("rows", None, None, "modes"), P(), P()),
        check_vma=False,
    )
```

```python
import math

import jax
import jax.numpy as jnp
import numpy as np
from jax import lax
from jax.experimental import pallas as pl
from jax.experimental.pallas import tpu as pltpu
from jax.sharding import PartitionSpec as P

MESH = pl.DeviceIdType.MESH
BF = jnp.bfloat16
F32 = jnp.float32
VMEM = pl.BlockSpec(memory_space=pltpu.VMEM)


def dot(a, b):
    return jnp.dot(a, b, preferred_element_type=F32)


def lanes_of(shape):
    return lax.broadcasted_iota(jnp.int32, shape, len(shape) - 1)


def column_constants():
    k = np.arange(128) // 2
    w = np.arange(2048)
    ang = ((w[:, None] * k[None, :]) % 2048) * (2.0 * math.pi / 2048)
    even = (np.arange(128) % 2 == 0)[None, :]
    ana = np.where(even, np.cos(ang), -np.sin(ang))
    swap = np.where(even, -np.sin(ang), -np.cos(ang))
    return np.concatenate([ana, swap], axis=1).reshape(4, 512, 256).astype(np.float32).astype(jnp.bfloat16)


def row_constants():
    slot = np.arange(64)
    core, z, x, jj = slot // 32, (slot // 8) % 4, (slot // 2) % 4, slot % 2
    mode = x * 16 + z * 4 + core * 2 + jj
    freq = np.where(mode < 32, mode, mode - 64)
    rows = np.arange(2048).reshape(32, 64)
    ang = ((freq[None, :, None] * rows[:, None, :]) % 2048) * (2.0 * math.pi / 2048)
    return np.stack([np.cos(ang), np.sin(ang)], axis=1).astype(np.float32).astype(jnp.bfloat16)


def kron8(table, flip):
    up = (lax.broadcasted_iota(jnp.int32, (512, 64), 0) >> 3 == lax.broadcasted_iota(jnp.int32, (512, 64), 1)).astype(BF)
    wide = (lax.broadcasted_iota(jnp.int32, (64, 512), 1) >> 3 == lax.broadcasted_iota(jnp.int32, (64, 512), 0)).astype(BF)
    keep = (lax.broadcasted_iota(jnp.int32, (512, 512), 0) ^ lax.broadcasted_iota(jnp.int32, (512, 512), 1)) & 7 == 0
    left = lax.dot_general(up, table, (((1,), (1 if flip else 0,)), ((), ())), preferred_element_type=F32).astype(BF)
    return jnp.where(keep, dot(left, wide), 0.0).astype(BF)


class Spot:
    def __init__(self):
        r, y = lax.axis_index("rows"), lax.axis_index("modes")
        x, z, core = lax.div(r, 8), lax.rem(lax.div(r, 2), 4), lax.rem(r, 2)
        p, q = y * (1 - core) + z * core, z * (1 - core) + y * core
        self.core, self.other = core, 1 - core
        self.p = [lax.rem(p + d, 4) for d in range(4)]
        self.q = [lax.rem(q + d, 4) for d in range(4)]
        self.x = [lax.rem(x + d, 4) for d in range(4)]
        self.sibling = (r + 1 - 2 * core, y)
        self.first = [self.at(v, q, x) for v in self.p]
        self.plane = [[self.at(p, v, u) for u in self.x] for v in self.q]

    def at(self, p, q, x):
        y, z = p * self.other + q * self.core, q * self.other + p * self.core
        return ((x * 4 + z) * 2 + self.core, y)


def signal_peers(spot):
    barrier = pltpu.get_barrier_semaphore()
    peers = [spot.sibling] + spot.first[1:] + [spot.plane[k // 4][k % 4] for k in range(1, 16)]
    for peer in peers:
        pl.semaphore_signal(barrier, inc=1, device_id=peer, device_id_type=MESH)


def wait_peers():
    pl.semaphore_wait(pltpu.get_barrier_semaphore(), 19)


def remote(src, dst, send, recv, target):
    return pltpu.make_async_remote_copy(src_ref=src, dst_ref=dst, send_sem=send, recv_sem=recv, device_id=target, device_id_type=MESH)


def columns(block, tab, xs_ref, h0, count):
    prod = dot(block.reshape(count * 64, 512), tab).reshape(count, 8, 8, 256)
    for a in range(4):
        for g in range(2):
            v = prod[:, 2 * a + g].reshape(count * 8, 256).astype(BF)
            xs_ref[g, pl.ds(h0 * 8, count * 8), 128 * a : 128 * a + 128] = v[:, :128]
            xs_ref[g, pl.ds(512 + h0 * 8, count * 8), 128 * a : 128 * a + 128] = v[:, 128:]


def row_modes(xs_ref, rmat_ref, t_ref, owner):
    block = lanes_of((256, 128)) >> 5
    for g in range(2):
        o = dot(rmat_ref[pl.ds(pl.multiple_of(owner * 256, 256), 256), :], xs_ref[g])
        for m in range(4):
            total = None
            for a in range(4):
                v = o[:, 128 * a : 128 * a + 128]
                shift = (32 * (a - m)) % 128
                if shift:
                    v = pltpu.roll(v, shift, 1)
                total = v if total is None else jnp.where(block == a, v, total)
            total = total.astype(BF).reshape(4, 4, 16, 128)
            for z in range(4):
                t_ref[owner, m * (1 - owner) + z * owner, z * (1 - owner) + m * owner, :, g] = total[z]


def inverse(g_ref, imat_ref, out_ref, after=lambda b: None):
    even = lanes_of((512, 128)) & 1 == 0
    block = lanes_of((512, 128)) >> 5
    for b in range(4):
        cols = []
        for g in range(2):
            total = None
            for m in range(4):
                parts = [g_ref[0, m, :, :, g].reshape(256, 128)]
                parts += [g_ref[1, z, m, :, g].reshape(64, 128) for z in range(4)]
                v = jnp.concatenate(parts, axis=0).astype(F32)
                shift = (32 * (m - b)) % 128
                if shift:
                    v = pltpu.roll(v, shift, 1)
                total = v if total is None else jnp.where(block == m, v, total)
            swapped = jnp.where(even, -pltpu.roll(total, 127, 1), pltpu.roll(total, 1, 1))
            cols.append(jnp.concatenate([total.astype(BF), swapped.astype(BF)], axis=0))
        o = dot(imat_ref[...], jnp.concatenate(cols, axis=1))
        both = jnp.concatenate([o[:, :128].reshape(64, 8, 128), o[:, 128:].reshape(64, 8, 128)], axis=1)
        out_ref[:, 16 * b : 16 * b + 16, :] = both.astype(BF)
        after(b)


def gelu_grad(z):
    u = (0.3275911 * 0.7071067811865476) * jnp.abs(z)
    e = jnp.exp2((-0.5 * 1.4426950408889634) * z * z)
    t = 1.0 / (1.0 + u)
    poly = t * (0.5 * 0.254829592 + t * (-0.5 * 0.284496736 + t * (0.5 * 1.421413741 + t * (-0.5 * 1.453152027 + t * (0.5 * 1.061405429)))))
    r = (poly - (0.3989422804014327 / (0.3275911 * 0.7071067811865476)) * u) * e
    return jnp.where(z >= 0, 1.0 - r, r)


def duplicate(v):
    even = lax.broadcasted_iota(jnp.int32, v.shape, 0) & 1 == 0
    return jnp.where(even, v, pltpu.roll(v, 1, 0)), jnp.where(even, pltpu.roll(v, v.shape[0] - 1, 0), v)


def to_columns(block):
    turned = [[block[g] if a == 0 else pltpu.roll(block[g], 128 - 32 * a, 1) for g in range(2)] for a in range(4)]
    out = []
    for jj in range(2):
        rows = [turned[a][g][8 * jj : 8 * jj + 8] for a in range(4) for g in range(2)]
        out.append(jnp.concatenate(rows + rows, axis=0).T[:32, :64])
    return out


def to_block(cols):
    block = lanes_of((8, 128)) >> 5
    parts = []
    for v in cols:
        square = jnp.concatenate([jnp.concatenate([v, v], axis=1)] * 4, axis=0).T
        parts.append([])
        for g in range(2):
            out = square[8 * g : 8 * g + 8]
            for a in range(1, 4):
                out = jnp.where(block == a, square[16 * a + 8 * g : 16 * a + 8 * g + 8], out)
            parts[-1].append(out)
    return [jnp.concatenate([parts[0][g], parts[1][g]], axis=0) for g in range(2)]


def weigh(s, w_ref, jj):
    re, im = duplicate(s)
    t1 = jnp.zeros((32, 64), F32)
    t2 = jnp.zeros((32, 64), F32)
    for c in range(64):
        w = w_ref[jj, c].astype(F32)
        t1 += re[:, c : c + 1] * w
        t2 += im[:, c : c + 1] * w
    even = lax.broadcasted_iota(jnp.int32, (32, 64), 0) & 1 == 0
    return t1 + jnp.where(even, -pltpu.roll(t2, 31, 0), pltpu.roll(t2, 1, 0))


def weigh_back(d, w_ref, jj):
    even = lax.broadcasted_iota(jnp.int32, (32, 64), 0) & 1 == 0
    dsw = jnp.where(even, pltpu.roll(d, 31, 0), pltpu.roll(d, 1, 0))
    lane = lanes_of((32, 64))
    u1 = jnp.zeros((32, 64), F32)
    u2 = jnp.zeros((32, 64), F32)
    for c in range(64):
        w = w_ref[jj, c].astype(F32)
        u1 = jnp.where(lane == c, jnp.sum(w * d, axis=1, keepdims=True), u1)
        u2 = jnp.where(lane == c, jnp.sum(w * dsw, axis=1, keepdims=True), u2)
    return jnp.where(even, u1 + pltpu.roll(u1, 31, 0), pltpu.roll(u2, 1, 0) - u2)


FAR = (2, 1, 3, 0)
NEAR = (0, 1, 3, 2)


def arrived(spot, ref, recv, k):
    remote(ref, ref, recv.at[k], recv.at[k], spot.sibling).wait_recv()


def sent(spot, ref, send, k):
    remote(ref, ref, send.at[k], send.at[k], spot.sibling).wait_send()


def start_core(spot, t_ref, b0, send, recv):
    for d in FAR:
        row = spot.p[d]
        remote(t_ref.at[spot.other, :, row], b0.at[:, row], send.at[0], recv.at[d], spot.sibling).start()


def reduce_scatter(spot, t_ref, bufs, send, recv, between):
    b0, a1, b1, a2, b2 = bufs
    core, p, q, x = spot.core, spot.p[0], spot.q[0], spot.x[0]
    for d in FAR:
        row = spot.q[d]
        arrived(spot, b0.at[:, row], recv, d)
        for e in FAR:
            pt = spot.p[e]
            a1[pt, row] = (t_ref[core, pt, row].astype(F32) + b0[pt, row].astype(F32)).astype(BF)
            if e:
                remote(a1.at[pt, row], b1.at[e - 1, row], send.at[1], recv.at[4 + d], spot.first[e]).start()
    between(0)
    for d in FAR:
        row = spot.q[d]
        arrived(spot, b1.at[:, row], recv, 4 + d)
        a2[row] = (a1[p, row].astype(F32) + b1[0, row].astype(F32) + b1[1, row].astype(F32) + b1[2, row].astype(F32)).astype(BF)
        for n in FAR:
            k = 4 * d + n
            if k:
                remote(a2.at[row, spot.x[n]], b2.at[k - 1], send.at[2], recv.at[8], spot.plane[d][n]).start()
    own = a1[p, q, x].astype(F32)
    for k in range(3):
        own += b1[k, q, x].astype(F32)
    between(1)
    arrived(spot, b2, recv, 8)
    for k in range(15):
        own += b2[k].astype(F32)
    return own


def drain_scatter(spot, t_ref, bufs, send):
    sent(spot, t_ref.at[0], send, 0)
    sent(spot, bufs[2], send, 1)
    sent(spot, bufs[4], send, 2)


def all_gather(spot, g_ref, send, recv, between):
    core, p = spot.core, spot.p[0]
    mine = g_ref.at[core, p, spot.q[0], spot.x[0]]
    for d in (0, 2, 1, 3):
        for n in FAR:
            if 4 * d + n:
                remote(mine, mine, send.at[2], recv.at[8 + d], spot.plane[d][n]).start()
    between(2)
    for d in NEAR:
        row = spot.q[(4 - d) % 4]
        arrived(spot, g_ref.at[core, p, row, pl.ds(0, 4 if d else 3)], recv, 8 + d)
        mine = g_ref.at[core, p, row]
        for e in (2, 1, 3):
            remote(mine, mine, send.at[1], recv.at[4 + d], spot.first[e]).start()
    between(3)
    for d in NEAR:
        row = spot.q[(4 - d) % 4]
        arrived(spot, g_ref.at[core, pl.ds(0, 3), row], recv, 4 + d)
        theirs = g_ref.at[core, :, row]
        remote(theirs, theirs, send.at[0], recv.at[0], spot.sibling).start()
    between(4)
    arrived(spot, g_ref.at[spot.other], recv, 0)


def drain_gather(spot, g_ref, bufs, send):
    sent(spot, g_ref.at[0], send, 0)
    sent(spot, g_ref.at[0, pl.ds(0, 3)], send, 1)
    sent(spot, bufs[4], send, 2)


def main_kernel(act_hbm, cot_hbm, w_hbm, coltab_hbm, rowtab_hbm, lw_ref, bias_ref,
                loc_hbm, rf2_hbm, s_ref, d_ref, lin_out_ref,
                act, cot, w_ref, tab, dtab, syn, rowtab, rmat, imat_ref, lw_t, bias_col, xs, rf, dpre, loc, lin, t1, t2, g1, g2_ref, part,
                b0, a1, b1, a2, b2, c0, e1, c1, e2, c2,
                in_sem, out_sem, send1, recv1, send2, recv2, send3, recv3, send4, recv4, send5, recv5):
    spot = Spot()
    core, p, q, x = spot.core, spot.p[0], spot.q[0], spot.x[0]
    signal_peers(spot)
    row_dev, mode_dev = lax.axis_index("rows"), lax.axis_index("modes")
    def load_act(i):
        some = pl.ds(16 * i, 16)
        return pltpu.make_async_copy(act_hbm.at[some], act.at[some], in_sem.at[2 + i])

    load_rows = pltpu.make_async_copy(rowtab_hbm.at[row_dev], rowtab, in_sem.at[1])
    load_cols = pltpu.make_async_copy(coltab_hbm.at[mode_dev], tab, in_sem.at[0])
    load_w = pltpu.make_async_copy(w_hbm, w_ref, in_sem.at[6])
    load_cot = pltpu.make_async_copy(cot_hbm, cot, in_sem.at[7])
    load_rows.start()
    load_cols.start()
    for i in range(4):
        load_act(i).start()
    load_rows.wait()
    rmat[:, :512] = kron8(rowtab[0], False)
    rmat[:, 512:] = kron8(rowtab[1], False)
    load_cols.wait()

    def analyse(i, _):
        load_act(i).wait()
        columns(act[pl.ds(16 * i, 16)], tab[...], xs, pl.multiple_of(16 * i, 16), 16)
        return 0

    lax.fori_loop(0, 4, analyse, 0)
    load_w.start()
    load_cot.start()
    row_modes(xs, rmat, t1, spot.other)
    wait_peers()
    start_core(spot, t1, b0, send1, recv1)
    row_modes(xs, rmat, t1, core)

    def prepare(i):
        if i == 0:
            imat_ref[:, :512] = kron8(rowtab[0], True)
            imat_ref[:, 512:] = kron8(rowtab[1], True)
            lw_t[...] = lw_ref[...].astype(F32).T.astype(BF)
            bias_col[...] = jnp.broadcast_to(bias_ref[...], (128, 64)).T
        if i == 1:
            lane = lanes_of((512, 256)) % 128
            scaled = tab[...].astype(F32) * jnp.where(lane < 2, 2.0**-22, 2.0**-21)
            dtab[...] = scaled.astype(BF)
            syn[...] = scaled[:, :128].T.astype(BF)

    first, second = (b0, a1, b1, a2, b2), (c0, e1, c1, e2, c2)
    own = reduce_scatter(spot, t1, first, send1, recv1, prepare)
    load_w.wait()
    s = to_columns(own.astype(BF).astype(F32))
    mixed = []
    for jj in range(2):
        s_ref[jj] = s[jj]
        mixed.append(weigh(s[jj], w_ref, jj))
    for g, v in enumerate(to_block(mixed)):
        g1[core, p, q, x, g] = v.astype(BF)
    all_gather(spot, g1, send2, recv2, lambda i: drain_scatter(spot, t1, first, send1) if i == 3 else None)

    inverse(g1, imat_ref, rf)
    load_cot.wait()

    def rows(i, _):
        bias = jnp.concatenate([bias_col[...]] * 4, axis=1)
        for n in range(2):
            first = pl.multiple_of(16 * i + 8 * n, 8)
            ds = []
            for k in range(8):
                h = first + k
                lhs = jnp.concatenate([rf[h], lw_t[...]], axis=1)
                rhs = jnp.concatenate([syn[...], act[h]], axis=0)
                d = (cot[h].astype(F32) * gelu_grad(dot(lhs, rhs) + bias)).astype(BF)
                dpre[h] = d
                ds.append(d)
            columns(jnp.concatenate(ds, axis=0).reshape(8, 64, 512), dtab[...], xs, first, 8)
        return 0

    lax.fori_loop(0, 4, rows, 0)
    row_modes(xs, rmat, t2, spot.other)
    start_core(spot, t2, c0, send3, recv3)
    row_modes(xs, rmat, t2, core)

    steps = (
        (p, spot.first[1:]),
        (q, [spot.plane[d][0] for d in (1, 2, 3)]),
        (x, [spot.plane[0][d] for d in (1, 2, 3)]),
    )

    def swap_lin():
        part[0, core] = lin[...]
        drain_gather(spot, g1, first, send2)
        remote(part.at[0, core], part.at[0, core], send5.at[0], recv5.at[0], spot.sibling).start()

    def join_lin(i):
        if i == 0:
            sent(spot, part.at[0, 0], send5, 0)
            arrived(spot, part.at[0, 0], recv5, 0)
            return part[0, 0] + part[0, 1]
        sent(spot, part.at[i, pl.ds(0, 3)], send5, i)
        arrived(spot, part.at[i, pl.ds(0, 3)], recv5, i)
        return part[i, 0] + part[i, 1] + part[i, 2] + part[i, 3]

    def pass_lin(i):
        me, peers = steps[i]
        part[i + 1, me] = join_lin(i)
        mine = part.at[i + 1, me]
        for peer in peers:
            remote(mine, mine, send5.at[i + 1], recv5.at[i + 1], peer).start()

    def products(i, _):
        left = jnp.concatenate([act[4 * i + k] for k in range(4)], axis=1)
        right = jnp.concatenate([dpre[4 * i + k] for k in range(4)], axis=1)
        left = jnp.concatenate([left, jnp.ones((16, 2048), BF)], axis=0)
        lin[...] += lax.dot_general(left, right, (((1,), (1,)), ((), ())), preferred_element_type=F32)
        return 0

    def local_products(i):
        if i == 0:
            lin[...] = jnp.zeros_like(lin)
            lax.fori_loop(0, 8, products, 0)
        if i == 1:
            lax.fori_loop(8, 16, products, 0)
            swap_lin()
        if i >= 2:
            pass_lin(i - 2)
        if i == 3:
            drain_scatter(spot, t2, second, send3)
        if i in (2, 3):
            lax.fori_loop(2 * i - 4, 2 * i - 2, pointwise, 0)

    def pointwise(i, _):
        def some_rows(n, _):
            for k in range(8):
                h = 16 * i + 8 * n + k
                loc[h] = dot(lw_ref[...], dpre[h]).astype(BF)
            return 0

        lax.fori_loop(0, 2, some_rows, 0)
        some = pl.ds(16 * i, 16)
        pltpu.make_async_copy(loc.at[some], loc_hbm.at[some], out_sem.at[i]).start()
        return 0

    own = reduce_scatter(spot, t2, second, send3, recv3, local_products)
    d = to_columns(own.astype(BF).astype(F32))
    back = []
    for jj in range(2):
        d_ref[jj] = d[jj]
        back.append(weigh_back(d[jj], w_ref, jj))
    for g, v in enumerate(to_block(back)):
        g2_ref[core, p, q, x, g] = v.astype(BF)
    all_gather(spot, g2_ref, send4, recv4, local_products)

    def ship(b):
        return pltpu.make_async_copy(rf.at[:, pl.ds(16 * b, 16)], rf2_hbm.at[:, pl.ds(16 * b, 16)], out_sem.at[4 + b])

    inverse(g2_ref, imat_ref, rf, lambda b: ship(b).start())
    lin_out_ref[...] = join_lin(3) * (1.0 / 2048)
    drain_gather(spot, g2_ref, second, send4)
    for i in range(4):
        some = pl.ds(16 * i, 16)
        pltpu.make_async_copy(loc.at[some], loc_hbm.at[some], out_sem.at[i]).wait()
        ship(i).wait()


def last_kernel(rf_hbm, loc_hbm, coltab_hbm, s_ref, d_ref, lin_ref,
                gin_hbm, gspec_hbm, glin_ref, gbias_ref, rf, loc, tab, ana, gin, gspec, in_sem, out_sem):
    load = pltpu.make_async_copy(coltab_hbm.at[lax.axis_index("modes")], tab, in_sem.at[8])
    load.start()

    def copy(n, i):
        some = pl.ds(16 * i, 16)
        if n == 2:
            return pltpu.make_async_copy(gin.at[some], gin_hbm.at[some], out_sem.at[i])
        src, dst = ((rf_hbm, rf), (loc_hbm, loc))[n]
        return pltpu.make_async_copy(src.at[some], dst.at[some], in_sem.at[2 * i + n])

    for i in range(4):
        copy(0, i).start()
        copy(1, i).start()
    glin_ref[...] = lin_ref[:64]
    gbias_ref[...] = lin_ref[64:65]
    even = lax.broadcasted_iota(jnp.int32, (32, 64), 0) & 1 == 0
    def products(jj, _):
        re, im = duplicate(s_ref[jj])
        d = d_ref[jj]
        dsw = jnp.where(even, pltpu.roll(d, 31, 0), -pltpu.roll(d, 1, 0))
        for c in range(64):
            gspec[jj, c] = re[:, c : c + 1] * d + im[:, c : c + 1] * dsw
        pltpu.make_async_copy(gspec.at[jj], gspec_hbm.at[jj], out_sem.at[4 + jj]).start()
        return 0

    lax.fori_loop(0, 2, products, 0)
    load.wait()
    ana[...] = tab[:, :128].astype(F32).T.astype(BF)

    def row(i, _):
        copy(0, i).wait()
        copy(1, i).wait()
        for k in range(4):
            some = pl.ds(16 * i + 4 * k, 4)
            part = dot(rf[some].reshape(256, 128), ana[...]).reshape(4, 64, 512)
            gin[some] = (part + loc[some].astype(F32)).astype(BF)
        copy(2, i).start()
        return 0

    lax.fori_loop(0, 4, row, 0)
    for jj in range(2):
        pltpu.make_async_copy(gspec.at[jj], gspec_hbm.at[jj], out_sem.at[4 + jj]).wait()
    for i in range(4):
        copy(2, i).wait()


SPEC = (2, 4, 4, 4, 2, 16, 128)
ANY = pl.BlockSpec(memory_space=pl.ANY)
HBM = pl.BlockSpec(memory_space=pltpu.HBM)


def body(activations, cotangent, spectral_weight, linear_weight, bias):
    w = spectral_weight.transpose(0, 1, 3, 2)
    coltab, rowtab = jnp.asarray(column_constants()), jnp.asarray(row_constants())
    dma = pltpu.SemaphoreType.DMA
    quarter = (4, 4, 4, 2, 16, 128)
    buffers = [pltpu.VMEM(quarter, BF), pltpu.VMEM(quarter, BF), pltpu.VMEM((3, 4, 4, 2, 16, 128), BF),
               pltpu.VMEM((4, 4, 2, 16, 128), BF), pltpu.VMEM((15, 2, 16, 128), BF)]
    shape = jax.ShapeDtypeStruct
    loc, rf, s, d, lin = pl.pallas_call(
        main_kernel,
        out_shape=[shape((64, 64, 512), BF), shape((64, 64, 128), BF), shape((2, 32, 64), F32), shape((2, 32, 64), F32),
                   shape((80, 64), F32)],
        in_specs=[HBM] * 5 + [VMEM] * 2,
        out_specs=[ANY] * 2 + [VMEM] * 3,
        scratch_shapes=[
            pltpu.VMEM((64, 64, 512), BF), pltpu.VMEM((64, 64, 512), BF), pltpu.VMEM((2, 64, 32, 64), BF),
            pltpu.VMEM((512, 256), BF), pltpu.VMEM((512, 256), BF), pltpu.VMEM((128, 512), BF), pltpu.VMEM((2, 64, 64), BF),
            pltpu.VMEM((512, 1024), BF), pltpu.VMEM((512, 1024), BF), pltpu.VMEM((64, 64), BF), pltpu.VMEM((64, 128), F32),
            pltpu.VMEM((2, 1024, 512), BF),
            pltpu.VMEM((64, 64, 128), BF), pltpu.VMEM((64, 64, 512), BF), pltpu.VMEM((64, 64, 512), BF), pltpu.VMEM((80, 64), F32),
            pltpu.VMEM(SPEC, BF), pltpu.VMEM(SPEC, BF), pltpu.VMEM(SPEC, BF), pltpu.VMEM(SPEC, BF), pltpu.VMEM((4, 4, 80, 64), F32),
        ] + buffers + buffers + [dma((8,)), dma((8,))] + [dma((3,)), dma((12,))] * 4 + [dma((4,))] * 2,
        compiler_params=pltpu.CompilerParams(vmem_limit_bytes=44 * 1024 * 1024, collective_id=0, has_side_effects=True),
        name="main",
    )(activations, cotangent, w, coltab, rowtab, linear_weight, bias.reshape(1, 64))
    gin, gspec, glin, gbias = pl.pallas_call(
        last_kernel,
        out_shape=[shape((64, 64, 512), BF), shape((2, 64, 32, 64), F32), shape((64, 64), F32), shape((1, 64), F32)],
        in_specs=[ANY] * 2 + [HBM] + [VMEM] * 3,
        out_specs=[ANY] * 2 + [VMEM] * 2,
        scratch_shapes=[pltpu.VMEM((64, 64, 128), BF), pltpu.VMEM((64, 64, 512), BF), pltpu.VMEM((512, 256), BF),
                        pltpu.VMEM((128, 512), BF), pltpu.VMEM((64, 64, 512), BF), pltpu.VMEM((2, 64, 32, 64), F32),
                        dma((9,)), dma((6,))],
        compiler_params=pltpu.CompilerParams(vmem_limit_bytes=24 * 1024 * 1024),
        name="last",
    )(rf, loc, coltab, s, d, lin)
    return gin, gspec.transpose(0, 1, 3, 2), glin, gbias.reshape(64)


def solution(mesh):
    return jax.shard_map(
        body,
        mesh=mesh,
        in_specs=(
            P("rows", None, "modes"),
            P("rows", None, "modes"),
            P("rows", None, None, "modes"),
            P(),
            P(),
        ),
        out_specs=(P("rows", None, "modes"), P("rows", None, None, "modes"), P(), P()),
        check_vma=False,
    )
```

```python
import math

import jax
import jax.numpy as jnp
import numpy as np
from jax import lax
from jax.experimental import pallas as pl
from jax.experimental.pallas import tpu as pltpu
from jax.sharding import PartitionSpec as P

MESH = pl.DeviceIdType.MESH
BF = jnp.bfloat16
F32 = jnp.float32
VMEM = pl.BlockSpec(memory_space=pltpu.VMEM)


def dot(a, b):
    return jnp.dot(a, b, preferred_element_type=F32)


def lanes_of(shape):
    return lax.broadcasted_iota(jnp.int32, shape, len(shape) - 1)


def column_constants():
    k = np.arange(128) // 2
    w = np.arange(2048)
    ang = ((w[:, None] * k[None, :]) % 2048) * (2.0 * math.pi / 2048)
    even = (np.arange(128) % 2 == 0)[None, :]
    ana = np.where(even, np.cos(ang), -np.sin(ang))
    swap = np.where(even, -np.sin(ang), -np.cos(ang))
    return np.concatenate([ana, swap], axis=1).reshape(4, 512, 256).astype(np.float32).astype(jnp.bfloat16)


def row_constants():
    slot = np.arange(64)
    core, z, x, jj = slot // 32, (slot // 8) % 4, (slot // 2) % 4, slot % 2
    mode = x * 16 + z * 4 + core * 2 + jj
    freq = np.where(mode < 32, mode, mode - 64)
    rows = np.arange(2048).reshape(32, 64)
    ang = ((freq[None, :, None] * rows[:, None, :]) % 2048) * (2.0 * math.pi / 2048)
    return np.stack([np.cos(ang), np.sin(ang)], axis=1).astype(np.float32).astype(jnp.bfloat16)


def kron8(table, flip):
    up = (lax.broadcasted_iota(jnp.int32, (512, 64), 0) >> 3 == lax.broadcasted_iota(jnp.int32, (512, 64), 1)).astype(BF)
    wide = (lax.broadcasted_iota(jnp.int32, (64, 512), 1) >> 3 == lax.broadcasted_iota(jnp.int32, (64, 512), 0)).astype(BF)
    keep = (lax.broadcasted_iota(jnp.int32, (512, 512), 0) ^ lax.broadcasted_iota(jnp.int32, (512, 512), 1)) & 7 == 0
    left = lax.dot_general(up, table, (((1,), (1 if flip else 0,)), ((), ())), preferred_element_type=F32).astype(BF)
    return jnp.where(keep, dot(left, wide), 0.0).astype(BF)


class Spot:
    def __init__(self):
        r, y = lax.axis_index("rows"), lax.axis_index("modes")
        x, z, core = lax.div(r, 8), lax.rem(lax.div(r, 2), 4), lax.rem(r, 2)
        p, q = y * (1 - core) + z * core, z * (1 - core) + y * core
        self.core, self.other = core, 1 - core
        self.p = [lax.rem(p + d, 4) for d in range(4)]
        self.q = [lax.rem(q + d, 4) for d in range(4)]
        self.x = [lax.rem(x + d, 4) for d in range(4)]
        self.sibling = (r + 1 - 2 * core, y)
        self.first = [self.at(v, q, x) for v in self.p]
        self.plane = [[self.at(p, v, u) for u in self.x] for v in self.q]

    def at(self, p, q, x):
        y, z = p * self.other + q * self.core, q * self.other + p * self.core
        return ((x * 4 + z) * 2 + self.core, y)


def signal_peers(spot):
    barrier = pltpu.get_barrier_semaphore()
    peers = [spot.sibling] + spot.first[1:] + [spot.plane[k // 4][k % 4] for k in range(1, 16)]
    for peer in peers:
        pl.semaphore_signal(barrier, inc=1, device_id=peer, device_id_type=MESH)


def wait_peers():
    pl.semaphore_wait(pltpu.get_barrier_semaphore(), 19)


def remote(src, dst, send, recv, target):
    return pltpu.make_async_remote_copy(src_ref=src, dst_ref=dst, send_sem=send, recv_sem=recv, device_id=target, device_id_type=MESH)


def columns(block, tab, xs_ref, h0, count):
    prod = dot(block.reshape(count * 64, 512), tab).reshape(count, 8, 8, 256)
    for a in range(4):
        for g in range(2):
            v = prod[:, 2 * a + g].reshape(count * 8, 256).astype(BF)
            xs_ref[g, pl.ds(h0 * 8, count * 8), 128 * a : 128 * a + 128] = v[:, :128]
            xs_ref[g, pl.ds(512 + h0 * 8, count * 8), 128 * a : 128 * a + 128] = v[:, 128:]


def row_modes(xs_ref, rmat_ref, t_ref, owner):
    block = lanes_of((256, 128)) >> 5
    for g in range(2):
        o = dot(rmat_ref[pl.ds(pl.multiple_of(owner * 256, 256), 256), :], xs_ref[g])
        for m in range(4):
            total = None
            for a in range(4):
                v = o[:, 128 * a : 128 * a + 128]
                shift = (32 * (a - m)) % 128
                if shift:
                    v = pltpu.roll(v, shift, 1)
                total = v if total is None else jnp.where(block == a, v, total)
            total = total.astype(BF).reshape(4, 4, 16, 128)
            for z in range(4):
                t_ref[owner, m * (1 - owner) + z * owner, z * (1 - owner) + m * owner, :, g] = total[z]


def inverse(g_ref, imat_ref, out_ref, after=lambda b: None):
    even = lanes_of((512, 128)) & 1 == 0
    block = lanes_of((512, 128)) >> 5
    for b in range(4):
        cols = []
        for g in range(2):
            total = None
            for m in range(4):
                parts = [g_ref[0, m, :, :, g].reshape(256, 128)]
                parts += [g_ref[1, z, m, :, g].reshape(64, 128) for z in range(4)]
                v = jnp.concatenate(parts, axis=0).astype(F32)
                shift = (32 * (m - b)) % 128
                if shift:
                    v = pltpu.roll(v, shift, 1)
                total = v if total is None else jnp.where(block == m, v, total)
            swapped = jnp.where(even, -pltpu.roll(total, 127, 1), pltpu.roll(total, 1, 1))
            cols.append(jnp.concatenate([total.astype(BF), swapped.astype(BF)], axis=0))
        o = dot(imat_ref[...], jnp.concatenate(cols, axis=1))
        both = jnp.concatenate([o[:, :128].reshape(64, 8, 128), o[:, 128:].reshape(64, 8, 128)], axis=1)
        out_ref[:, 16 * b : 16 * b + 16, :] = both.astype(BF)
        after(b)


def gelu_grad(z):
    u = (0.3275911 * 0.7071067811865476) * jnp.abs(z)
    e = jnp.exp2((-0.5 * 1.4426950408889634) * z * z)
    t = 1.0 / (1.0 + u)
    poly = t * (0.5 * 0.254829592 + t * (-0.5 * 0.284496736 + t * (0.5 * 1.421413741 + t * (-0.5 * 1.453152027 + t * (0.5 * 1.061405429)))))
    r = (poly - (0.3989422804014327 / (0.3275911 * 0.7071067811865476)) * u) * e
    return jnp.where(z >= 0, 1.0 - r, r)


def duplicate(v):
    even = lax.broadcasted_iota(jnp.int32, v.shape, 0) & 1 == 0
    return jnp.where(even, v, pltpu.roll(v, 1, 0)), jnp.where(even, pltpu.roll(v, v.shape[0] - 1, 0), v)


def to_columns(block):
    turned = [[block[g] if a == 0 else pltpu.roll(block[g], 128 - 32 * a, 1) for g in range(2)] for a in range(4)]
    out = []
    for jj in range(2):
        rows = [turned[a][g][8 * jj : 8 * jj + 8] for a in range(4) for g in range(2)]
        out.append(jnp.concatenate(rows + rows, axis=0).T[:32, :64])
    return out


def to_block(cols):
    block = lanes_of((8, 128)) >> 5
    parts = []
    for v in cols:
        square = jnp.concatenate([jnp.concatenate([v, v], axis=1)] * 4, axis=0).T
        parts.append([])
        for g in range(2):
            out = square[8 * g : 8 * g + 8]
            for a in range(1, 4):
                out = jnp.where(block == a, square[16 * a + 8 * g : 16 * a + 8 * g + 8], out)
            parts[-1].append(out)
    return [jnp.concatenate([parts[0][g], parts[1][g]], axis=0) for g in range(2)]


def weigh(s, w_ref, jj):
    re, im = duplicate(s)
    t1 = jnp.zeros((32, 64), F32)
    t2 = jnp.zeros((32, 64), F32)
    for c in range(64):
        w = w_ref[jj, c].astype(F32)
        t1 += re[:, c : c + 1] * w
        t2 += im[:, c : c + 1] * w
    even = lax.broadcasted_iota(jnp.int32, (32, 64), 0) & 1 == 0
    return t1 + jnp.where(even, -pltpu.roll(t2, 31, 0), pltpu.roll(t2, 1, 0))


def weigh_back(d, w_ref, jj):
    even = lax.broadcasted_iota(jnp.int32, (32, 64), 0) & 1 == 0
    dsw = jnp.where(even, pltpu.roll(d, 31, 0), pltpu.roll(d, 1, 0))
    lane = lanes_of((32, 64))
    u1 = jnp.zeros((32, 64), F32)
    u2 = jnp.zeros((32, 64), F32)
    for c in range(64):
        w = w_ref[jj, c].astype(F32)
        u1 = jnp.where(lane == c, jnp.sum(w * d, axis=1, keepdims=True), u1)
        u2 = jnp.where(lane == c, jnp.sum(w * dsw, axis=1, keepdims=True), u2)
    return jnp.where(even, u1 + pltpu.roll(u1, 31, 0), pltpu.roll(u2, 1, 0) - u2)


FAR = (2, 1, 3, 0)
NEAR = (0, 1, 3, 2)


def arrived(spot, ref, recv, k):
    remote(ref, ref, recv.at[k], recv.at[k], spot.sibling).wait_recv()


def sent(spot, ref, send, k):
    remote(ref, ref, send.at[k], send.at[k], spot.sibling).wait_send()


def start_core(spot, t_ref, b0, send, recv):
    for d in FAR:
        row = spot.p[d]
        remote(t_ref.at[spot.other, :, row], b0.at[:, row], send.at[0], recv.at[d], spot.sibling).start()


def reduce_scatter(spot, t_ref, bufs, send, recv, between):
    b0, a1, b1, a2, b2 = bufs
    core, p, q, x = spot.core, spot.p[0], spot.q[0], spot.x[0]
    for d in FAR:
        row = spot.q[d]
        arrived(spot, b0.at[:, row], recv, d)
        for e in FAR:
            pt = spot.p[e]
            a1[pt, row] = (t_ref[core, pt, row].astype(F32) + b0[pt, row].astype(F32)).astype(BF)
            if e:
                remote(a1.at[pt, row], b1.at[e - 1, row], send.at[1], recv.at[4 + d], spot.first[e]).start()
    between(0)
    for d in FAR:
        row = spot.q[d]
        arrived(spot, b1.at[:, row], recv, 4 + d)
        a2[row] = (a1[p, row].astype(F32) + b1[0, row].astype(F32) + b1[1, row].astype(F32) + b1[2, row].astype(F32)).astype(BF)
        for n in FAR:
            k = 4 * d + n
            if k:
                remote(a2.at[row, spot.x[n]], b2.at[k - 1], send.at[2], recv.at[8], spot.plane[d][n]).start()
    own = a1[p, q, x].astype(F32)
    for k in range(3):
        own += b1[k, q, x].astype(F32)
    between(1)
    arrived(spot, b2, recv, 8)
    for k in range(15):
        own += b2[k].astype(F32)
    return own


def drain_scatter(spot, t_ref, bufs, send):
    sent(spot, t_ref.at[0], send, 0)
    sent(spot, bufs[2], send, 1)
    sent(spot, bufs[4], send, 2)


def all_gather(spot, g_ref, send, recv, between):
    core, p = spot.core, spot.p[0]
    mine = g_ref.at[core, p, spot.q[0], spot.x[0]]
    for d in (0, 2, 1, 3):
        for n in FAR:
            if 4 * d + n:
                remote(mine, mine, send.at[2], recv.at[8 + d], spot.plane[d][n]).start()
    between(2)
    for d in NEAR:
        row = spot.q[(4 - d) % 4]
        arrived(spot, g_ref.at[core, p, row, pl.ds(0, 4 if d else 3)], recv, 8 + d)
        mine = g_ref.at[core, p, row]
        for e in (2, 1, 3):
            remote(mine, mine, send.at[1], recv.at[4 + d], spot.first[e]).start()
    between(3)
    for d in NEAR:
        row = spot.q[(4 - d) % 4]
        arrived(spot, g_ref.at[core, pl.ds(0, 3), row], recv, 4 + d)
        theirs = g_ref.at[core, :, row]
        remote(theirs, theirs, send.at[0], recv.at[0], spot.sibling).start()
    between(4)
    arrived(spot, g_ref.at[spot.other], recv, 0)


def drain_gather(spot, g_ref, bufs, send):
    sent(spot, g_ref.at[0], send, 0)
    sent(spot, g_ref.at[0, pl.ds(0, 3)], send, 1)
    sent(spot, bufs[4], send, 2)


def main_kernel(act_hbm, cot_hbm, w_hbm, coltab_hbm, rowtab_hbm, lw_hbm, bias_hbm,
                loc_hbm, rf2_hbm, s_ref, d_ref, lin_out_ref,
                lw_ref, bias_ref, act, cot, w_ref, tab, dtab, syn, rowtab, rmat, imat_ref, lw_t, bias_col, xs, rf, dpre, loc, lin, t1, t2, g1, g2_ref, part,
                b0, a1, b1, a2, b2, c0, e1, c1, e2, c2,
                in_sem, out_sem, send1, recv1, send2, recv2, send3, recv3, send4, recv4, send5, recv5):
    spot = Spot()
    core, p, q, x = spot.core, spot.p[0], spot.q[0], spot.x[0]
    signal_peers(spot)
    row_dev, mode_dev = lax.axis_index("rows"), lax.axis_index("modes")
    def load_act(i):
        some = pl.ds(16 * i, 16)
        return pltpu.make_async_copy(act_hbm.at[some], act.at[some], in_sem.at[2 + i])

    load_rows = pltpu.make_async_copy(rowtab_hbm.at[row_dev], rowtab, in_sem.at[1])
    load_cols = pltpu.make_async_copy(coltab_hbm.at[mode_dev], tab, in_sem.at[0])
    load_w = pltpu.make_async_copy(w_hbm, w_ref, in_sem.at[6])
    load_cot = pltpu.make_async_copy(cot_hbm, cot, in_sem.at[7])
    load_rows.start()
    load_cols.start()
    for i in range(4):
        load_act(i).start()
    load_rows.wait()
    rmat[:, :512] = kron8(rowtab[0], False)
    rmat[:, 512:] = kron8(rowtab[1], False)
    load_cols.wait()

    def analyse(i, _):
        load_act(i).wait()
        columns(act[pl.ds(16 * i, 16)], tab[...], xs, pl.multiple_of(16 * i, 16), 16)
        return 0

    lax.fori_loop(0, 4, analyse, 0)
    load_lw = pltpu.make_async_copy(lw_hbm, lw_ref, in_sem.at[8])
    load_bias = pltpu.make_async_copy(bias_hbm, bias_ref, in_sem.at[9])
    for cp in (load_lw, load_bias, load_w, load_cot):
        cp.start()
    row_modes(xs, rmat, t1, spot.other)
    wait_peers()
    start_core(spot, t1, b0, send1, recv1)
    row_modes(xs, rmat, t1, core)

    def prepare(i):
        if i == 0:
            imat_ref[:, :512] = kron8(rowtab[0], True)
            imat_ref[:, 512:] = kron8(rowtab[1], True)
            load_lw.wait()
            load_bias.wait()
            lw_t[...] = lw_ref[...].astype(F32).T.astype(BF)
            bias_col[...] = jnp.broadcast_to(bias_ref[...], (128, 64)).T
        if i == 1:
            lane = lanes_of((512, 256)) % 128
            scaled = tab[...].astype(F32) * jnp.where(lane < 2, 2.0**-22, 2.0**-21)
            dtab[...] = scaled.astype(BF)
            syn[...] = scaled[:, :128].T.astype(BF)

    first, second = (b0, a1, b1, a2, b2), (c0, e1, c1, e2, c2)
    own = reduce_scatter(spot, t1, first, send1, recv1, prepare)
    load_w.wait()
    s = to_columns(own.astype(BF).astype(F32))
    mixed = []
    for jj in range(2):
        s_ref[jj] = s[jj]
        mixed.append(weigh(s[jj], w_ref, jj))
    for g, v in enumerate(to_block(mixed)):
        g1[core, p, q, x, g] = v.astype(BF)
    all_gather(spot, g1, send2, recv2, lambda i: drain_scatter(spot, t1, first, send1) if i == 3 else None)

    inverse(g1, imat_ref, rf)
    load_cot.wait()

    def rows(i, _):
        bias = jnp.concatenate([bias_col[...]] * 4, axis=1)
        for n in range(2):
            first = pl.multiple_of(16 * i + 8 * n, 8)
            ds = []
            for k in range(8):
                h = first + k
                lhs = jnp.concatenate([rf[h], lw_t[...]], axis=1)
                rhs = jnp.concatenate([syn[...], act[h]], axis=0)
                d = (cot[h].astype(F32) * gelu_grad(dot(lhs, rhs) + bias)).astype(BF)
                dpre[h] = d
                ds.append(d)
            columns(jnp.concatenate(ds, axis=0).reshape(8, 64, 512), dtab[...], xs, first, 8)
        return 0

    lax.fori_loop(0, 4, rows, 0)
    row_modes(xs, rmat, t2, spot.other)
    start_core(spot, t2, c0, send3, recv3)
    row_modes(xs, rmat, t2, core)

    steps = (
        (p, spot.first[1:]),
        (q, [spot.plane[d][0] for d in (1, 2, 3)]),
        (x, [spot.plane[0][d] for d in (1, 2, 3)]),
    )

    def swap_lin():
        part[0, core] = lin[...]
        drain_gather(spot, g1, first, send2)
        remote(part.at[0, core], part.at[0, core], send5.at[0], recv5.at[0], spot.sibling).start()

    def join_lin(i):
        if i == 0:
            sent(spot, part.at[0, 0], send5, 0)
            arrived(spot, part.at[0, 0], recv5, 0)
            return part[0, 0] + part[0, 1]
        sent(spot, part.at[i, pl.ds(0, 3)], send5, i)
        arrived(spot, part.at[i, pl.ds(0, 3)], recv5, i)
        return part[i, 0] + part[i, 1] + part[i, 2] + part[i, 3]

    def pass_lin(i):
        me, peers = steps[i]
        part[i + 1, me] = join_lin(i)
        mine = part.at[i + 1, me]
        for peer in peers:
            remote(mine, mine, send5.at[i + 1], recv5.at[i + 1], peer).start()

    def products(i, _):
        left = jnp.concatenate([act[4 * i + k] for k in range(4)], axis=1)
        right = jnp.concatenate([dpre[4 * i + k] for k in range(4)], axis=1)
        left = jnp.concatenate([left, jnp.ones((16, 2048), BF)], axis=0)
        lin[...] += lax.dot_general(left, right, (((1,), (1,)), ((), ())), preferred_element_type=F32)
        return 0

    def local_products(i):
        if i == 0:
            lin[...] = jnp.zeros_like(lin)
            lax.fori_loop(0, 8, products, 0)
        if i == 1:
            lax.fori_loop(8, 16, products, 0)
            swap_lin()
        if i >= 2:
            pass_lin(i - 2)
        if i == 3:
            drain_scatter(spot, t2, second, send3)
        if i in (2, 3):
            lax.fori_loop(2 * i - 4, 2 * i - 2, pointwise, 0)

    def pointwise(i, _):
        def some_rows(n, _):
            for k in range(8):
                h = 16 * i + 8 * n + k
                loc[h] = dot(lw_ref[...], dpre[h]).astype(BF)
            return 0

        lax.fori_loop(0, 2, some_rows, 0)
        some = pl.ds(16 * i, 16)
        pltpu.make_async_copy(loc.at[some], loc_hbm.at[some], out_sem.at[i]).start()
        return 0

    own = reduce_scatter(spot, t2, second, send3, recv3, local_products)
    d = to_columns(own.astype(BF).astype(F32))
    back = []
    for jj in range(2):
        d_ref[jj] = d[jj]
        back.append(weigh_back(d[jj], w_ref, jj))
    for g, v in enumerate(to_block(back)):
        g2_ref[core, p, q, x, g] = v.astype(BF)
    all_gather(spot, g2_ref, send4, recv4, local_products)

    def ship(b):
        return pltpu.make_async_copy(rf.at[:, pl.ds(16 * b, 16)], rf2_hbm.at[:, pl.ds(16 * b, 16)], out_sem.at[4 + b])

    inverse(g2_ref, imat_ref, rf, lambda b: ship(b).start())
    lin_out_ref[...] = join_lin(3) * (1.0 / 2048)
    drain_gather(spot, g2_ref, second, send4)
    for i in range(4):
        some = pl.ds(16 * i, 16)
        pltpu.make_async_copy(loc.at[some], loc_hbm.at[some], out_sem.at[i]).wait()
        ship(i).wait()


def last_kernel(rf_hbm, loc_hbm, coltab_hbm, s_ref, d_ref, lin_ref,
                gin_hbm, gspec_hbm, glin_ref, gbias_ref, rf, loc, tab, ana, gin, gspec, in_sem, out_sem):
    load = pltpu.make_async_copy(coltab_hbm.at[lax.axis_index("modes")], tab, in_sem.at[8])
    load.start()

    def copy(n, i):
        some = pl.ds(16 * i, 16)
        if n == 2:
            return pltpu.make_async_copy(gin.at[some], gin_hbm.at[some], out_sem.at[i])
        src, dst = ((rf_hbm, rf), (loc_hbm, loc))[n]
        return pltpu.make_async_copy(src.at[some], dst.at[some], in_sem.at[2 * i + n])

    for i in range(4):
        copy(0, i).start()
        copy(1, i).start()
    glin_ref[...] = lin_ref[:64]
    gbias_ref[...] = lin_ref[64:65]
    even = lax.broadcasted_iota(jnp.int32, (32, 64), 0) & 1 == 0
    def products(jj, _):
        re, im = duplicate(s_ref[jj])
        d = d_ref[jj]
        dsw = jnp.where(even, pltpu.roll(d, 31, 0), -pltpu.roll(d, 1, 0))
        for c in range(64):
            gspec[jj, c] = re[:, c : c + 1] * d + im[:, c : c + 1] * dsw
        pltpu.make_async_copy(gspec.at[jj], gspec_hbm.at[jj], out_sem.at[4 + jj]).start()
        return 0

    lax.fori_loop(0, 2, products, 0)
    load.wait()
    ana[...] = tab[:, :128].astype(F32).T.astype(BF)

    def row(i, _):
        copy(0, i).wait()
        copy(1, i).wait()
        for k in range(4):
            some = pl.ds(16 * i + 4 * k, 4)
            part = dot(rf[some].reshape(256, 128), ana[...]).reshape(4, 64, 512)
            gin[some] = (part + loc[some].astype(F32)).astype(BF)
        copy(2, i).start()
        return 0

    lax.fori_loop(0, 4, row, 0)
    for jj in range(2):
        pltpu.make_async_copy(gspec.at[jj], gspec_hbm.at[jj], out_sem.at[4 + jj]).wait()
    for i in range(4):
        copy(2, i).wait()


SPEC = (2, 4, 4, 4, 2, 16, 128)
ANY = pl.BlockSpec(memory_space=pl.ANY)
HBM = pl.BlockSpec(memory_space=pltpu.HBM)


def body(activations, cotangent, spectral_weight, linear_weight, bias):
    w = spectral_weight.transpose(0, 1, 3, 2)
    coltab, rowtab = jnp.asarray(column_constants()), jnp.asarray(row_constants())
    dma = pltpu.SemaphoreType.DMA
    quarter = (4, 4, 4, 2, 16, 128)
    buffers = [pltpu.VMEM(quarter, BF), pltpu.VMEM(quarter, BF), pltpu.VMEM((3, 4, 4, 2, 16, 128), BF),
               pltpu.VMEM((4, 4, 2, 16, 128), BF), pltpu.VMEM((15, 2, 16, 128), BF)]
    shape = jax.ShapeDtypeStruct
    given = (activations, cotangent, w, coltab, rowtab, linear_weight, bias.reshape(1, 64))
    loc, rf, s, d, lin = pl.pallas_call(
        main_kernel,
        out_shape=[shape((64, 64, 512), BF), shape((64, 64, 128), BF), shape((2, 32, 64), F32), shape((2, 32, 64), F32),
                   shape((80, 64), F32)],
        in_specs=[HBM] * 7,
        out_specs=[ANY] * 2 + [VMEM] * 3,
        scratch_shapes=[
            pltpu.VMEM((64, 64), BF), pltpu.VMEM((1, 64), F32),
            pltpu.VMEM((64, 64, 512), BF), pltpu.VMEM((64, 64, 512), BF), pltpu.VMEM((2, 64, 32, 64), BF),
            pltpu.VMEM((512, 256), BF), pltpu.VMEM((512, 256), BF), pltpu.VMEM((128, 512), BF), pltpu.VMEM((2, 64, 64), BF),
            pltpu.VMEM((512, 1024), BF), pltpu.VMEM((512, 1024), BF), pltpu.VMEM((64, 64), BF), pltpu.VMEM((64, 128), F32),
            pltpu.VMEM((2, 1024, 512), BF),
            pltpu.VMEM((64, 64, 128), BF), pltpu.VMEM((64, 64, 512), BF), pltpu.VMEM((64, 64, 512), BF), pltpu.VMEM((80, 64), F32),
            pltpu.VMEM(SPEC, BF), pltpu.VMEM(SPEC, BF), pltpu.VMEM(SPEC, BF), pltpu.VMEM(SPEC, BF), pltpu.VMEM((4, 4, 80, 64), F32),
        ] + buffers + buffers + [dma((10,)), dma((8,))] + [dma((3,)), dma((12,))] * 4 + [dma((4,))] * 2,
        compiler_params=pltpu.CompilerParams(vmem_limit_bytes=44 * 1024 * 1024, collective_id=0, has_side_effects=True),
        name="main",
    )(*[pltpu.with_memory_space_constraint(v, pltpu.HBM) for v in given])
    gin, gspec, glin, gbias = pl.pallas_call(
        last_kernel,
        out_shape=[shape((64, 64, 512), BF), shape((2, 64, 32, 64), F32), shape((64, 64), F32), shape((1, 64), F32)],
        in_specs=[ANY] * 2 + [HBM] + [VMEM] * 3,
        out_specs=[ANY] * 2 + [VMEM] * 2,
        scratch_shapes=[pltpu.VMEM((64, 64, 128), BF), pltpu.VMEM((64, 64, 512), BF), pltpu.VMEM((512, 256), BF),
                        pltpu.VMEM((128, 512), BF), pltpu.VMEM((64, 64, 512), BF), pltpu.VMEM((2, 64, 32, 64), F32),
                        dma((9,)), dma((6,))],
        compiler_params=pltpu.CompilerParams(vmem_limit_bytes=24 * 1024 * 1024),
        name="last",
    )(rf, loc, pltpu.with_memory_space_constraint(coltab, pltpu.HBM), s, d, lin)
    return gin, gspec.transpose(0, 1, 3, 2), glin, gbias.reshape(64)


def solution(mesh):
    return jax.shard_map(
        body,
        mesh=mesh,
        in_specs=(
            P("rows", None, "modes"),
            P("rows", None, "modes"),
            P("rows", None, None, "modes"),
            P(),
            P(),
        ),
        out_specs=(P("rows", None, "modes"), P("rows", None, None, "modes"), P(), P()),
        check_vma=False,
    )
```
